32 devices in a mesh: dp: 4 (over x, core), ctx: 4 (over z), tensor: 2 (over y).
Axes of the slice: x: 2, y: 2, z: 4, core: 2. Of those that a mesh axis runs over, the one named last changes fastest.
Arguments:
- tokens: bfloat16 [4, 1024, 1024], P('dp', 'ctx'), may hold values from -6 to 6
- seq_lengths: int32 [4], P('dp'), may hold values from 256 to 1024, as said below
- qkv_weight: bfloat16 [1024, 3, 1024], P(('dp', 'ctx'), None, 'tensor'), may hold values from -4 to 4
- out_weight: bfloat16 [1024, 1024], P(('dp', 'ctx'), 'tensor'), may hold values from -1.5 to 1.5
- up_weight: bfloat16 [1024, 4096], P(('dp', 'ctx'), 'tensor'), may hold values from -0.1875 to 0.1875
- down_weight: bfloat16 [1024, 4096], P(('dp', 'ctx'), 'tensor'), may hold values from -0.09375 to 0.09375
- head_bias: bfloat16 [16, 128], P('tensor', ('dp', 'ctx')), may hold values from -3 to 3
- hidden_bias: bfloat16 [32, 128], P('tensor', ('dp', 'ctx')), may hold values from -3 to 3
- norm_gains: bfloat16 [2, 1024], P(None, ('dp', 'ctx')), may hold values from 0.25 to 1.75
- out_biases: bfloat16 [4, 1024], P(None, ('dp', 'ctx')), may hold values from -3 to 3
- cotangent: bfloat16 [4, 1024, 1024], P('dp', 'ctx'), may hold values from -6 to 6
Outputs:
- output: bfloat16 [4, 1024, 1024], P('dp', 'ctx')
- input_grad: float32 [4, 1024, 1024], P('dp', 'ctx')
- qkv_grad: float32 [1024, 3, 1024], P(('dp', 'ctx'), None, 'tensor')
- out_weight_grad: float32 [1024, 1024], P(('dp', 'ctx'), 'tensor')
- up_grad: float32 [1024, 4096], P(('dp', 'ctx'), 'tensor')
- down_grad: float32 [1024, 4096], P(('dp', 'ctx'), 'tensor')
- head_bias_grad: float32 [16, 128], P('tensor', ('dp', 'ctx'))
- hidden_bias_grad: float32 [32, 128], P('tensor', ('dp', 'ctx'))
- gains_grad: float32 [2, 1024], P(None, ('dp', 'ctx'))
- biases_grad: float32 [4, 1024], P(None, ('dp', 'ctx'))
The draws below stay inside these ranges and needn't reach their ends.
Inputs may be any that keep to these rules, and one draw needn't show every extreme that they name: `seq_lengths`: valid tokens of each sequence; in every draw some sequence has exactly 1024.
All inputs are finite; a program needn't handle non-finite values.
Results may differ from the reference program's by a relative error of at most 0.011.
The reference program's roundings to bfloat16 on the way count: a program that leaves them out, or rounds other values in their place, can miss the bound.
Values may be sent and summed in bfloat16 or wider, within the bound.
A program may use at most 128 MiB of HBM per device.

```python
import math
import jax
import jax.numpy as jnp
from jax import lax

D = 1024
H = 16
HD = 64
FF = 4096
L = 1024
SEQS = 4


def draw_tokens(key, part):
    values = jax.random.normal(key, (SEQS, L, D), jnp.float32)
    return jnp.clip(values, -6.0, 6.0).astype(jnp.bfloat16)


def draw_qkv_weight(key, part):
    base = jax.random.normal(key, (D, 3, D), jnp.float32) * D ** (-0.5)
    return jnp.clip(base, -4.0, 4.0).astype(jnp.bfloat16)


def draw_seq_lengths(key, part):
    lengths = jax.random.randint(key, (SEQS,), L // 4, L + 1, dtype=jnp.int32)
    chosen = jax.random.randint(jax.random.fold_in(key, 5), (), 0, SEQS, dtype=jnp.int32)
    return jnp.where(jnp.arange(SEQS) == chosen, L, lengths).astype(jnp.int32)


def block_levels(key, extent, pieces, smallest, top_value):
    loudness, own = 1.0, jax.random.fold_in(key, 6)
    for axis_at, parts in pieces:
        steps = jnp.exp(jax.random.uniform(jax.random.fold_in(own, axis_at), (parts,), jnp.float32, smallest / len(pieces), top_value / len(pieces)))
        loudness = loudness * jnp.repeat(steps, extent[axis_at] // parts).reshape([-1 if axis == axis_at else 1 for axis in range(len(extent))])
    return loudness


def gaussian(rng, extent, scale, limit, shards=(), kind=jnp.bfloat16):
    entries = jax.random.normal(rng, extent, jnp.float32) * scale
    if len(shards) > 0:
        entries = block_levels(rng, extent, shards, -0.22, 0.18) * entries
    return jnp.clip(entries, min=-limit, max=limit).astype(kind)


def setup_inputs(seed: int = 0) -> dict:
    splits = jax.random.split(jax.random.key(seed), 12)
    return {
        "tokens": draw_tokens(jax.random.fold_in(splits[11], 71), 0),
        "seq_lengths": draw_seq_lengths(jax.random.fold_in(splits[11], 71), 0),
        "qkv_weight": draw_qkv_weight(jax.random.fold_in(splits[11], 71), 0),
        "out_weight": gaussian(splits[3], (D, D), (D // 64) ** -0.5, 1.5, ((0, 16), (1, 2))),
        "up_weight": gaussian(splits[4], (D, FF), D ** -0.5, 0.1875, ((0, 16), (1, 2))),
        "down_weight": gaussian(splits[5], (D, FF), FF ** -0.5, 0.09375, ((0, 16), (1, 2))),
        "head_bias": gaussian(splits[6], (H, 2 * HD), 0.5, 3.0, ((0, 2), (1, 16))),
        "hidden_bias": gaussian(splits[7], (FF // (2 * HD), 2 * HD), 0.5, 3.0, ((0, 2), (1, 16))),
        "norm_gains": jnp.clip(1.0 + 0.15 * jax.random.normal(splits[8], (2, D), jnp.float32), 0.25, 1.75).astype(jnp.bfloat16),
        "out_biases": gaussian(splits[9], (4, D), 0.5, 3.0, ((1, 16),)),
        "cotangent": gaussian(splits[10], (SEQS, L, D), 1.0, 6.0, ((0, 4), (1, 4))),
    }


EPSILON = 1e-05
SCALE = 0.125
NEG_BIG = -1000000000.0
INV_ROOT_TWO = 1.0 / math.sqrt(2.0)
INV_ROOT_TWO_PI = 1.0 / math.sqrt(2.0 * math.pi)

def low_f32(values):
    return lax.optimization_barrier(values.astype(jnp.bfloat16)).astype(jnp.float32)

def layer_norm(hidden_in, gain, shift):
    centred = hidden_in - lax.optimization_barrier(jnp.mean(hidden_in, axis=-1, keepdims=True))
    variance = lax.optimization_barrier(jnp.mean(centred * centred, axis=-1, keepdims=True))
    inv_std = lax.rsqrt(variance + EPSILON)
    normed = centred * inv_std
    return (normed * gain + shift, normed, inv_std)

def norm_back(grad_out, normed, inv_std, gain):
    grad_normed = grad_out * gain
    first_mean = lax.optimization_barrier(jnp.mean(grad_normed, axis=-1, keepdims=True))
    second_mean = lax.optimization_barrier(jnp.mean(grad_normed * normed, axis=-1, keepdims=True))
    grad_in = inv_std * (grad_normed - first_mean - normed * second_mean)
    return (grad_in, lax.optimization_barrier(jnp.sum(grad_out * normed, axis=0)), lax.optimization_barrier(jnp.sum(grad_out, axis=0)))

def gelu_parts(pre_act):
    cdf_val = 0.5 * (1.0 + jax.scipy.special.erf(pre_act * INV_ROOT_TWO))
    return (pre_act * cdf_val, cdf_val + pre_act * jnp.exp(-0.5 * pre_act * pre_act) * INV_ROOT_TWO_PI)

def ref_scores(queries, key_rows, valid):
    scores = jnp.einsum('qhd,khd->hqk', queries.astype(jnp.float32), key_rows.astype(jnp.float32)) * SCALE
    return jnp.where(valid[None, None, :], scores, NEG_BIG)

def ref_attend(queries, key_rows, value_rows, valid):
    scores = ref_scores(queries, key_rows, valid)
    peak = lax.optimization_barrier(jnp.max(scores, axis=-1, keepdims=True))
    log_total = peak + jnp.log(lax.optimization_barrier(jnp.sum(jnp.exp(scores - peak), axis=-1, keepdims=True)))
    probs = low_f32(jnp.exp(scores - log_total))
    mixed = jnp.einsum('hqk,khd->qhd', probs, value_rows.astype(jnp.float32)).astype(jnp.bfloat16)
    return (mixed, log_total)

def ref_attend_back(queries, key_rows, value_rows, valid, mixed, log_total, grad_mixed):
    scores = ref_scores(queries, key_rows, valid)
    probs = jnp.exp(scores - log_total)
    grad_wide = grad_mixed.astype(jnp.float32)
    grad_values = jnp.einsum('hqk,qhd->khd', low_f32(probs), grad_wide)
    grad_probs = jnp.einsum('qhd,khd->hqk', grad_wide, value_rows.astype(jnp.float32))
    inner = jnp.einsum('qhd,qhd->hq', grad_wide, mixed.astype(jnp.float32))
    grad_scores = low_f32(probs * (grad_probs - inner[:, :, None]))
    grad_queries = jnp.einsum('hqk,khd->qhd', grad_scores, key_rows.astype(jnp.float32)) * SCALE
    grad_keys = jnp.einsum('hqk,qhd->khd', grad_scores, queries.astype(jnp.float32)) * SCALE
    return (grad_queries, grad_keys, grad_values)

def reference(tokens, seq_lengths, qkv_weight, out_weight, up_weight, down_weight, head_bias, hidden_bias, norm_gains, out_biases, cotangent):
    qkv_flat = qkv_weight.reshape(D, 3 * D)
    bias_query = head_bias[:, :HD].reshape(D).astype(jnp.float32)
    bias_value = head_bias[:, HD:].reshape(D).astype(jnp.float32)
    bias_hidden = hidden_bias.reshape(FF).astype(jnp.float32)
    gains_wide = norm_gains.astype(jnp.float32)
    biases_wide = out_biases.astype(jnp.float32)
    positions = jnp.arange(L)

    def one_sequence(carry, inputs):
        seq_tokens, seq_cot, length = inputs
        valid = positions < length
        projected = jnp.dot(seq_tokens, qkv_flat, preferred_element_type=jnp.float32).reshape(L, 3, D)
        queries = (projected[:, 0] + bias_query).astype(jnp.bfloat16).reshape(L, H, HD)
        key_rows = projected[:, 1].astype(jnp.bfloat16).reshape(L, H, HD)
        value_rows = (projected[:, 2] + bias_value).astype(jnp.bfloat16).reshape(L, H, HD)
        mixed, log_total = ref_attend(queries, key_rows, value_rows, valid)
        attn_flat = mixed.reshape(L, D)
        attn_proj = jnp.dot(attn_flat, out_weight.T, preferred_element_type=jnp.float32)
        first_sum = seq_tokens.astype(jnp.float32) + attn_proj + biases_wide[0]
        normed_one, z_one, rstd_one = layer_norm(first_sum, gains_wide[0], biases_wide[1])
        normed_low = normed_one.astype(jnp.bfloat16)
        pre_act = jnp.dot(normed_low, up_weight, preferred_element_type=jnp.float32) + bias_hidden
        activated, slope = gelu_parts(pre_act)
        hidden_low = activated.astype(jnp.bfloat16)
        mlp_out = jnp.dot(hidden_low, down_weight.T, preferred_element_type=jnp.float32)
        second_sum = normed_one + mlp_out + biases_wide[2]
        result, z_two, rstd_two = layer_norm(second_sum, gains_wide[1], biases_wide[3])
        output_rows = result.astype(jnp.bfloat16)
        grad_out = seq_cot.astype(jnp.float32)
        grad_two, gain_two_grad, shift_two_grad = norm_back(grad_out, z_two, rstd_two, gains_wide[1])
        grad_two_low = grad_two.astype(jnp.bfloat16)
        down_part = jnp.dot(grad_two_low.T, hidden_low, preferred_element_type=jnp.float32)
        grad_hidden = jnp.dot(grad_two_low, down_weight, preferred_element_type=jnp.float32)
        grad_pre = grad_hidden * slope
        grad_pre_low = grad_pre.astype(jnp.bfloat16)
        up_part = jnp.dot(normed_low.T, grad_pre_low, preferred_element_type=jnp.float32)
        grad_normed = jnp.dot(grad_pre_low, up_weight.T, preferred_element_type=jnp.float32) + grad_two
        grad_one, gain_one_grad, shift_one_grad = norm_back(grad_normed, z_one, rstd_one, gains_wide[0])
        grad_one_low = grad_one.astype(jnp.bfloat16)
        out_part = jnp.dot(grad_one_low.T, attn_flat, preferred_element_type=jnp.float32)
        grad_attn = jnp.dot(grad_one_low, out_weight, preferred_element_type=jnp.float32).astype(jnp.bfloat16)
        grad_queries, grad_keys, grad_values = ref_attend_back(queries, key_rows, value_rows, valid, mixed, log_total, grad_attn.reshape(L, H, HD))
        grad_queries = grad_queries.reshape(L, D)
        grad_values = grad_values.reshape(L, D)
        grad_proj = jnp.stack([grad_queries, grad_keys.reshape(L, D), grad_values], axis=1).astype(jnp.bfloat16).reshape(L, 3 * D)
        qkv_part = jnp.dot(seq_tokens.T, grad_proj, preferred_element_type=jnp.float32)
        input_rows = jnp.dot(grad_proj, qkv_flat.T, preferred_element_type=jnp.float32) + grad_one
        terms = (qkv_part, out_part, up_part, down_part, lax.optimization_barrier(jnp.sum(grad_queries, axis=0)), lax.optimization_barrier(jnp.sum(grad_values, axis=0)), lax.optimization_barrier(jnp.sum(grad_pre, axis=0)), jnp.stack([gain_one_grad, gain_two_grad]), jnp.stack([lax.optimization_barrier(jnp.sum(grad_one, axis=0)), shift_one_grad, lax.optimization_barrier(jnp.sum(grad_two, axis=0)), shift_two_grad]))
        new_carry = tuple((total + term for total, term in zip(carry, terms)))
        return (new_carry, (output_rows, input_rows))
    start = (jnp.zeros((D, 3 * D), jnp.float32), jnp.zeros((D, D), jnp.float32), jnp.zeros((D, FF), jnp.float32), jnp.zeros((D, FF), jnp.float32), jnp.zeros((D,), jnp.float32), jnp.zeros((D,), jnp.float32), jnp.zeros((FF,), jnp.float32), jnp.zeros((2, D), jnp.float32), jnp.zeros((4, D), jnp.float32))
    totals, (output, input_grad) = lax.scan(one_sequence, start, (tokens, cotangent, seq_lengths))
    qkv_grad = totals[0].reshape(D, 3, D)
    head_bias_grad = jnp.concatenate([totals[4].reshape(H, HD), totals[5].reshape(H, HD)], axis=1)
    hidden_bias_grad = totals[6].reshape(FF // (2 * HD), 2 * HD)
    return (output, input_grad, qkv_grad, totals[1], totals[2], totals[3], head_bias_grad, hidden_bias_grad, totals[7], totals[8])
```

```python
import functools
import math

import jax
import jax.numpy as jnp
from jax import lax
from jax.experimental import pallas as pl
from jax.experimental.pallas import tpu as pltpu
from jax.sharding import PartitionSpec as P

EPSILON = 1e-05
SCALE = 0.125
NEG_BIG = -1000000000.0
INV_ROOT_TWO = 1.0 / math.sqrt(2.0)
INV_ROOT_TWO_PI = 1.0 / math.sqrt(2.0 * math.pi)


def contract_last(left, right):
    return lax.dot_general(
        left, right, (((1,), (1,)), ((), ())), preferred_element_type=jnp.float32
    )


def contract_first(left, right):
    return lax.dot_general(
        left, right, (((0,), (0,)), ((), ())), preferred_element_type=jnp.float32
    )


def layer_norm(hidden_in, gain, shift):
    centred = hidden_in - jnp.mean(hidden_in, axis=-1, keepdims=True)
    variance = jnp.mean(centred * centred, axis=-1, keepdims=True)
    inv_std = lax.rsqrt(variance + EPSILON)
    normed = centred * inv_std
    return (normed * gain + shift, normed, inv_std)


def norm_back(grad_out, normed, inv_std, gain):
    grad_normed = grad_out * gain
    first_mean = jnp.mean(grad_normed, axis=-1, keepdims=True)
    second_mean = jnp.mean(grad_normed * normed, axis=-1, keepdims=True)
    grad_in = inv_std * (grad_normed - first_mean - normed * second_mean)
    return (grad_in, jnp.sum(grad_out * normed, axis=0), jnp.sum(grad_out, axis=0))


def gelu_parts(pre_act):
    cdf_val = 0.5 * (1.0 + jax.scipy.special.erf(pre_act * INV_ROOT_TWO))
    return (
        pre_act * cdf_val,
        cdf_val + pre_act * jnp.exp(-0.5 * pre_act * pre_act) * INV_ROOT_TWO_PI,
    )


def block_scores(queries, key_rows, valid):
    scores = (
        jnp.einsum("qhd,khd->hqk", queries, key_rows, preferred_element_type=jnp.float32) * SCALE
    )
    return jnp.where(valid[None, None, :], scores, NEG_BIG)


def attend_forward(inputs):
    queries, key_rows, value_rows, valid = inputs
    scores = block_scores(queries, key_rows, valid)
    peak = jnp.max(scores, axis=-1, keepdims=True)
    log_total = peak + jnp.log(jnp.sum(jnp.exp(scores - peak), axis=-1, keepdims=True))
    probs = jnp.exp(scores - log_total).astype(jnp.bfloat16)
    mixed = jnp.einsum(
        "hqk,khd->qhd", probs, value_rows, preferred_element_type=jnp.float32
    ).astype(jnp.bfloat16)
    return (mixed, log_total)


def attend_backward(inputs):
    queries, key_rows, value_rows, valid, mixed, log_total, grad_mixed = inputs
    scores = block_scores(queries, key_rows, valid)
    probs = jnp.exp(scores - log_total)
    grad_values = jnp.einsum(
        "hqk,qhd->khd", probs.astype(jnp.bfloat16), grad_mixed, preferred_element_type=jnp.float32
    )
    grad_probs = jnp.einsum(
        "qhd,khd->hqk", grad_mixed, value_rows, preferred_element_type=jnp.float32
    )
    inner = jnp.einsum("qhd,qhd->hq", grad_mixed.astype(jnp.float32), mixed.astype(jnp.float32))
    grad_scores = (probs * (grad_probs - inner[:, :, None])).astype(jnp.bfloat16)
    grad_queries = (
        jnp.einsum("hqk,khd->qhd", grad_scores, key_rows, preferred_element_type=jnp.float32)
        * SCALE
    )
    grad_keys = (
        jnp.einsum("hqk,qhd->khd", grad_scores, queries, preferred_element_type=jnp.float32) * SCALE
    )
    return (grad_queries, grad_keys, grad_values)


def comm_kernel(sizes, kinds, copies, *refs):
    n_outer, n_core, n_ctx, n_tensor = sizes
    count = len(kinds)
    ins, outs = refs[:count], refs[count : 2 * count]
    send_sem, recv_sem, own_sem = refs[2 * count :]
    dp, ctx, tensor = (lax.axis_index(name) for name in ("dp", "ctx", "tensor"))
    outer, core = dp // n_core, dp % n_core

    def coords(offset, sign=1):
        def move(at, step, size):
            return at if step == 0 else (at + (step if sign > 0 else size - step)) % size

        outer_at = move(outer, offset[0], n_outer)
        core_at = move(core, offset[1], n_core)
        return outer_at * n_core + core_at, move(ctx, offset[2], n_ctx), move(tensor, offset[3], n_tensor)

    def device(offset):
        dp_at, ctx_at, tensor_at = coords(offset)
        return {"dp": dp_at, "ctx": ctx_at, "tensor": tensor_at}

    offsets = peer_offsets(sizes, kinds)
    barrier = pltpu.get_barrier_semaphore()
    for offset in offsets:
        pl.semaphore_signal(
            barrier, inc=1, device_id=device(offset), device_id_type=pl.DeviceIdType.MESH
        )
    pl.semaphore_wait(barrier, len(offsets))

    started, used = [], [0]

    def put(source, target, offset):
        number = used[0]
        used[0] += 1
        copy = pltpu.make_async_remote_copy(
            src_ref=source,
            dst_ref=target,
            send_sem=send_sem.at[number],
            recv_sem=recv_sem.at[number],
            device_id=device(offset),
            device_id_type=pl.DeviceIdType.MESH,
        )
        copy.start()
        started.append(copy)
        return number

    def arrived(number, target, offset):
        pltpu.make_async_remote_copy(
            src_ref=target,
            dst_ref=target,
            send_sem=send_sem.at[number],
            recv_sem=recv_sem.at[number],
            device_id=device(offset),
            device_id_type=pl.DeviceIdType.MESH,
        ).wait_recv()

    partner = (0, 1, 0, 0)
    pending, own_copies = [], []
    first = {}
    for at, kind in enumerate(kinds):
        source, target = ins[at], outs[at]
        index = functools.partial(slot_of, kind, n_ctx)
        mine = index(*coords((0, 0, 0, 0)))
        if kind == "swap":
            for offset in direct_offsets(sizes, kind):
                number = put(source, target.at[offset[3] - 1], offset)
                pending.append((number, target.at[offset[3] - 1], offset))
            continue
        if kind in ("ctx", "cg", "dp", "all"):
            for offset in direct_offsets(sizes, kind):
                block = source if kind == "cg" else source.at[index(*coords(offset))]
                number = put(block, target.at[mine], offset)
                pending.append((number, target.at[index(*coords(offset, -1))], offset))
            block = source if kind == "cg" else source.at[mine]
            own = pltpu.make_async_copy(block, target.at[mine], own_sem.at[at])
        else:
            stage = []
            if kind == "wg":
                for step in range(1, n_ctx):
                    offset = (0, 0, step, 0)
                    stage.append((put(source, target.at[mine], offset), offset))
            crossing = []
            for step in range(1, n_outer):
                offset = (step, 0, 0, 0)
                crossing.append((put(source, target.at[mine], offset), offset, (0, 0, 0, 0)))
            pending.append(
                (put(source, target.at[mine], partner), target.at[index(*coords(partner, -1))], partner)
            )
            own = pltpu.make_async_copy(source, target.at[mine], own_sem.at[at])
            first[at] = (stage, crossing)
        own.start()
        own_copies.append(own)
    for at in first:
        target = outs[at]
        index = functools.partial(slot_of, kinds[at], n_ctx)
        stage, crossing = first[at]
        for number, offset in stage:
            slot = index(*coords(offset, -1))
            arrived(number, target.at[slot], offset)
            for step in range(1, n_outer):
                across = (step, 0, 0, 0)
                crossing.append((put(target.at[slot], target.at[slot], across), across, offset))
            both = (0, 1, offset[2], 0)
            pending.append(
                (put(target.at[slot], target.at[slot], partner), target.at[index(*coords(both, -1))], partner)
            )
    for at in first:
        target = outs[at]
        index = functools.partial(slot_of, kinds[at], n_ctx)
        for number, across, offset in first[at][1]:
            origin = (across[0], 0, offset[2], 0)
            slot = index(*coords(origin, -1))
            arrived(number, target.at[slot], across)
            both = (across[0], 1, offset[2], 0)
            pending.append(
                (put(target.at[slot], target.at[slot], partner), target.at[index(*coords(both, -1))], partner)
            )
    for number, target, offset in pending:
        arrived(number, target, offset)
    for own in own_copies:
        own.wait()
    for copy in started:
        copy.wait_send()


def slot_of(kind, n_ctx, dp_at, ctx_at, tensor_at):
    if kind in ("ctx", "cg"):
        return ctx_at
    if kind in ("dp", "dpg"):
        return dp_at
    return dp_at * n_ctx + ctx_at


def direct_offsets(sizes, kind):
    n_outer, n_core, n_ctx, n_tensor = sizes
    if kind == "swap":
        return [(0, 0, 0, step) for step in range(1, n_tensor)]
    if kind in ("ctx", "cg"):
        return [(0, 0, step, 0) for step in range(1, n_ctx)]
    ctx_steps = range(n_ctx) if kind == "all" else range(1)
    return [
        (o, c, k, 0) for k in ctx_steps for o in range(n_outer) for c in range(n_core) if o + c + k
    ]


def peer_offsets(sizes, kinds):
    n_outer, n_core, n_ctx, n_tensor = sizes
    found = set()
    for kind in kinds:
        if kind in ("wg", "dpg"):
            found.update((o, 0, 0, 0) for o in range(1, n_outer))
            found.add((0, 1, 0, 0))
            if kind == "wg":
                found.update((0, 0, k, 0) for k in range(1, n_ctx))
        else:
            found.update(direct_offsets(sizes, kind))
    return sorted(found)


def exchange(sizes, number, ops):
    n_outer, n_core, n_ctx, n_tensor = sizes
    n_dp = n_outer * n_core
    kinds = tuple(kind for kind, _ in ops)
    shapes, copies, moved = [], 0, 0
    for kind, array in ops:
        if kind == "swap":
            lead, sends = (n_tensor - 1,), n_tensor - 1
        elif kind == "dpg":
            lead, sends = (n_dp,), n_dp - 1
        elif kind == "cg":
            lead, sends = (n_ctx,), n_ctx - 1
        elif kind == "wg":
            lead, sends = (n_dp * n_ctx,), n_dp * n_ctx - 1
        else:
            lead, sends = (), array.shape[0] - 1
        shapes.append(jax.ShapeDtypeStruct(lead + array.shape, array.dtype))
        copies += sends
        moved += math.prod(lead + array.shape) * array.dtype.itemsize
    vmem = pl.BlockSpec(memory_space=pltpu.VMEM)
    return pl.pallas_call(
        functools.partial(comm_kernel, sizes, kinds, copies),
        out_shape=tuple(shapes),
        in_specs=[vmem] * len(ops),
        out_specs=tuple(
            pl.BlockSpec(memory_space=pl.ANY) if kind == "wg" else vmem for kind in kinds
        ),
        scratch_shapes=[
            pltpu.SemaphoreType.DMA((copies,)),
            pltpu.SemaphoreType.DMA((copies,)),
            pltpu.SemaphoreType.DMA((len(ops),)),
        ],
        compiler_params=pltpu.CompilerParams(
            collective_id=number, has_side_effects=True, vmem_limit_bytes=60 * 2**20
        ),
        cost_estimate=pl.CostEstimate(
            flops=0, bytes_accessed=moved * 10, transcendentals=0
        ),
        name=f"exchange_{number}",
    )(*(array for _, array in ops))


def pack(parts, lead, unit):
    flat = jnp.concatenate([part.reshape(lead, -1) for part in parts], axis=1)
    wide = -(-flat.shape[1] // unit) * unit
    return jnp.pad(flat, ((0, 0), (0, wide - flat.shape[1]))).reshape(lead, wide // 128, 128)


def unpack(packed, shapes):
    flat = packed.reshape(packed.shape[0], -1)
    out, at = [], 0
    for shape in shapes:
        size = math.prod(shape)
        out.append(flat[:, at : at + size].reshape((packed.shape[0],) + shape))
        at += size
    return out


def on_device(
    sizes,
    tokens,
    seq_lengths,
    qkv_weight,
    out_weight,
    up_weight,
    down_weight,
    head_bias,
    hidden_bias,
    norm_gains,
    out_biases,
    cotangent,
):
    n_outer, n_core, n_ctx, n_tensor = sizes
    n_dp = n_outer * n_core
    shards = n_dp * n_ctx
    seq_count, local_len, width = tokens.shape
    row_count = seq_count * local_len
    total_len = n_ctx * local_len
    local_width = qkv_weight.shape[2]
    feature_rows = width // n_dp
    token_rows = tokens.reshape(row_count, width)

    def feature_slices(rows):
        return rows.reshape(row_count, n_dp, feature_rows).transpose(1, 0, 2)

    smalls = (head_bias, hidden_bias, norm_gains, out_biases)
    qkv_got, out_got, small_got, token_slices = exchange(
        sizes,
        1,
        [
            ("wg", qkv_weight.reshape(qkv_weight.shape[0], 3 * local_width)),
            ("wg", out_weight),
            ("wg", pack(smalls, 1, 2048)[0]),
            ("dp", feature_slices(token_rows)),
        ],
    )
    qkv_full = qkv_got.reshape(width, 3 * local_width)
    out_full = out_got.reshape(width, -1)
    up_full = lax.all_gather(up_weight, ("dp", "ctx"), axis=0, tiled=True)
    down_full = lax.all_gather(down_weight, ("dp", "ctx"), axis=0, tiled=True)
    head_full, hidden_full, gains_full, biases_full = (
        part.transpose(1, 0, 2).reshape(part.shape[1], -1)
        for part in unpack(small_got, [small.shape for small in smalls])
    )
    local_heads = head_full.shape[0]
    head_size = head_full.shape[1] // 2
    heads_here = local_heads // n_ctx
    group_width = heads_here * head_size
    bias_query = head_full[:, :head_size].reshape(local_width).astype(jnp.float32)
    bias_value = head_full[:, head_size:].reshape(local_width).astype(jnp.float32)
    bias_hidden = hidden_full.reshape(-1).astype(jnp.float32)
    gains_wide = gains_full.astype(jnp.float32)
    biases_wide = biases_full.astype(jnp.float32)

    def to_positions(chunks, parts):
        return (
            chunks.reshape(n_ctx, parts, seq_count, local_len, group_width)
            .transpose(1, 2, 0, 3, 4)
            .reshape(parts, seq_count, total_len, heads_here, head_size)
        )

    def by_position(parts):
        return (
            jnp.stack(parts)
            .reshape(len(parts), seq_count, n_ctx, local_len, group_width)
            .transpose(2, 0, 1, 3, 4)
            .reshape(n_ctx, len(parts), row_count, group_width)
        )

    def by_heads(rows, parts):
        return rows.reshape(row_count, parts, n_ctx, group_width).transpose(2, 1, 0, 3)

    def to_rows(chunks, parts):
        return (
            chunks.reshape(n_ctx, parts, row_count, group_width)
            .transpose(2, 1, 0, 3)
            .reshape(row_count, parts * local_width)
        )

    projected = jnp.dot(token_rows, qkv_full, preferred_element_type=jnp.float32)
    shift = jnp.concatenate([bias_query, jnp.zeros_like(bias_query), bias_value])
    projected = (projected + shift).astype(jnp.bfloat16)
    (qkv_chunks,) = exchange(sizes, 2, [("ctx", by_heads(projected, 3))])
    queries, key_rows, value_rows = to_positions(qkv_chunks, 3)
    valid = jnp.arange(total_len)[None, :] < seq_lengths[:, None]
    mixed, log_total = lax.map(attend_forward, (queries, key_rows, value_rows, valid))
    (mixed_chunks,) = exchange(sizes, 3, [("ctx", by_position([mixed]))])
    attn_flat = to_rows(mixed_chunks, 1)
    attn_part = contract_last(attn_flat, out_full)
    attn_other, attn_all = exchange(sizes, 4, [("swap", attn_part), ("dpg", attn_flat)])
    attn_proj = attn_part + jnp.sum(attn_other, axis=0)
    first_sum = token_rows.astype(jnp.float32) + attn_proj + biases_wide[0]
    normed_one, z_one, rstd_one = layer_norm(first_sum, gains_wide[0], biases_wide[1])
    normed_low = normed_one.astype(jnp.bfloat16)
    pre_act = jnp.dot(normed_low, up_full, preferred_element_type=jnp.float32) + bias_hidden
    activated, slope = gelu_parts(pre_act)
    hidden_low = activated.astype(jnp.bfloat16)
    mlp_part = contract_last(hidden_low, down_full)
    half = n_dp // 2
    mlp_other, hidden_all, token_low = exchange(
        sizes,
        5,
        [("swap", mlp_part), ("dpg", hidden_low), ("cg", token_slices[:half])],
    )
    mlp_out = mlp_part + jnp.sum(mlp_other, axis=0)
    second_sum = normed_one + mlp_out + biases_wide[2]
    result, z_two, rstd_two = layer_norm(second_sum, gains_wide[1], biases_wide[3])
    output = result.astype(jnp.bfloat16).reshape(seq_count, local_len, width)
    grad_out = cotangent.reshape(row_count, width).astype(jnp.float32)
    grad_two, gain_two_grad, shift_two_grad = norm_back(grad_out, z_two, rstd_two, gains_wide[1])
    grad_two_low = grad_two.astype(jnp.bfloat16)
    grad_hidden = jnp.dot(grad_two_low, down_full, preferred_element_type=jnp.float32)
    grad_pre = grad_hidden * slope
    grad_pre_low = grad_pre.astype(jnp.bfloat16)
    hidden_part = jnp.sum(grad_pre, axis=0).reshape(hidden_full.shape)
    normed_part = contract_last(grad_pre_low, up_full)
    normed_other, grad_pre_all, grad_two_slices, token_high = exchange(
        sizes,
        6,
        [
            ("swap", normed_part),
            ("dpg", grad_pre_low),
            ("dp", feature_slices(grad_two_low)),
            ("cg", token_slices[half:]),
        ],
    )

    def over_rows(slices, wide):
        return contract_first(
            slices.reshape(n_dp * row_count, feature_rows), wide.reshape(n_dp * row_count, -1)
        )

    down_grad = lax.psum_scatter(
        over_rows(grad_two_slices, hidden_all), "ctx", scatter_dimension=0, tiled=True
    )
    grad_normed = normed_part + jnp.sum(normed_other, axis=0) + grad_two
    grad_one, gain_one_grad, shift_one_grad = norm_back(grad_normed, z_one, rstd_one, gains_wide[0])
    grad_one_low = grad_one.astype(jnp.bfloat16)
    grad_attn = jnp.dot(grad_one_low, out_full, preferred_element_type=jnp.float32).astype(
        jnp.bfloat16
    )
    grad_chunks, grad_one_slices, normed_slices = exchange(
        sizes,
        7,
        [
            ("ctx", by_heads(grad_attn, 1)),
            ("dp", feature_slices(grad_one_low)),
            ("dp", feature_slices(normed_low)),
        ],
    )
    up_grad = lax.psum_scatter(
        over_rows(normed_slices, grad_pre_all), "ctx", scatter_dimension=0, tiled=True
    )
    grad_mixed = to_positions(grad_chunks, 1)[0]
    out_grad = over_rows(grad_one_slices, attn_all)
    grad_queries, grad_keys, grad_values = lax.map(
        attend_backward, (queries, key_rows, value_rows, valid, mixed, log_total, grad_mixed)
    )
    proj_parts = by_position(
        [part.astype(jnp.bfloat16) for part in (grad_queries, grad_keys, grad_values)]
    )
    proj_wide = proj_parts.transpose(0, 2, 1, 3).reshape(n_ctx * row_count, 3 * group_width)
    proj_chunks, proj_all = exchange(sizes, 8, [("ctx", proj_parts), ("dpg", proj_wide)])
    token_all = (
        jnp.concatenate([token_low, token_high], axis=1)
        .transpose(1, 0, 2, 3)
        .reshape(n_dp * n_ctx * row_count, feature_rows)
    )
    qkv_part = contract_first(token_all, proj_all.reshape(n_dp * n_ctx * row_count, -1))
    grad_proj = to_rows(proj_chunks, 3)
    input_part = contract_last(grad_proj, qkv_full)
    head_rows = jnp.concatenate(
        [jnp.sum(grad_queries, axis=(0, 1)), jnp.sum(grad_values, axis=(0, 1))], axis=1
    )
    head_part = lax.dynamic_update_slice(
        jnp.zeros((local_heads, 2 * head_size), jnp.float32),
        head_rows,
        (lax.axis_index("ctx") * heads_here, 0),
    )
    gains_part = jnp.stack([gain_one_grad, gain_two_grad])
    biases_part = jnp.stack(
        [jnp.sum(grad_one, axis=0), shift_one_grad, jnp.sum(grad_two, axis=0), shift_two_grad]
    )
    small_parts = [
        part.reshape(part.shape[0], shards, -1).transpose(1, 0, 2)
        for part in (head_part, hidden_part, gains_part, biases_part)
    ]
    input_other, small_sums, out_blocks, qkv_blocks = exchange(
        sizes,
        9,
        [
            ("swap", input_part),
            ("all", pack(small_parts, shards, 1024)),
            ("ctx", out_grad.reshape(n_ctx, feature_rows // n_ctx, -1)),
            ("ctx", qkv_part.reshape(n_ctx, feature_rows // n_ctx, -1)),
        ],
    )
    input_grad = (input_part + jnp.sum(input_other, axis=0) + grad_one).reshape(
        seq_count, local_len, width
    )
    qkv_grad = (
        qkv_blocks.reshape(n_ctx, -1, 3, group_width)
        .transpose(1, 2, 0, 3)
        .reshape(-1, 3, local_width)
    )
    small_grads = unpack(
        jnp.sum(small_sums, axis=0)[None], [part.shape[1:] for part in small_parts]
    )
    return (
        output,
        input_grad,
        qkv_grad,
        jnp.sum(out_blocks, axis=0),
        up_grad,
        down_grad,
        *(part[0] for part in small_grads),
    )


MESH = pl.DeviceIdType.MESH


def dot_nn(left, right):
    return jnp.dot(left, right, preferred_element_type=jnp.float32)


class Links:
    def __init__(self, send_sem, recv_sem, own_sem, partner):
        self.send_sem, self.recv_sem, self.own_sem = send_sem, recv_sem, own_sem
        self.partner, self.sent, self.used, self.kept = partner, [], 0, 0

    def put(self, source, target, to):
        number = self.used
        self.used += 1
        copy = pltpu.make_async_remote_copy(
            src_ref=source,
            dst_ref=target,
            send_sem=self.send_sem.at[number],
            recv_sem=self.recv_sem.at[number],
            device_id=to,
            device_id_type=MESH,
        )
        copy.start()
        self.sent.append(copy)
        return number

    def arrive(self, number, target):
        pltpu.make_async_remote_copy(
            src_ref=target,
            dst_ref=target,
            send_sem=self.send_sem.at[number],
            recv_sem=self.recv_sem.at[number],
            device_id=self.partner,
            device_id_type=MESH,
        ).wait_recv()

    def keep(self, source, target):
        copy = pltpu.make_async_copy(source, target, self.own_sem.at[self.kept])
        self.kept += 1
        copy.start()
        return copy

    def sent_all(self, number):
        self.sent[number].wait_send()
        self.sent[number] = None

    def close(self):
        for copy in self.sent:
            if copy is not None:
                copy.wait_send()


class RowGather:
    def __init__(self, net, at, source, slot, block):
        self.net, self.at, self.source, self.slot, self.block = net, at, source, slot, block

    def start(self):
        net, at = self.net, self.at
        mine = self.slot(at.dp, at.z)
        self.own = net.keep(self.source, mine)
        self.along = [net.put(self.source, mine, at.z_to(k)) for k in range(1, at.nz)]
        self.across = [(net.put(self.source, mine, at.x_to), at.z)]

    def cross(self):
        net, at = self.net, self.at
        for k in range(1, at.nz):
            origin = at.z_from(k)
            got = self.slot(at.dp, origin)
            net.arrive(self.along[k - 1], got)
            self.across.append((net.put(got, got, at.x_to), origin))
        self.own.wait()
        block = self.block(at.dp)
        self.near = net.put(block, block, at.c_to)

    def relay(self):
        net, at = self.net, self.at
        for number, origin in self.across:
            net.arrive(number, self.slot(at.x_dp, origin))
        block = self.block(at.x_dp)
        self.far = net.put(block, block, at.c_to)

    def finish(self):
        self.net.arrive(self.near, self.block(self.at.c_dp))
        self.net.arrive(self.far, self.block(self.at.xc_dp))


class Place:
    def __init__(self, nz):
        self.nz = nz
        self.dp, self.z, self.y = (lax.axis_index(name) for name in ("dp", "ctx", "tensor"))
        dp, z, y = self.dp, self.z, self.y
        self.x, self.c = dp // 2, dp % 2
        self.c_dp = self.x * 2 + 1 - self.c
        self.x_dp = (1 - self.x) * 2 + self.c
        self.xc_dp = (1 - self.x) * 2 + 1 - self.c
        self.x_to = {"dp": self.x_dp, "ctx": z, "tensor": y}
        self.c_to = {"dp": self.c_dp, "ctx": z, "tensor": y}
        self.xc_to = {"dp": self.xc_dp, "ctx": z, "tensor": y}
        self.y_to = {"dp": dp, "ctx": z, "tensor": 1 - y}

    def z_at(self, k):
        return (self.z + k) % self.nz

    def z_from(self, k):
        return (self.z + self.nz - k) % self.nz

    def z_to(self, k):
        return {"dp": self.dp, "ctx": self.z_at(k), "tensor": self.y}

    def zy_to(self, k):
        return {"dp": self.dp, "ctx": self.z_at(k), "tensor": 1 - self.y}

    def greet(self):
        peers = [self.x_to, self.c_to, self.xc_to, self.y_to]
        for k in range(1, self.nz):
            peers += [self.z_to(k), self.zy_to(k)]
        barrier = pltpu.get_barrier_semaphore()
        for peer in peers:
            pl.semaphore_signal(barrier, inc=1, device_id=peer, device_id_type=MESH)
        pl.semaphore_wait(barrier, len(peers))


def rows_at(index, size):
    return pl.ds(pl.multiple_of(index * size, size), size)


def row_sum(value):
    return jnp.sum(value, axis=0, keepdims=True)


def norm_back_rows(grad_out, normed, inv_std, gain):
    grad_normed = grad_out * gain
    first_mean = jnp.mean(grad_normed, axis=-1, keepdims=True)
    second_mean = jnp.mean(grad_normed * normed, axis=-1, keepdims=True)
    return inv_std * (grad_normed - first_mean - normed * second_mean)


def last_by_tiles(target, lefts, rights, tile=512):
    count = target.shape[1]
    tile = min(tile, count)

    def step(number, carry):
        columns = rows_at(number, tile)
        value = contract_last(lefts[0](), rights[0](columns))
        for left, right in zip(lefts[1:], rights[1:]):
            value += contract_last(left(), right(columns))
        target[:, columns] = value
        return carry

    lax.fori_loop(0, count // tile, step, 0)


class ColumnGrad:
    def __init__(self, net, at, turned, turned_all, wide, wide_all, total, got, swap, out):
        self.net, self.at = net, at
        self.turned, self.turned_all = turned, turned_all
        self.wide, self.wide_all = wide, wide_all
        self.total, self.got, self.swap, self.out = total, got, swap, out
        self.half = wide_all.shape[2]
        self.block = turned_all.shape[0]
        self.rows = turned.shape[1]

    def send_wide(self):
        net, at = self.net, self.at
        mine = self.wide.at[:, rows_at(at.c, self.half)]
        theirs = self.wide.at[:, rows_at(1 - at.c, self.half)]
        slot = self.wide_all.at[at.dp]
        self.waits_wide = [
            (net.put(mine, slot, at.x_to), at.x_dp),
            (net.put(theirs, slot, at.xc_to), at.xc_dp),
            (net.put(theirs, slot, at.c_to), at.c_dp),
        ]
        self.own_wide = net.keep(mine, slot)

    def send_turned(self):
        net, at = self.net, self.at
        mine = self.turned.at[rows_at(at.x, self.block)]
        theirs = self.turned.at[rows_at(1 - at.x, self.block)]
        slot = self.turned_all.at[:, rows_at(at.dp, self.rows)]
        self.waits_turned = [
            (net.put(theirs, slot, at.x_to), at.x_dp),
            (net.put(theirs, slot, at.xc_to), at.xc_dp),
            (net.put(mine, slot, at.c_to), at.c_dp),
        ]
        self.own_turned = net.keep(mine, slot)

    def multiply(self):
        net = self.net
        self.own_wide.wait()
        self.own_turned.wait()
        for number, dp in self.waits_wide:
            net.arrive(number, self.wide_all.at[dp])
        for number, dp in self.waits_turned:
            net.arrive(number, self.turned_all.at[:, rows_at(dp, self.rows)])
        tile = min(256, self.half)
        n_dp = self.wide_all.shape[0]

        def step(number, carry):
            columns = rows_at(number, tile)
            value = dot_nn(self.turned_all[:, : self.rows], self.wide_all[0, :, columns])
            for dp in range(1, n_dp):
                value += dot_nn(
                    self.turned_all[:, dp * self.rows : (dp + 1) * self.rows],
                    self.wide_all[dp, :, columns],
                )
            self.total[:, columns] = value
            return carry

        lax.fori_loop(0, self.half // tile, step, 0)

    def spread(self):
        net, at = self.net, self.at
        depth = self.block // (2 * at.nz)
        self.depth = depth
        self.waits = []
        for k in range(1, at.nz):
            for core in range(2):
                part = self.total.at[rows_at(core * at.nz + at.z_at(k), depth)]
                slot = self.got.at[k - 1, pl.ds(core * depth, depth)]
                self.waits.append((net.put(part, slot, at.z_to(k)), slot))

    def swap_cores(self):
        net, at, depth = self.net, self.at, self.depth
        for number, slot in self.waits:
            net.arrive(number, slot)

        def added(core):
            value = self.total[rows_at(core * at.nz + at.z, depth), :]
            for k in range(1, at.nz):
                value += self.got[k - 1, rows_at(core, depth), :]
            return value

        self.swap[...] = added(1 - at.c)
        self.last = net.put(self.swap, self.out.at[:, rows_at(at.c, self.half)], at.c_to)
        self.out[:, rows_at(at.c, self.half)] = added(at.c)

    def finish(self):
        self.net.arrive(self.last, self.out.at[:, rows_at(1 - self.at.c, self.half)])


def layer_kernel(dims, names, *refs):
    (nz, head_size, small_rows) = dims
    r = dict(zip(names, refs))

    class Refs:
        pass

    m = Refs()
    m.__dict__.update(r)
    at = Place(nz)
    net = Links(m.send_sem, m.recv_sem, m.own_sem, at.c_to)
    rows, width = m.tok.shape
    half = rows // 2
    total_len = rows * nz
    group = m.queries.shape[1]
    heads = group // head_size
    shard = m.outw.shape[0]
    part_rows = nz * shard
    local_width = m.outw.shape[1]
    hidden = m.upw.shape[1]
    groups_wide = width // 128
    bf16, f32 = jnp.bfloat16, jnp.float32
    mine, other = rows_at(at.y, half), rows_at(1 - at.y, half)
    at.greet()

    def gather(source, full):
        return RowGather(
            net,
            at,
            source,
            lambda dp, z: full.at[rows_at(dp * nz + z, source.shape[0])],
            lambda dp: full.at[rows_at(dp, nz * source.shape[0])],
        )

    def qkv_slot(g, dp, z):
        return m.wfull.at[g, rows_at(dp * nz + z, shard)]

    def qkv_block(g, dp):
        return m.wfull.at[g, rows_at(dp, part_rows)]

    own_qkv = net.keep(m.wq.at[at.z], qkv_slot(at.z, at.dp, at.z))
    qkv_along = [
        net.put(m.wq.at[at.z_at(k)], qkv_slot(at.z_at(k), at.dp, at.z), at.z_to(k))
        for k in range(1, nz)
    ]
    qkv_across = [(net.put(m.wq.at[at.z], qkv_slot(at.z, at.dp, at.z), at.x_to), at.z)]
    small = gather(m.small, m.small_all)
    small.start()
    own_rows = net.keep(m.tok, m.xall.at[rows_at(at.z, rows)])

    def half_of(z, y):
        return m.xall.at[rows_at(z * 2 + y, half)]

    token_along = [
        net.put(m.tok.at[mine], half_of(at.z, at.y), at.z_to(k)) for k in range(1, nz)
    ]
    outs = gather(m.outw, m.outf.at[at.y])
    outs.start()
    for k in range(1, nz):
        origin = at.z_from(k)
        got = qkv_slot(at.z, at.dp, origin)
        net.arrive(qkv_along[k - 1], got)
        qkv_across.append((net.put(got, got, at.x_to), origin))
    own_qkv.wait()
    near = qkv_block(at.z, at.dp)
    qkv_near = net.put(near, near, at.c_to)
    small.cross()
    token_y = []
    for k in range(1, nz):
        origin = at.z_from(k)
        got = half_of(origin, at.y)
        net.arrive(token_along[k - 1], got)
        token_y.append((net.put(got, got, at.y_to), origin))
    ups = gather(m.upw, m.up)
    ups.start()
    for number, origin in qkv_across:
        net.arrive(number, qkv_slot(at.z, at.x_dp, origin))
    far = qkv_block(at.z, at.x_dp)
    qkv_far = net.put(far, far, at.c_to)
    small.relay()
    outs.cross()
    small.finish()
    small_sum = m.small_all[:small_rows, :].astype(f32)
    for slot in range(1, 4 * nz):
        small_sum += m.small_all[slot * small_rows : (slot + 1) * small_rows, :].astype(f32)
    m.smalls[...] = small_sum
    for row in range(6):
        for j in range(groups_wide):
            at_row = row * groups_wide + j
            m.norms[row : row + 1, j * 128 : (j + 1) * 128] = m.smalls[at_row : at_row + 1, :]
    query_row = 6 * groups_wide
    value_row = query_row + nz
    hidden_row = value_row + nz
    for j in range(hidden // 128):
        m.hbias[:, j * 128 : (j + 1) * 128] = m.smalls[hidden_row + j : hidden_row + j + 1, :]
    net.arrive(qkv_near, qkv_block(at.z, at.c_dp))
    net.arrive(qkv_far, qkv_block(at.z, at.xc_dp))
    outs.relay()
    downs = gather(m.downw, m.down)
    own_rows.wait()
    for number, origin in token_y:
        net.arrive(number, half_of(origin, 1 - at.y))
    bias_q = m.smalls[pl.ds(query_row + at.z, 1), :]
    bias_v = m.smalls[pl.ds(value_row + at.z, 1), :]

    def project(block, carry):
        place = rows_at(block, rows)
        value = dot_nn(m.xall[place, :], m.wfull[at.z])
        m.queries[place, :] = (value[:, :group] + bias_q).astype(bf16)
        key = value[:, group : 2 * group]
        m.keys[place, :] = key.astype(bf16)
        m.keys_t[:, place] = key.T.astype(bf16)
        val = value[:, 2 * group :] + bias_v
        m.values[place, :] = val.astype(bf16)
        m.values_t[:, place] = val.T.astype(bf16)
        return carry

    lax.fori_loop(0, nz, project, 0)
    downs.start()
    outs.finish()
    y_rows = width // 2
    out_half = m.outf.at[at.y, rows_at(at.c, y_rows)]
    out_y = net.put(out_half, out_half, at.y_to)

    valid = lax.broadcasted_iota(jnp.int32, (total_len, 1), 0) < m.lens[0]
    lane_head = lax.broadcasted_iota(jnp.int32, (1, group), 1) // head_size
    row_head = lax.broadcasted_iota(jnp.int32, (group, 1), 0) // head_size

    def head_of(value, h):
        return jnp.where(lane_head == h, value, jnp.zeros_like(value))

    def scores_of(query):
        return jnp.where(valid, contract_last(m.keys[...], query) * SCALE, NEG_BIG)

    def attend(block):
        place = rows_at(block, rows)
        query = m.queries[place, :]
        mixed = jnp.zeros((group, rows), f32)
        for h in range(heads):
            score = scores_of(head_of(query, h))
            peak = jnp.max(score, axis=0, keepdims=True)
            grown = jnp.exp(score - peak)
            total = jnp.sum(grown, axis=0, keepdims=True)
            m.log_total[h : h + 1, place] = peak + jnp.log(total)
            probs = (grown * (1.0 / total)).astype(bf16)
            mixed = jnp.where(row_head == h, dot_nn(m.values_t[...], probs), mixed)
        m.mixed[place, :] = mixed.T.astype(bf16)

    def columns_of(y, z):
        return m.attn.at[:, rows_at(y * nz + z, group)]

    mixed_along = []
    for k in list(range(1, nz)) + [0]:
        attend(at.z_at(k))
        part = m.mixed.at[rows_at(at.z_at(k), rows)]
        if k:
            mixed_along.append(net.put(part, columns_of(at.y, at.z), at.z_to(k)))
            if k == 1:
                ups.cross()
        else:
            own_mixed = net.keep(part, columns_of(at.y, at.z))
            mixed_y = [(net.put(part, columns_of(at.y, at.z), at.y_to), at.z)]
    for k in range(1, nz):
        origin = at.z_from(k)
        got = columns_of(at.y, origin)
        net.arrive(mixed_along[k - 1], got)
        mixed_y.append((net.put(got, got, at.y_to), origin))
    got = m.outf.at[1 - at.y, rows_at(at.c, y_rows)]
    net.arrive(out_y, got)
    out_near = net.put(got, got, at.c_to)

    def turn_rows(block, carry):
        place = rows_at(block, rows)
        m.xall_t[:, place] = m.xall[place, :].T
        return carry

    lax.fori_loop(0, nz, turn_rows, 0)
    net.arrive(out_near, m.outf.at[1 - at.y, rows_at(1 - at.c, y_rows)])
    own_mixed.wait()
    for number, origin in mixed_y:
        net.arrive(number, columns_of(1 - at.y, origin))

    gain_one, gain_two = m.norms[0:1, :], m.norms[1:2, :]
    shift = [m.norms[2 + i : 3 + i, :] for i in range(4)]

    def first_norm(place, kept):
        first_sum = (
            m.tok[place, :].astype(f32)
            + contract_last(m.attn[place, :local_width], m.outf[0])
            + contract_last(m.attn[place, local_width:], m.outf[1])
            + shift[0]
        )
        normed, z_one, rstd = layer_norm(first_sum, gain_one, shift[1])
        if kept:
            m.normed[...] = normed
            m.z_one[...] = z_one
            m.rstd[...] = rstd
        m.normed_low[place, :] = normed.astype(bf16)
        m.normed_t[:, place] = normed.T.astype(bf16)

    first_norm(other, False)
    first_norm(mine, True)
    ups.relay()
    downs.cross()
    ups.finish()

    tile = min(512, hidden)

    def feed(place):
        def step(number, carry):
            columns = rows_at(number, tile)
            pre = dot_nn(m.normed_low[place, :], m.up[:, columns]) + m.hbias[:, columns]
            activated, slope = gelu_parts(pre)
            m.hid[place, columns] = activated.astype(bf16)
            m.slope[place, columns] = slope
            return carry

        lax.fori_loop(0, hidden // tile, step, 0)

    feed(other)
    feed(mine)
    downs.relay()
    down_grad = ColumnGrad(
        net, at, m.grad_two_t, m.grad_two_all, m.hid, m.hid_all, m.down_total, m.down_got, m.down_swap, m.down_grad
    )
    up_grad = ColumnGrad(
        net, at, m.normed_t, m.normed_all, m.grad_pre, m.grad_pre_all, m.up_total, m.up_got, m.up_swap, m.up_grad
    )
    out_grad = ColumnGrad(
        net,
        at,
        m.grad_one_t,
        m.grad_one_all,
        m.attn.at[:, rows_at(at.y, local_width)],
        m.attn_all,
        m.out_total,
        m.out_got,
        m.out_swap,
        m.out_grad,
    )
    downs.finish()
    down_grad.send_wide()
    last_by_tiles(m.part_a, [lambda: m.hid[other, :]], [lambda at_rows: m.down[at_rows, :]])
    part_a = net.put(m.part_a, m.got_a, at.y_to)
    last_by_tiles(m.kept, [lambda: m.hid[mine, :]], [lambda at_rows: m.down[at_rows, :]])
    up_grad.send_turned()
    out_grad.send_wide()
    net.arrive(part_a, m.got_a)
    second_sum = m.normed[...] + (m.kept[...] + m.got_a[...]) + shift[2]
    result, z_two, rstd_two = layer_norm(second_sum, gain_two, shift[3])
    grad_out = m.cot[mine, :].astype(f32)
    grad_two = norm_back_rows(grad_out, z_two, rstd_two, gain_two)
    m.grad_two[...] = grad_two
    m.grad_two_low[mine, :] = grad_two.astype(bf16)
    two_y = net.put(m.grad_two_low.at[mine], m.grad_two_low.at[mine], at.y_to)
    m.output[mine, :] = result.astype(bf16)
    output_y = net.put(m.output.at[mine], m.output.at[mine], at.y_to)
    sums = {1: row_sum(grad_out * z_two), 5: row_sum(grad_out), 4: row_sum(grad_two)}

    m.hidden_sum[...] = jnp.zeros_like(m.hidden_sum)

    def feed_back(place):
        def step(number, carry):
            columns = rows_at(number, tile)
            grad_hidden = dot_nn(m.grad_two_low[place, :], m.down[:, columns])
            grad_pre = grad_hidden * m.slope[place, columns]
            m.grad_pre[place, columns] = grad_pre.astype(bf16)
            m.hidden_sum[:, columns] += row_sum(grad_pre)
            return carry

        lax.fori_loop(0, hidden // tile, step, 0)

    feed_back(mine)
    net.arrive(two_y, m.grad_two_low.at[other])
    feed_back(other)
    net.sent_all(part_a)
    last_by_tiles(m.part_a, [lambda: m.grad_pre[other, :]], [lambda at_rows: m.up[at_rows, :]])
    part_b = net.put(m.part_a, m.got_b, at.y_to)
    m.grad_two_t[...] = m.grad_two_low[...].T
    down_grad.send_turned()
    up_grad.send_wide()
    last_by_tiles(m.kept, [lambda: m.grad_pre[mine, :]], [lambda at_rows: m.up[at_rows, :]])
    net.arrive(part_b, m.got_b)
    grad_normed = m.kept[...] + m.got_b[...] + m.grad_two[...]
    z_mine = m.z_one[...]
    grad_one = norm_back_rows(grad_normed, z_mine, m.rstd[...], gain_one)
    m.grad_one[...] = grad_one
    m.grad_one_low[mine, :] = grad_one.astype(bf16)
    sums[0] = row_sum(grad_normed * z_mine)
    sums[3] = row_sum(grad_normed)
    sums[2] = row_sum(grad_one)
    def back_step(y, carry):
        value = dot_nn(m.grad_one_low[mine, :], m.outf[y])
        m.grad_attn[:, rows_at(y, local_width)] = value.astype(bf16)
        return carry

    lax.fori_loop(0, 2, back_step, 0)

    def attn_part(y, z):
        return m.grad_attn.at[:, rows_at(y * nz + z, group)]

    my_slot = m.grad_mixed.at[rows_at(at.z * 2 + at.y, half)]
    grad_along = []
    for k in range(1, nz):
        grad_along.append((net.put(attn_part(at.y, at.z_at(k)), my_slot, at.z_to(k)), at.z_from(k), at.y))
        grad_along.append(
            (net.put(attn_part(1 - at.y, at.z_at(k)), my_slot, at.zy_to(k)), at.z_from(k), 1 - at.y)
        )
    grad_along.append((net.put(attn_part(1 - at.y, at.z), my_slot, at.y_to), at.z, 1 - at.y))
    own_grad = net.keep(attn_part(at.y, at.z), my_slot)
    one_y = net.put(m.grad_one_low.at[mine], m.grad_one_low.at[mine], at.y_to)

    late = []
    for k in range(1, nz):
        for j in range(1, nz):
            g = at.z_at(k + j)
            target = qkv_slot(g, at.dp, at.z)
            late.append((net.put(m.wq.at[g], target, at.z_to(k)), k, j))
    late_own = [
        net.keep(m.wq.at[at.z_at(j)], qkv_slot(at.z_at(j), at.dp, at.z)) for j in range(1, nz)
    ]
    for number, origin, y in grad_along:
        net.arrive(number, m.grad_mixed.at[rows_at(origin * 2 + y, half)])
    own_grad.wait()
    net.arrive(one_y, m.grad_one_low.at[other])
    m.grad_one_t[...] = m.grad_one_low[...].T
    out_grad.send_turned()

    m.acc_keys[...] = jnp.zeros_like(m.acc_keys)
    m.acc_values[...] = jnp.zeros_like(m.acc_values)
    ones_row = jnp.ones((8, group), f32)

    def attend_back(block, carry):
        place = rows_at(block, rows)
        query = m.queries[place, :]
        grad = m.grad_mixed[place, :]
        product = grad.astype(f32) * m.mixed[place, :].astype(f32)
        turned = product.T
        grad_query = jnp.zeros((group, rows), f32)
        grad_keys = jnp.zeros((total_len, group), f32)
        grad_values = jnp.zeros((total_len, group), f32)
        for h in range(heads):
            query_h = head_of(query, h)
            grad_h = head_of(grad, h)
            probs = jnp.exp(scores_of(query_h) - m.log_total[h : h + 1, place])
            grad_values += dot_nn(probs.astype(bf16), grad_h)
            inner = row_sum(turned[h * head_size : (h + 1) * head_size, :])
            grad_probs = contract_last(m.values[...], grad_h)
            grad_scores = (probs * (grad_probs - inner)).astype(bf16)
            grad_keys += dot_nn(grad_scores, query_h)
            grad_query = jnp.where(row_head == h, dot_nn(m.keys_t[...], grad_scores), grad_query)
        m.acc_keys[...] += grad_keys
        m.acc_values[...] += grad_values
        grad_query = grad_query.T * SCALE
        m.grad_proj[place, :group] = grad_query.astype(bf16)
        return carry + row_sum(grad_query)

    query_sum = lax.fori_loop(0, nz, attend_back, jnp.zeros((1, group), f32))
    m.grad_proj[:, group : 2 * group] = (m.acc_keys[...] * SCALE).astype(bf16)
    m.grad_proj[:, 2 * group :] = m.acc_values[...].astype(bf16)
    value_sum = row_sum(m.acc_values[...])
    proj_along = [
        net.put(m.grad_proj.at[rows_at(at.z_at(k), rows)], m.proj_rows.at[at.z], at.z_to(k))
        for k in range(1, nz)
    ]
    own_proj = net.keep(m.grad_proj.at[rows_at(at.z, rows)], m.proj_rows.at[at.z])

    m.small_sum[...] = jnp.zeros_like(m.small_sum)
    for row in range(6):
        for j in range(groups_wide):
            at_row = row * groups_wide + j
            m.small_sum[at_row : at_row + 1, :] = sums[row][:, j * 128 : (j + 1) * 128]
    m.small_sum[pl.ds(query_row + at.z, 1), :] = query_sum
    m.small_sum[pl.ds(value_row + at.z, 1), :] = value_sum
    for j in range(hidden // 128):
        m.small_sum[hidden_row + j : hidden_row + j + 1, :] = m.hidden_sum[:, j * 128 : (j + 1) * 128]
    small_along = [net.put(m.small_sum, m.small_got.at[k - 1], at.z_to(k)) for k in range(1, nz)]

    down_grad.multiply()
    down_grad.spread()
    late_x = []
    for number, k, j in late:
        got = qkv_slot(at.z_at(j), at.dp, at.z_from(k))
        net.arrive(number, got)
    for copy in late_own:
        copy.wait()
    for j in range(1, nz):
        block = qkv_block(at.z_at(j), at.dp)
        late_x.append((net.put(block, block, at.x_to), net.put(block, block, at.c_to), j))
    def qkv_step(block, carry):
        place = rows_at(block, rows)
        m.qkv_total[place, :] = dot_nn(m.xall_t[place, :], m.grad_proj[...])
        return carry

    lax.fori_loop(0, width // rows, qkv_step, 0)
    core_waits = []
    for x in range(2):
        part = m.qkv_total.at[rows_at(x * 2 + 1 - at.c, part_rows)]
        core_waits.append(net.put(part, m.qkv_core.at[x], at.c_to))
    up_grad.multiply()
    up_grad.spread()
    for x in range(2):
        net.arrive(core_waits[x], m.qkv_core.at[x])
    m.qkv_part[...] = m.qkv_total[rows_at(at.x_dp, part_rows), :] + m.qkv_core[1 - at.x]
    qkv_x = net.put(m.qkv_part, m.qkv_got, at.x_to)
    out_grad.multiply()
    out_grad.spread()
    for k in range(1, nz):
        net.arrive(small_along[k - 1], m.small_got.at[k - 1])
    value = m.small_sum[...]
    for k in range(1, nz):
        value += m.small_got[k - 1]
    m.small_two[...] = value
    small_x = net.put(m.small_two, m.small_got.at[nz - 1], at.x_to)
    late_c = []
    for across, near, j in late_x:
        block = qkv_block(at.z_at(j), at.x_dp)
        net.arrive(across, block)
        late_c.append((net.put(block, block, at.c_to), near, j))
    for across, near, j in late_c:
        net.arrive(near, qkv_block(at.z_at(j), at.c_dp))
        net.arrive(across, qkv_block(at.z_at(j), at.xc_dp))
    own_proj.wait()
    for k in range(1, nz):
        net.arrive(proj_along[k - 1], m.proj_rows.at[at.z_from(k)])

    def input_part(target, place):
        last_by_tiles(
            target,
            [lambda g=g: m.proj_rows[g, place, :] for g in range(nz)],
            [lambda at_rows, g=g: m.wfull[g, at_rows, :] for g in range(nz)],
        )

    net.sent_all(part_b)
    input_part(m.part_a, other)
    part_c = net.put(m.part_a, m.got_c, at.y_to)
    input_part(m.kept, mine)
    net.arrive(qkv_x, m.qkv_got)
    m.qkv_sum[...] = (
        m.qkv_total[rows_at(at.dp, part_rows), :] + m.qkv_core[at.x] + m.qkv_got[...]
    )
    qkv_z = [
        net.put(m.qkv_sum.at[rows_at(at.z_at(k), shard)], m.qkv_grad.at[at.z], at.z_to(k))
        for k in range(1, nz)
    ]
    m.qkv_grad[at.z] = m.qkv_sum[rows_at(at.z, shard), :]
    net.arrive(small_x, m.small_got.at[nz - 1])
    m.small_three[...] = m.small_two[...] + m.small_got[nz - 1]
    small_c = net.put(m.small_three, m.small_got.at[nz], at.c_to)
    net.arrive(part_c, m.got_c)
    m.input_grad[mine, :] = m.kept[...] + m.got_c[...] + m.grad_one[...]
    input_y = net.put(m.input_grad.at[mine], m.input_grad.at[mine], at.y_to)
    net.arrive(small_c, m.small_got.at[nz])
    m.small_four[...] = m.small_three[...] + m.small_got[nz]
    small_y = net.put(m.small_four, m.small_got.at[nz + 1], at.y_to)
    down_grad.swap_cores()
    up_grad.swap_cores()
    out_grad.swap_cores()
    net.arrive(small_y, m.small_got.at[nz + 1])
    shared = lax.broadcasted_iota(jnp.int32, (small_rows, 1), 0) < query_row
    m.small_grad[...] = m.small_four[...] + jnp.where(shared, m.small_got[nz + 1], 0.0)
    for k in range(1, nz):
        net.arrive(qkv_z[k - 1], m.qkv_grad.at[at.z_from(k)])
    net.arrive(output_y, m.output.at[other])
    net.arrive(input_y, m.input_grad.at[other])
    for item in (down_grad, up_grad, out_grad):
        item.finish()
    net.close()


def fused(
    sizes,
    tokens,
    seq_lengths,
    qkv_weight,
    out_weight,
    up_weight,
    down_weight,
    head_bias,
    hidden_bias,
    norm_gains,
    out_biases,
    cotangent,
):
    n_outer, n_core, nz, n_tensor = sizes
    n_dp = n_outer * n_core
    shards = n_dp * nz
    _, rows, width = tokens.shape
    shard, _, local_width = qkv_weight.shape
    hidden = up_weight.shape[1]
    head_size = head_bias.shape[1] * shards // 2
    group = local_width // nz
    total_len = rows * nz
    bf16, f32 = jnp.bfloat16, jnp.float32
    place = lax.axis_index("dp") * nz + lax.axis_index("ctx")

    def spread(part):
        wide = part.shape[1] * shards
        return lax.dynamic_update_slice(
            jnp.zeros((part.shape[0], wide), bf16), part, (0, place * part.shape[1])
        )

    head_wide = spread(head_bias)
    pieces = [
        spread(norm_gains),
        spread(out_biases),
        head_wide[:, :head_size],
        head_wide[:, head_size:],
        spread(hidden_bias),
    ]
    small = jnp.concatenate([piece.reshape(-1, 128) for piece in pieces], axis=0)
    used = small.shape[0]
    small_rows = -(-used // 16) * 16
    small = jnp.pad(small, ((0, small_rows - used), (0, 0)))
    wq = qkv_weight.reshape(shard, 3, nz, group).transpose(2, 0, 1, 3).reshape(nz, shard, 3 * group)
    tok = tokens.reshape(rows, width)
    cot = cotangent.reshape(rows, width)
    half = rows // 2
    ins = dict(
        lens=seq_lengths, tok=tok, cot=cot, wq=wq, outw=out_weight, upw=up_weight, downw=down_weight, small=small
    )
    outs = dict(
        output=((rows, width), bf16),
        input_grad=((rows, width), f32),
        qkv_grad=((nz, shard, 3 * group), f32),
        out_grad=((shard, local_width), f32),
        up_grad=((shard, hidden), f32),
        down_grad=((shard, hidden), f32),
        small_grad=((small_rows, 128), f32),
    )
    block = 2 * nz * shard
    part_rows = nz * shard
    scratch = dict(
        small_all=((shards * small_rows, 128), bf16),
        smalls=((small_rows, 128), f32),
        norms=((8, width), f32),
        hbias=((1, hidden), f32),
        wfull=((nz, width, 3 * group), bf16),
        xall=((total_len, width), bf16),
        xall_t=((width, total_len), bf16),
        outf=((2, width, local_width), bf16),
        up=((width, hidden), bf16),
        down=((width, hidden), bf16),
        queries=((total_len, group), bf16),
        keys=((total_len, group), bf16),
        values=((total_len, group), bf16),
        keys_t=((group, total_len), bf16),
        values_t=((group, total_len), bf16),
        mixed=((total_len, group), bf16),
        log_total=((max(8, group // head_size), total_len), f32),
        attn=((rows, width), bf16),
        normed=((half, width), f32),
        z_one=((half, width), f32),
        rstd=((half, 1), f32),
        normed_low=((rows, width), bf16),
        normed_t=((width, rows), bf16),
        hid=((rows, hidden), bf16),
        slope=((rows, hidden), f32),
        part_a=((half, width), f32),
        got_a=((half, width), f32),
        got_b=((half, width), f32),
        got_c=((half, width), f32),
        kept=((half, width), f32),
        grad_two=((half, width), f32),
        grad_two_low=((rows, width), bf16),
        grad_two_t=((width, rows), bf16),
        grad_pre=((rows, hidden), bf16),
        hidden_sum=((1, hidden), f32),
        grad_one=((half, width), f32),
        grad_one_low=((rows, width), bf16),
        grad_one_t=((width, rows), bf16),
        grad_attn=((half, width), bf16),
        grad_mixed=((total_len, group), bf16),
        acc_keys=((total_len, group), f32),
        acc_values=((total_len, group), f32),
        grad_proj=((total_len, 3 * group), bf16),
        proj_rows=((nz, rows, 3 * group), bf16),
        small_sum=((small_rows, 128), f32),
        small_two=((small_rows, 128), f32),
        small_three=((small_rows, 128), f32),
        small_four=((small_rows, 128), f32),
        small_got=((nz + 2, small_rows, 128), f32),
        qkv_total=((width, 3 * group), f32),
        qkv_core=((2, part_rows, 3 * group), f32),
        qkv_part=((part_rows, 3 * group), f32),
        qkv_got=((part_rows, 3 * group), f32),
        qkv_sum=((part_rows, 3 * group), f32),
        hid_all=((n_dp, rows, hidden // 2), bf16),
        grad_two_all=((block, n_dp * rows), bf16),
        down_total=((block, hidden // 2), f32),
        down_got=((nz - 1, 2 * shard, hidden // 2), f32),
        down_swap=((shard, hidden // 2), f32),
        grad_pre_all=((n_dp, rows, hidden // 2), bf16),
        normed_all=((block, n_dp * rows), bf16),
        up_total=((block, hidden // 2), f32),
        up_got=((nz - 1, 2 * shard, hidden // 2), f32),
        up_swap=((shard, hidden // 2), f32),
        attn_all=((n_dp, rows, local_width // 2), bf16),
        grad_one_all=((block, n_dp * rows), bf16),
        out_total=((block, local_width // 2), f32),
        out_got=((nz - 1, 2 * shard, local_width // 2), f32),
        out_swap=((shard, local_width // 2), f32),
    )
    names = tuple(ins) + tuple(outs) + tuple(scratch) + ("send_sem", "recv_sem", "own_sem")
    vmem = pl.BlockSpec(memory_space=pltpu.VMEM)
    copies = 200
    result = pl.pallas_call(
        functools.partial(layer_kernel, (nz, head_size, small_rows), names),
        out_shape=tuple(jax.ShapeDtypeStruct(*spec) for spec in outs.values()),
        in_specs=[pl.BlockSpec(memory_space=pltpu.SMEM)] + [vmem] * (len(ins) - 1),
        out_specs=(vmem,) * len(outs),
        scratch_shapes=[pltpu.VMEM(*spec) for spec in scratch.values()]
        + [
            pltpu.SemaphoreType.DMA((copies,)),
            pltpu.SemaphoreType.DMA((copies,)),
            pltpu.SemaphoreType.DMA((40,)),
        ],
        compiler_params=pltpu.CompilerParams(
            collective_id=1, has_side_effects=True, vmem_limit_bytes=64 * 2**20 - 2**18
        ),
        name="layer",
    )(*ins.values())
    output, input_grad, qkv_grad, out_grad, up_grad, down_grad, small_grad = result
    qkv_grad = (
        qkv_grad.reshape(nz, shard, 3, group).transpose(1, 2, 0, 3).reshape(shard, 3, local_width)
    )

    def mine(part, like):
        return lax.dynamic_slice(
            part.reshape(like.shape[0], -1), (0, place * like.shape[1]), like.shape
        )

    at, cut = 0, []
    for piece in pieces:
        count = piece.size // 128
        cut.append(small_grad[at : at + count])
        at += count
    heads = head_bias.shape[0]
    head_grad = jnp.concatenate(
        [cut[2].reshape(heads, head_size), cut[3].reshape(heads, head_size)], axis=1
    )
    return (
        output.reshape(tokens.shape),
        input_grad.reshape(tokens.shape),
        qkv_grad,
        out_grad,
        up_grad,
        down_grad,
        mine(head_grad, head_bias),
        mine(cut[4], hidden_bias),
        mine(cut[0], norm_gains),
        mine(cut[1], out_biases),
    )


def fits(sizes, mesh):
    n_outer, n_core, nz, n_tensor = sizes
    return n_outer == 2 and n_core == 2 and n_tensor == 2 and nz == 4


def solution(mesh):
    in_specs = (
        P("dp", "ctx", None),
        P("dp"),
        P(("dp", "ctx"), None, "tensor"),
        P(("dp", "ctx"), "tensor"),
        P(("dp", "ctx"), "tensor"),
        P(("dp", "ctx"), "tensor"),
        P("tensor", ("dp", "ctx")),
        P("tensor", ("dp", "ctx")),
        P(None, ("dp", "ctx")),
        P(None, ("dp", "ctx")),
        P("dp", "ctx", None),
    )
    out_specs = (
        P("dp", "ctx", None),
        P("dp", "ctx", None),
        P(("dp", "ctx"), None, "tensor"),
        P(("dp", "ctx"), "tensor"),
        P(("dp", "ctx"), "tensor"),
        P(("dp", "ctx"), "tensor"),
        P("tensor", ("dp", "ctx")),
        P("tensor", ("dp", "ctx")),
        P(None, ("dp", "ctx")),
        P(None, ("dp", "ctx")),
    )
    n_core = 2 if mesh.shape["dp"] % 2 == 0 else 1
    sizes = (mesh.shape["dp"] // n_core, n_core, mesh.shape["ctx"], mesh.shape["tensor"])
    body = fused if fits(sizes, mesh) else on_device
    return jax.shard_map(
        functools.partial(body, sizes), mesh=mesh, in_specs=in_specs, out_specs=out_specs, check_vma=False
    )
```

```python
import functools
import math

import jax
import jax.numpy as jnp
from jax import lax
from jax.experimental import pallas as pl
from jax.experimental.pallas import tpu as pltpu
from jax.sharding import PartitionSpec as P

EPSILON = 1e-05
SCALE = 0.125
NEG_BIG = -1000000000.0
INV_ROOT_TWO = 1.0 / math.sqrt(2.0)
INV_ROOT_TWO_PI = 1.0 / math.sqrt(2.0 * math.pi)


def contract_last(left, right):
    return lax.dot_general(
        left, right, (((1,), (1,)), ((), ())), preferred_element_type=jnp.float32
    )


def contract_first(left, right):
    return lax.dot_general(
        left, right, (((0,), (0,)), ((), ())), preferred_element_type=jnp.float32
    )


def layer_norm(hidden_in, gain, shift):
    centred = hidden_in - jnp.mean(hidden_in, axis=-1, keepdims=True)
    variance = jnp.mean(centred * centred, axis=-1, keepdims=True)
    inv_std = lax.rsqrt(variance + EPSILON)
    normed = centred * inv_std
    return (normed * gain + shift, normed, inv_std)


def norm_back(grad_out, normed, inv_std, gain):
    grad_normed = grad_out * gain
    first_mean = jnp.mean(grad_normed, axis=-1, keepdims=True)
    second_mean = jnp.mean(grad_normed * normed, axis=-1, keepdims=True)
    grad_in = inv_std * (grad_normed - first_mean - normed * second_mean)
    return (grad_in, jnp.sum(grad_out * normed, axis=0), jnp.sum(grad_out, axis=0))


def gelu_parts(pre_act):
    cdf_val = 0.5 * (1.0 + jax.scipy.special.erf(pre_act * INV_ROOT_TWO))
    return (
        pre_act * cdf_val,
        cdf_val + pre_act * jnp.exp(-0.5 * pre_act * pre_act) * INV_ROOT_TWO_PI,
    )


def block_scores(queries, key_rows, valid):
    scores = (
        jnp.einsum("qhd,khd->hqk", queries, key_rows, preferred_element_type=jnp.float32) * SCALE
    )
    return jnp.where(valid[None, None, :], scores, NEG_BIG)


def attend_forward(inputs):
    queries, key_rows, value_rows, valid = inputs
    scores = block_scores(queries, key_rows, valid)
    peak = jnp.max(scores, axis=-1, keepdims=True)
    log_total = peak + jnp.log(jnp.sum(jnp.exp(scores - peak), axis=-1, keepdims=True))
    probs = jnp.exp(scores - log_total).astype(jnp.bfloat16)
    mixed = jnp.einsum(
        "hqk,khd->qhd", probs, value_rows, preferred_element_type=jnp.float32
    ).astype(jnp.bfloat16)
    return (mixed, log_total)


def attend_backward(inputs):
    queries, key_rows, value_rows, valid, mixed, log_total, grad_mixed = inputs
    scores = block_scores(queries, key_rows, valid)
    probs = jnp.exp(scores - log_total)
    grad_values = jnp.einsum(
        "hqk,qhd->khd", probs.astype(jnp.bfloat16), grad_mixed, preferred_element_type=jnp.float32
    )
    grad_probs = jnp.einsum(
        "qhd,khd->hqk", grad_mixed, value_rows, preferred_element_type=jnp.float32
    )
    inner = jnp.einsum("qhd,qhd->hq", grad_mixed.astype(jnp.float32), mixed.astype(jnp.float32))
    grad_scores = (probs * (grad_probs - inner[:, :, None])).astype(jnp.bfloat16)
    grad_queries = (
        jnp.einsum("hqk,khd->qhd", grad_scores, key_rows, preferred_element_type=jnp.float32)
        * SCALE
    )
    grad_keys = (
        jnp.einsum("hqk,qhd->khd", grad_scores, queries, preferred_element_type=jnp.float32) * SCALE
    )
    return (grad_queries, grad_keys, grad_values)


def comm_kernel(sizes, kinds, copies, *refs):
    n_outer, n_core, n_ctx, n_tensor = sizes
    count = len(kinds)
    ins, outs = refs[:count], refs[count : 2 * count]
    send_sem, recv_sem, own_sem = refs[2 * count :]
    dp, ctx, tensor = (lax.axis_index(name) for name in ("dp", "ctx", "tensor"))
    outer, core = dp // n_core, dp % n_core

    def coords(offset, sign=1):
        def move(at, step, size):
            return at if step == 0 else (at + (step if sign > 0 else size - step)) % size

        outer_at = move(outer, offset[0], n_outer)
        core_at = move(core, offset[1], n_core)
        return outer_at * n_core + core_at, move(ctx, offset[2], n_ctx), move(tensor, offset[3], n_tensor)

    def device(offset):
        dp_at, ctx_at, tensor_at = coords(offset)
        return {"dp": dp_at, "ctx": ctx_at, "tensor": tensor_at}

    offsets = peer_offsets(sizes, kinds)
    barrier = pltpu.get_barrier_semaphore()
    for offset in offsets:
        pl.semaphore_signal(
            barrier, inc=1, device_id=device(offset), device_id_type=pl.DeviceIdType.MESH
        )
    pl.semaphore_wait(barrier, len(offsets))

    started, used = [], [0]

    def put(source, target, offset):
        number = used[0]
        used[0] += 1
        copy = pltpu.make_async_remote_copy(
            src_ref=source,
            dst_ref=target,
            send_sem=send_sem.at[number],
            recv_sem=recv_sem.at[number],
            device_id=device(offset),
            device_id_type=pl.DeviceIdType.MESH,
        )
        copy.start()
        started.append(copy)
        return number

    def arrived(number, target, offset):
        pltpu.make_async_remote_copy(
            src_ref=target,
            dst_ref=target,
            send_sem=send_sem.at[number],
            recv_sem=recv_sem.at[number],
            device_id=device(offset),
            device_id_type=pl.DeviceIdType.MESH,
        ).wait_recv()

    partner = (0, 1, 0, 0)
    pending, own_copies = [], []
    first = {}
    for at, kind in enumerate(kinds):
        source, target = ins[at], outs[at]
        index = functools.partial(slot_of, kind, n_ctx)
        mine = index(*coords((0, 0, 0, 0)))
        if kind == "swap":
            for offset in direct_offsets(sizes, kind):
                number = put(source, target.at[offset[3] - 1], offset)
                pending.append((number, target.at[offset[3] - 1], offset))
            continue
        if kind in ("ctx", "cg", "dp", "all"):
            for offset in direct_offsets(sizes, kind):
                block = source if kind == "cg" else source.at[index(*coords(offset))]
                number = put(block, target.at[mine], offset)
                pending.append((number, target.at[index(*coords(offset, -1))], offset))
            block = source if kind == "cg" else source.at[mine]
            own = pltpu.make_async_copy(block, target.at[mine], own_sem.at[at])
        else:
            stage = []
            if kind == "wg":
                for step in range(1, n_ctx):
                    offset = (0, 0, step, 0)
                    stage.append((put(source, target.at[mine], offset), offset))
            crossing = []
            for step in range(1, n_outer):
                offset = (step, 0, 0, 0)
                crossing.append((put(source, target.at[mine], offset), offset, (0, 0, 0, 0)))
            pending.append(
                (put(source, target.at[mine], partner), target.at[index(*coords(partner, -1))], partner)
            )
            own = pltpu.make_async_copy(source, target.at[mine], own_sem.at[at])
            first[at] = (stage, crossing)
        own.start()
        own_copies.append(own)
    for at in first:
        target = outs[at]
        index = functools.partial(slot_of, kinds[at], n_ctx)
        stage, crossing = first[at]
        for number, offset in stage:
            slot = index(*coords(offset, -1))
            arrived(number, target.at[slot], offset)
            for step in range(1, n_outer):
                across = (step, 0, 0, 0)
                crossing.append((put(target.at[slot], target.at[slot], across), across, offset))
            both = (0, 1, offset[2], 0)
            pending.append(
                (put(target.at[slot], target.at[slot], partner), target.at[index(*coords(both, -1))], partner)
            )
    for at in first:
        target = outs[at]
        index = functools.partial(slot_of, kinds[at], n_ctx)
        for number, across, offset in first[at][1]:
            origin = (across[0], 0, offset[2], 0)
            slot = index(*coords(origin, -1))
            arrived(number, target.at[slot], across)
            both = (across[0], 1, offset[2], 0)
            pending.append(
                (put(target.at[slot], target.at[slot], partner), target.at[index(*coords(both, -1))], partner)
            )
    for number, target, offset in pending:
        arrived(number, target, offset)
    for own in own_copies:
        own.wait()
    for copy in started:
        copy.wait_send()


def slot_of(kind, n_ctx, dp_at, ctx_at, tensor_at):
    if kind in ("ctx", "cg"):
        return ctx_at
    if kind in ("dp", "dpg"):
        return dp_at
    return dp_at * n_ctx + ctx_at


def direct_offsets(sizes, kind):
    n_outer, n_core, n_ctx, n_tensor = sizes
    if kind == "swap":
        return [(0, 0, 0, step) for step in range(1, n_tensor)]
    if kind in ("ctx", "cg"):
        return [(0, 0, step, 0) for step in range(1, n_ctx)]
    ctx_steps = range(n_ctx) if kind == "all" else range(1)
    return [
        (o, c, k, 0) for k in ctx_steps for o in range(n_outer) for c in range(n_core) if o + c + k
    ]


def peer_offsets(sizes, kinds):
    n_outer, n_core, n_ctx, n_tensor = sizes
    found = set()
    for kind in kinds:
        if kind in ("wg", "dpg"):
            found.update((o, 0, 0, 0) for o in range(1, n_outer))
            found.add((0, 1, 0, 0))
            if kind == "wg":
                found.update((0, 0, k, 0) for k in range(1, n_ctx))
        else:
            found.update(direct_offsets(sizes, kind))
    return sorted(found)


def exchange(sizes, number, ops):
    n_outer, n_core, n_ctx, n_tensor = sizes
    n_dp = n_outer * n_core
    kinds = tuple(kind for kind, _ in ops)
    shapes, copies, moved = [], 0, 0
    for kind, array in ops:
        if kind == "swap":
            lead, sends = (n_tensor - 1,), n_tensor - 1
        elif kind == "dpg":
            lead, sends = (n_dp,), n_dp - 1
        elif kind == "cg":
            lead, sends = (n_ctx,), n_ctx - 1
        elif kind == "wg":
            lead, sends = (n_dp * n_ctx,), n_dp * n_ctx - 1
        else:
            lead, sends = (), array.shape[0] - 1
        shapes.append(jax.ShapeDtypeStruct(lead + array.shape, array.dtype))
        copies += sends
        moved += math.prod(lead + array.shape) * array.dtype.itemsize
    vmem = pl.BlockSpec(memory_space=pltpu.VMEM)
    return pl.pallas_call(
        functools.partial(comm_kernel, sizes, kinds, copies),
        out_shape=tuple(shapes),
        in_specs=[vmem] * len(ops),
        out_specs=tuple(
            pl.BlockSpec(memory_space=pl.ANY) if kind == "wg" else vmem for kind in kinds
        ),
        scratch_shapes=[
            pltpu.SemaphoreType.DMA((copies,)),
            pltpu.SemaphoreType.DMA((copies,)),
            pltpu.SemaphoreType.DMA((len(ops),)),
        ],
        compiler_params=pltpu.CompilerParams(
            collective_id=number, has_side_effects=True, vmem_limit_bytes=60 * 2**20
        ),
        cost_estimate=pl.CostEstimate(
            flops=0, bytes_accessed=moved * 10, transcendentals=0
        ),
        name=f"exchange_{number}",
    )(*(array for _, array in ops))


def pack(parts, lead, unit):
    flat = jnp.concatenate([part.reshape(lead, -1) for part in parts], axis=1)
    wide = -(-flat.shape[1] // unit) * unit
    return jnp.pad(flat, ((0, 0), (0, wide - flat.shape[1]))).reshape(lead, wide // 128, 128)


def unpack(packed, shapes):
    flat = packed.reshape(packed.shape[0], -1)
    out, at = [], 0
    for shape in shapes:
        size = math.prod(shape)
        out.append(flat[:, at : at + size].reshape((packed.shape[0],) + shape))
        at += size
    return out


def on_device(
    sizes,
    tokens,
    seq_lengths,
    qkv_weight,
    out_weight,
    up_weight,
    down_weight,
    head_bias,
    hidden_bias,
    norm_gains,
    out_biases,
    cotangent,
):
    n_outer, n_core, n_ctx, n_tensor = sizes
    n_dp = n_outer * n_core
    shards = n_dp * n_ctx
    seq_count, local_len, width = tokens.shape
    row_count = seq_count * local_len
    total_len = n_ctx * local_len
    local_width = qkv_weight.shape[2]
    feature_rows = width // n_dp
    token_rows = tokens.reshape(row_count, width)

    def feature_slices(rows):
        return rows.reshape(row_count, n_dp, feature_rows).transpose(1, 0, 2)

    smalls = (head_bias, hidden_bias, norm_gains, out_biases)
    qkv_got, out_got, small_got, token_slices = exchange(
        sizes,
        1,
        [
            ("wg", qkv_weight.reshape(qkv_weight.shape[0], 3 * local_width)),
            ("wg", out_weight),
            ("wg", pack(smalls, 1, 2048)[0]),
            ("dp", feature_slices(token_rows)),
        ],
    )
    qkv_full = qkv_got.reshape(width, 3 * local_width)
    out_full = out_got.reshape(width, -1)
    up_full = lax.all_gather(up_weight, ("dp", "ctx"), axis=0, tiled=True)
    down_full = lax.all_gather(down_weight, ("dp", "ctx"), axis=0, tiled=True)
    head_full, hidden_full, gains_full, biases_full = (
        part.transpose(1, 0, 2).reshape(part.shape[1], -1)
        for part in unpack(small_got, [small.shape for small in smalls])
    )
    local_heads = head_full.shape[0]
    head_size = head_full.shape[1] // 2
    heads_here = local_heads // n_ctx
    group_width = heads_here * head_size
    bias_query = head_full[:, :head_size].reshape(local_width).astype(jnp.float32)
    bias_value = head_full[:, head_size:].reshape(local_width).astype(jnp.float32)
    bias_hidden = hidden_full.reshape(-1).astype(jnp.float32)
    gains_wide = gains_full.astype(jnp.float32)
    biases_wide = biases_full.astype(jnp.float32)

    def to_positions(chunks, parts):
        return (
            chunks.reshape(n_ctx, parts, seq_count, local_len, group_width)
            .transpose(1, 2, 0, 3, 4)
            .reshape(parts, seq_count, total_len, heads_here, head_size)
        )

    def by_position(parts):
        return (
            jnp.stack(parts)
            .reshape(len(parts), seq_count, n_ctx, local_len, group_width)
            .transpose(2, 0, 1, 3, 4)
            .reshape(n_ctx, len(parts), row_count, group_width)
        )

    def by_heads(rows, parts):
        return rows.reshape(row_count, parts, n_ctx, group_width).transpose(2, 1, 0, 3)

    def to_rows(chunks, parts):
        return (
            chunks.reshape(n_ctx, parts, row_count, group_width)
            .transpose(2, 1, 0, 3)
            .reshape(row_count, parts * local_width)
        )

    projected = jnp.dot(token_rows, qkv_full, preferred_element_type=jnp.float32)
    shift = jnp.concatenate([bias_query, jnp.zeros_like(bias_query), bias_value])
    projected = (projected + shift).astype(jnp.bfloat16)
    (qkv_chunks,) = exchange(sizes, 2, [("ctx", by_heads(projected, 3))])
    queries, key_rows, value_rows = to_positions(qkv_chunks, 3)
    valid = jnp.arange(total_len)[None, :] < seq_lengths[:, None]
    mixed, log_total = lax.map(attend_forward, (queries, key_rows, value_rows, valid))
    (mixed_chunks,) = exchange(sizes, 3, [("ctx", by_position([mixed]))])
    attn_flat = to_rows(mixed_chunks, 1)
    attn_part = contract_last(attn_flat, out_full)
    attn_other, attn_all = exchange(sizes, 4, [("swap", attn_part), ("dpg", attn_flat)])
    attn_proj = attn_part + jnp.sum(attn_other, axis=0)
    first_sum = token_rows.astype(jnp.float32) + attn_proj + biases_wide[0]
    normed_one, z_one, rstd_one = layer_norm(first_sum, gains_wide[0], biases_wide[1])
    normed_low = normed_one.astype(jnp.bfloat16)
    pre_act = jnp.dot(normed_low, up_full, preferred_element_type=jnp.float32) + bias_hidden
    activated, slope = gelu_parts(pre_act)
    hidden_low = activated.astype(jnp.bfloat16)
    mlp_part = contract_last(hidden_low, down_full)
    half = n_dp // 2
    mlp_other, hidden_all, token_low = exchange(
        sizes,
        5,
        [("swap", mlp_part), ("dpg", hidden_low), ("cg", token_slices[:half])],
    )
    mlp_out = mlp_part + jnp.sum(mlp_other, axis=0)
    second_sum = normed_one + mlp_out + biases_wide[2]
    result, z_two, rstd_two = layer_norm(second_sum, gains_wide[1], biases_wide[3])
    output = result.astype(jnp.bfloat16).reshape(seq_count, local_len, width)
    grad_out = cotangent.reshape(row_count, width).astype(jnp.float32)
    grad_two, gain_two_grad, shift_two_grad = norm_back(grad_out, z_two, rstd_two, gains_wide[1])
    grad_two_low = grad_two.astype(jnp.bfloat16)
    grad_hidden = jnp.dot(grad_two_low, down_full, preferred_element_type=jnp.float32)
    grad_pre = grad_hidden * slope
    grad_pre_low = grad_pre.astype(jnp.bfloat16)
    hidden_part = jnp.sum(grad_pre, axis=0).reshape(hidden_full.shape)
    normed_part = contract_last(grad_pre_low, up_full)
    normed_other, grad_pre_all, grad_two_slices, token_high = exchange(
        sizes,
        6,
        [
            ("swap", normed_part),
            ("dpg", grad_pre_low),
            ("dp", feature_slices(grad_two_low)),
            ("cg", token_slices[half:]),
        ],
    )

    def over_rows(slices, wide):
        return contract_first(
            slices.reshape(n_dp * row_count, feature_rows), wide.reshape(n_dp * row_count, -1)
        )

    down_grad = lax.psum_scatter(
        over_rows(grad_two_slices, hidden_all), "ctx", scatter_dimension=0, tiled=True
    )
    grad_normed = normed_part + jnp.sum(normed_other, axis=0) + grad_two
    grad_one, gain_one_grad, shift_one_grad = norm_back(grad_normed, z_one, rstd_one, gains_wide[0])
    grad_one_low = grad_one.astype(jnp.bfloat16)
    grad_attn = jnp.dot(grad_one_low, out_full, preferred_element_type=jnp.float32).astype(
        jnp.bfloat16
    )
    grad_chunks, grad_one_slices, normed_slices = exchange(
        sizes,
        7,
        [
            ("ctx", by_heads(grad_attn, 1)),
            ("dp", feature_slices(grad_one_low)),
            ("dp", feature_slices(normed_low)),
        ],
    )
    up_grad = lax.psum_scatter(
        over_rows(normed_slices, grad_pre_all), "ctx", scatter_dimension=0, tiled=True
    )
    grad_mixed = to_positions(grad_chunks, 1)[0]
    out_grad = over_rows(grad_one_slices, attn_all)
    grad_queries, grad_keys, grad_values = lax.map(
        attend_backward, (queries, key_rows, value_rows, valid, mixed, log_total, grad_mixed)
    )
    proj_parts = by_position(
        [part.astype(jnp.bfloat16) for part in (grad_queries, grad_keys, grad_values)]
    )
    proj_wide = proj_parts.transpose(0, 2, 1, 3).reshape(n_ctx * row_count, 3 * group_width)
    proj_chunks, proj_all = exchange(sizes, 8, [("ctx", proj_parts), ("dpg", proj_wide)])
    token_all = (
        jnp.concatenate([token_low, token_high], axis=1)
        .transpose(1, 0, 2, 3)
        .reshape(n_dp * n_ctx * row_count, feature_rows)
    )
    qkv_part = contract_first(token_all, proj_all.reshape(n_dp * n_ctx * row_count, -1))
    grad_proj = to_rows(proj_chunks, 3)
    input_part = contract_last(grad_proj, qkv_full)
    head_rows = jnp.concatenate(
        [jnp.sum(grad_queries, axis=(0, 1)), jnp.sum(grad_values, axis=(0, 1))], axis=1
    )
    head_part = lax.dynamic_update_slice(
        jnp.zeros((local_heads, 2 * head_size), jnp.float32),
        head_rows,
        (lax.axis_index("ctx") * heads_here, 0),
    )
    gains_part = jnp.stack([gain_one_grad, gain_two_grad])
    biases_part = jnp.stack(
        [jnp.sum(grad_one, axis=0), shift_one_grad, jnp.sum(grad_two, axis=0), shift_two_grad]
    )
    small_parts = [
        part.reshape(part.shape[0], shards, -1).transpose(1, 0, 2)
        for part in (head_part, hidden_part, gains_part, biases_part)
    ]
    input_other, small_sums, out_blocks, qkv_blocks = exchange(
        sizes,
        9,
        [
            ("swap", input_part),
            ("all", pack(small_parts, shards, 1024)),
            ("ctx", out_grad.reshape(n_ctx, feature_rows // n_ctx, -1)),
            ("ctx", qkv_part.reshape(n_ctx, feature_rows // n_ctx, -1)),
        ],
    )
    input_grad = (input_part + jnp.sum(input_other, axis=0) + grad_one).reshape(
        seq_count, local_len, width
    )
    qkv_grad = (
        qkv_blocks.reshape(n_ctx, -1, 3, group_width)
        .transpose(1, 2, 0, 3)
        .reshape(-1, 3, local_width)
    )
    small_grads = unpack(
        jnp.sum(small_sums, axis=0)[None], [part.shape[1:] for part in small_parts]
    )
    return (
        output,
        input_grad,
        qkv_grad,
        jnp.sum(out_blocks, axis=0),
        up_grad,
        down_grad,
        *(part[0] for part in small_grads),
    )


MESH = pl.DeviceIdType.MESH


def dot_nn(left, right):
    return jnp.dot(left, right, preferred_element_type=jnp.float32)


class Links:
    def __init__(self, send_sem, recv_sem, own_sem, partner):
        self.send_sem, self.recv_sem, self.own_sem = send_sem, recv_sem, own_sem
        self.partner, self.sent, self.used, self.kept = partner, {}, 0, 0
        self.at_close = []

    def reserve(self):
        self.used += 1
        return self.used - 1

    def copy(self, number, source, target, to, got=None):
        return pltpu.make_async_remote_copy(
            src_ref=source,
            dst_ref=target,
            send_sem=self.send_sem.at[number],
            recv_sem=self.recv_sem.at[number if got is None else got],
            device_id=to,
            device_id_type=MESH,
        )

    def put(self, source, target, to):
        number = self.reserve()
        copy = self.copy(number, source, target, to)
        copy.start()
        self.sent[number] = copy
        return number

    def put_if(self, condition, number, ends, got=None):
        @pl.when(condition)
        def _():
            self.copy(number, *ends(), got).start()

        self.at_close.append((condition, number, ends))

    def arrive(self, number, target):
        self.copy(number, target, target, self.partner).wait_recv()

    def keep(self, source, target):
        copy = pltpu.make_async_copy(source, target, self.own_sem.at[self.kept])
        self.kept += 1
        copy.start()
        return copy

    def sent_all(self, number):
        self.sent.pop(number).wait_send()

    def close(self):
        for copy in self.sent.values():
            copy.wait_send()
        for condition, number, ends in self.at_close:

            @pl.when(condition)
            def _():
                self.copy(number, *ends()).wait_send()


class RowGather:
    def __init__(self, net, at, source, slot, block):
        self.net, self.at, self.source, self.slot, self.block = net, at, source, slot, block

    def start(self):
        net, at = self.net, self.at
        mine = self.slot(at.dp, at.z)
        self.own = net.keep(self.source, mine)
        self.along = [net.put(self.source, mine, at.z_to(k)) for k in range(1, at.nz)]
        self.across = [(net.put(self.source, mine, at.x_to), at.z)]

    def cross(self):
        net, at = self.net, self.at
        for k in range(1, at.nz):
            origin = at.z_from(k)
            got = self.slot(at.dp, origin)
            net.arrive(self.along[k - 1], got)
            self.across.append((net.put(got, got, at.x_to), origin))
        self.own.wait()
        block = self.block(at.dp)
        self.near = net.put(block, block, at.c_to)

    def relay(self):
        net, at = self.net, self.at
        for number, origin in self.across:
            net.arrive(number, self.slot(at.x_dp, origin))
        block = self.block(at.x_dp)
        self.far = net.put(block, block, at.c_to)

    def finish(self):
        self.net.arrive(self.near, self.block(self.at.c_dp))
        self.net.arrive(self.far, self.block(self.at.xc_dp))


class LineGather(RowGather):
    def start(self):
        net, at = self.net, self.at
        mine = self.slot(at.dp, at.z)
        self.own = net.keep(self.source, mine)
        self.across = [(net.put(self.source, mine, at.x_to), at.z)]
        self.numbers = [
            [[net.reserve() for _ in range(2)] for _ in range(at.nz)] for _ in range(2)
        ]
        for way in range(2):
            net.put_if(
                self.ahead(way),
                self.numbers[way][1][0],
                lambda way=way: (self.source, self.slot(at.dp, at.z), at.next_to(way)),
            )

    def ahead(self, way):
        return self.at.z < self.at.nz - 1 if way == 0 else self.at.z > 0

    def behind(self, way, hop):
        return self.at.z >= hop if way == 0 else self.at.z + hop < self.at.nz

    def got(self, way, hop, dp):
        return self.slot(dp, (self.at.z + (-hop if way == 0 else hop) + self.at.nz) % self.at.nz)

    def hop(self, hop):
        net, at = self.net, self.at
        for way in range(2):
            along, across = self.numbers[way][hop]

            def ends(to, way=way):
                got = self.got(way, hop, at.dp)
                return got, got, to

            @pl.when(self.behind(way, hop))
            def _():
                net.arrive(along, self.got(way, hop, at.dp))

            if hop < at.nz - 1:
                net.put_if(
                    jnp.logical_and(self.behind(way, hop), self.ahead(way)),
                    self.numbers[way][hop + 1][0],
                    lambda ends=ends, way=way: ends(at.next_to(way)),
                )
            net.put_if(self.behind(way, hop), across, lambda ends=ends: ends(at.x_to))
        if hop == at.nz - 1:
            self.own.wait()
            block = self.block(at.dp)
            self.near = net.put(block, block, at.c_to)

    def relay(self):
        net, at = self.net, self.at
        for hop in range(1, at.nz):
            for way in range(2):

                @pl.when(self.behind(way, hop))
                def _():
                    net.arrive(self.numbers[way][hop][1], self.got(way, hop, at.x_dp))

        super().relay()


class Place:
    def __init__(self, nz):
        self.nz = nz
        self.dp, self.z, self.y = (lax.axis_index(name) for name in ("dp", "ctx", "tensor"))
        dp, z, y = self.dp, self.z, self.y
        self.x, self.c = dp // 2, dp % 2
        self.c_dp = self.x * 2 + 1 - self.c
        self.x_dp = (1 - self.x) * 2 + self.c
        self.xc_dp = (1 - self.x) * 2 + 1 - self.c
        self.x_to = {"dp": self.x_dp, "ctx": z, "tensor": y}
        self.c_to = {"dp": self.c_dp, "ctx": z, "tensor": y}
        self.xc_to = {"dp": self.xc_dp, "ctx": z, "tensor": y}
        self.y_to = {"dp": dp, "ctx": z, "tensor": 1 - y}

        self.is_end = jnp.logical_or(z == 0, z == nz - 1)

    def seen(self, k):
        return jnp.where(self.z < self.nz // 2, k, self.nz - 1 - k)

    def along_to(self, z):
        return {"dp": self.dp, "ctx": z, "tensor": self.y}

    def z_at(self, k):
        return (self.z + k) % self.nz

    def z_from(self, k):
        return (self.z + self.nz - k) % self.nz

    def z_to(self, k):
        return {"dp": self.dp, "ctx": self.z_at(k), "tensor": self.y}

    def next_to(self, way):
        return self.z_to(1 if way == 0 else self.nz - 1)

    def zy_to(self, k):
        return {"dp": self.dp, "ctx": self.z_at(k), "tensor": 1 - self.y}

    def greet(self):
        peers = [self.x_to, self.c_to, self.xc_to, self.y_to]
        for k in range(1, self.nz):
            peers += [self.z_to(k), self.zy_to(k)]
        barrier = pltpu.get_barrier_semaphore()
        for peer in peers:
            pl.semaphore_signal(barrier, inc=1, device_id=peer, device_id_type=MESH)
        pl.semaphore_wait(barrier, len(peers))


def rows_at(index, size):
    return pl.ds(pl.multiple_of(index * size, size), size)


def row_sum(value):
    return jnp.sum(value, axis=0, keepdims=True)


def norm_back_rows(grad_out, normed, inv_std, gain):
    grad_normed = grad_out * gain
    first_mean = jnp.mean(grad_normed, axis=-1, keepdims=True)
    second_mean = jnp.mean(grad_normed * normed, axis=-1, keepdims=True)
    return inv_std * (grad_normed - first_mean - normed * second_mean)


def last_by_tiles(target, lefts, rights, tile=512):
    count = target.shape[1]
    tile = min(tile, count)

    def step(number, carry):
        columns = rows_at(number, tile)
        value = contract_last(lefts[0](), rights[0](columns))
        for left, right in zip(lefts[1:], rights[1:]):
            value += contract_last(left(), right(columns))
        target[:, columns] = value
        return carry

    lax.fori_loop(0, count // tile, step, 0)


class ColumnGrad:
    def __init__(self, net, at, turned, turned_all, wide, wide_all, total, got, out):
        self.net, self.at = net, at
        self.turned, self.turned_all = turned, turned_all
        self.wide, self.wide_all = wide, wide_all
        self.total, self.got, self.out = total, got, out
        self.half = wide_all.shape[2]
        self.block = turned_all.shape[0]
        self.rows = turned.shape[1]
        self.depth = got.shape[2]

    def send_wide(self):
        net, at = self.net, self.at
        mine = self.wide.at[:, rows_at(at.c, self.half)]
        theirs = self.wide.at[:, rows_at(1 - at.c, self.half)]
        slot = self.wide_all.at[at.dp]
        self.waits_wide = [
            (net.put(mine, slot, at.x_to), at.x_dp),
            (net.put(theirs, slot, at.xc_to), at.xc_dp),
            (net.put(theirs, slot, at.c_to), at.c_dp),
        ]
        self.own_wide = net.keep(mine, slot)

    def turned_of(self, dp):
        return self.turned_all.at[:, rows_at(dp, self.rows)]

    def send_turned(self):
        net, at = self.net, self.at
        mine = self.turned.at[rows_at(at.x, self.block)]
        theirs = self.turned.at[rows_at(1 - at.x, self.block)]
        slot = self.turned_of(at.dp)
        self.turned_x = net.put(theirs, slot, at.x_to)
        self.turned_c = net.put(mine, slot, at.c_to)
        self.own_turned = net.keep(mine, slot)

    def hand_on(self):
        net, at = self.net, self.at
        got = self.turned_of(at.x_dp)
        net.arrive(self.turned_x, got)
        self.turned_xc = net.put(got, got, at.c_to)

    def multiply(self):
        net, at = self.net, self.at
        self.own_wide.wait()
        self.own_turned.wait()
        for number, dp in self.waits_wide:
            net.arrive(number, self.wide_all.at[dp])
        net.arrive(self.turned_c, self.turned_of(at.c_dp))
        net.arrive(self.turned_xc, self.turned_of(at.xc_dp))
        tile = min(256, self.half)
        n_dp = self.wide_all.shape[0]
        middle = self.block // 2

        def step(number, carry):
            columns = rows_at(number, tile)
            value = dot_nn(self.turned_all[:, : self.rows], self.wide_all[0, :, columns])
            for dp in range(1, n_dp):
                value += dot_nn(
                    self.turned_all[:, dp * self.rows : (dp + 1) * self.rows],
                    self.wide_all[dp, :, columns],
                )
            self.total[0, :, columns] = value[:middle]
            self.total[1, :, columns] = value[middle:]
            return carry

        lax.fori_loop(0, self.half // tile, step, 0)

    def chunk(self, z):
        return self.total.at[:, rows_at(z, self.depth)]

    def spread(self):
        net, at = self.net, self.at
        self.numbers = [net.reserve() for _ in range(5)]
        far_end, far_mid, plain, _, _ = self.numbers
        for slot, (number, to) in enumerate(((far_end, 3), (far_mid, 2))):
            net.put_if(
                at.is_end,
                number,
                lambda slot=slot, to=to: (self.chunk(at.seen(to)), self.got.at[slot], at.along_to(at.seen(1))),
            )
        net.put_if(
            at.is_end, plain, lambda: (self.chunk(at.seen(1)), self.got.at[2], at.along_to(at.seen(1)))
        )
        net.put_if(
            jnp.logical_not(at.is_end),
            plain,
            lambda: (self.chunk(at.seen(0)), self.got.at[2], at.along_to(at.seen(0))),
        )

    def pass_on(self, slot):
        net, at = self.net, self.at
        to = 3 - slot
        middle = jnp.logical_not(at.is_end)

        @pl.when(middle)
        def _():
            net.arrive(self.numbers[slot], self.got.at[slot])
            for core in range(2):
                self.got[slot, core] += self.total[core, rows_at(at.seen(to), self.depth), :]

        net.put_if(
            middle,
            self.numbers[3 + slot],
            lambda: (self.got.at[slot], self.got.at[3], at.along_to(at.seen(to))),
            self.numbers[3],
        )

    def swap_cores(self):
        net, at = self.net, self.at
        net.arrive(self.numbers[2], self.got.at[2])
        net.arrive(self.numbers[3], self.got.at[3])

        def added(core):
            return (
                self.total[core, rows_at(at.z, self.depth), :] + self.got[2, core] + self.got[3, core]
            )

        place = rows_at(at.c, self.half)
        self.got[2, 1 - at.c] = added(1 - at.c)
        self.last = net.put(self.got.at[2, 1 - at.c], self.out.at[:, place], at.c_to)
        self.out[:, place] = added(at.c)

    def finish(self):
        self.net.arrive(self.last, self.out.at[:, rows_at(1 - self.at.c, self.half)])


def layer_kernel(dims, names, *refs):
    (nz, head_size, small_rows) = dims
    r = dict(zip(names, refs))

    class Refs:
        pass

    m = Refs()
    m.__dict__.update(r)
    at = Place(nz)
    net = Links(m.send_sem, m.recv_sem, m.own_sem, at.c_to)
    rows, width = m.tok.shape
    half = rows // 2
    total_len = rows * nz
    group = m.queries.shape[1]
    heads = group // head_size
    shard = m.outw.shape[0]
    part_rows = nz * shard
    local_width = m.outw.shape[1]
    hidden = m.upw.shape[1]
    groups_wide = width // 128
    bf16, f32 = jnp.bfloat16, jnp.float32
    mine, other = rows_at(at.y, half), rows_at(1 - at.y, half)
    at.greet()

    def gather(source, full, form=RowGather):
        return form(
            net,
            at,
            source,
            lambda dp, z: full.at[rows_at(dp * nz + z, source.shape[0])],
            lambda dp: full.at[rows_at(dp, nz * source.shape[0])],
        )

    def qkv_slot(g, dp, z):
        return m.wfull.at[g, rows_at(dp * nz + z, shard)]

    def qkv_block(g, dp):
        return m.wfull.at[g, rows_at(dp, part_rows)]

    own_qkv = net.keep(m.wq.at[at.z], qkv_slot(at.z, at.dp, at.z))
    qkv_along = [
        net.put(m.wq.at[at.z_at(k)], qkv_slot(at.z_at(k), at.dp, at.z), at.z_to(k))
        for k in range(1, nz)
    ]
    qkv_across = [(net.put(m.wq.at[at.z], qkv_slot(at.z, at.dp, at.z), at.x_to), at.z)]
    small = gather(m.small, m.small_all)
    small.start()
    own_rows = net.keep(m.tok, m.xall.at[rows_at(at.z, rows)])

    def half_of(z, y):
        return m.xall.at[rows_at(z * 2 + y, half)]

    token_along = [
        net.put(m.tok.at[mine], half_of(at.z, at.y), at.z_to(k)) for k in range(1, nz)
    ]
    for k in range(1, nz):
        origin = at.z_from(k)
        got = qkv_slot(at.z, at.dp, origin)
        net.arrive(qkv_along[k - 1], got)
        qkv_across.append((net.put(got, got, at.x_to), origin))
    own_qkv.wait()
    near = qkv_block(at.z, at.dp)
    qkv_near = net.put(near, near, at.c_to)
    small.cross()
    token_y = []
    for k in range(1, nz):
        origin = at.z_from(k)
        got = half_of(origin, at.y)
        net.arrive(token_along[k - 1], got)
        token_y.append((net.put(got, got, at.y_to), origin))
    outs = gather(m.outw, m.outf.at[at.y])
    outs.start()
    ups = gather(m.upw, m.up, LineGather)
    ups.start()
    for number, origin in qkv_across:
        net.arrive(number, qkv_slot(at.z, at.x_dp, origin))
    far = qkv_block(at.z, at.x_dp)
    qkv_far = net.put(far, far, at.c_to)
    small.relay()
    small.finish()
    small_sum = m.small_all[:small_rows, :].astype(f32)
    for slot in range(1, 4 * nz):
        small_sum += m.small_all[slot * small_rows : (slot + 1) * small_rows, :].astype(f32)
    m.smalls[...] = small_sum
    for row in range(6):
        for j in range(groups_wide):
            at_row = row * groups_wide + j
            m.norms[row : row + 1, j * 128 : (j + 1) * 128] = m.smalls[at_row : at_row + 1, :]
    query_row = 6 * groups_wide
    value_row = query_row + nz
    hidden_row = value_row + nz
    for j in range(hidden // 128):
        m.hbias[:, j * 128 : (j + 1) * 128] = m.smalls[hidden_row + j : hidden_row + j + 1, :]
    net.arrive(qkv_near, qkv_block(at.z, at.c_dp))
    net.arrive(qkv_far, qkv_block(at.z, at.xc_dp))
    downs = gather(m.downw, m.down, LineGather)
    own_rows.wait()
    for number, origin in token_y:
        net.arrive(number, half_of(origin, 1 - at.y))
    bias_q = m.smalls[pl.ds(query_row + at.z, 1), :]
    bias_v = m.smalls[pl.ds(value_row + at.z, 1), :]

    def project(block, carry):
        place = rows_at(block, rows)
        value = dot_nn(m.xall[place, :], m.wfull[at.z])
        m.queries[place, :] = (value[:, :group] + bias_q).astype(bf16)
        key = value[:, group : 2 * group]
        m.keys[place, :] = key.astype(bf16)
        m.keys_t[:, place] = key.T.astype(bf16)
        val = value[:, 2 * group :] + bias_v
        m.values[place, :] = val.astype(bf16)
        m.values_t[:, place] = val.T.astype(bf16)
        return carry

    lax.fori_loop(0, nz, project, 0)
    outs.cross()
    y_rows = width // 2

    valid = lax.broadcasted_iota(jnp.int32, (total_len, 1), 0) < m.lens[0]
    lane_head = lax.broadcasted_iota(jnp.int32, (1, group), 1) // head_size
    row_head = lax.broadcasted_iota(jnp.int32, (group, 1), 0) // head_size

    def head_of(value, h):
        return jnp.where(lane_head == h, value, jnp.zeros_like(value))

    def scores_of(query):
        return jnp.where(valid, contract_last(m.keys[...], query) * SCALE, NEG_BIG)

    def attend(block):
        place = rows_at(block, rows)
        query = m.queries[place, :]
        mixed = jnp.zeros((group, rows), f32)
        for h in range(heads):
            score = scores_of(head_of(query, h))
            peak = jnp.max(score, axis=0, keepdims=True)
            grown = jnp.exp(score - peak)
            total = jnp.sum(grown, axis=0, keepdims=True)
            m.log_total[h : h + 1, place] = peak + jnp.log(total)
            probs = (grown * (1.0 / total)).astype(bf16)
            mixed = jnp.where(row_head == h, dot_nn(m.values_t[...], probs), mixed)
        m.mixed[place, :] = mixed.T.astype(bf16)

    def columns_of(y, z):
        return m.attn.at[:, rows_at(y * nz + z, group)]

    mixed_along = []
    for k in list(range(1, nz)) + [0]:
        attend(at.z_at(k))
        part = m.mixed.at[rows_at(at.z_at(k), rows)]
        if k:
            mixed_along.append(net.put(part, columns_of(at.y, at.z), at.z_to(k)))
            if k == 2:
                ups.hop(1)
        else:
            own_mixed = net.keep(part, columns_of(at.y, at.z))
            mixed_y = [(net.put(part, columns_of(at.y, at.z), at.y_to), at.z)]
    ups.hop(2)
    downs.start()
    outs.relay()
    for k in range(1, nz):
        origin = at.z_from(k)
        got = columns_of(at.y, origin)
        net.arrive(mixed_along[k - 1], got)
        mixed_y.append((net.put(got, got, at.y_to), origin))
    outs.finish()
    out_half = m.outf.at[at.y, rows_at(at.c, y_rows)]
    out_y = net.put(out_half, out_half, at.y_to)
    ups.hop(3)

    def turn_rows(block, carry):
        place = rows_at(block, rows)
        m.xall_t[:, place] = m.xall[place, :].T
        return carry

    lax.fori_loop(0, nz, turn_rows, 0)
    downs.hop(1)
    got = m.outf.at[1 - at.y, rows_at(at.c, y_rows)]
    net.arrive(out_y, got)
    out_near = net.put(got, got, at.c_to)
    net.arrive(out_near, m.outf.at[1 - at.y, rows_at(1 - at.c, y_rows)])
    own_mixed.wait()
    for number, origin in mixed_y:
        net.arrive(number, columns_of(1 - at.y, origin))

    gain_one, gain_two = m.norms[0:1, :], m.norms[1:2, :]
    shift = [m.norms[2 + i : 3 + i, :] for i in range(4)]

    def first_norm(place, kept):
        first_sum = (
            m.tok[place, :].astype(f32)
            + contract_last(m.attn[place, :local_width], m.outf[0])
            + contract_last(m.attn[place, local_width:], m.outf[1])
            + shift[0]
        )
        normed, z_one, rstd = layer_norm(first_sum, gain_one, shift[1])
        if kept:
            m.normed[...] = normed
            m.z_one[...] = z_one
            m.rstd[...] = rstd
        m.normed_low[place, :] = normed.astype(bf16)
        m.normed_t[:, place] = normed.T.astype(bf16)

    first_norm(other, False)
    first_norm(mine, True)
    ups.relay()
    downs.hop(2)
    ups.finish()

    tile = min(512, hidden)

    def feed(place):
        def step(number, carry):
            columns = rows_at(number, tile)
            pre = dot_nn(m.normed_low[place, :], m.up[:, columns]) + m.hbias[:, columns]
            activated, slope = gelu_parts(pre)
            m.hid[place, columns] = activated.astype(bf16)
            m.slope[place, columns] = slope
            return carry

        lax.fori_loop(0, hidden // tile, step, 0)

    feed(other)
    downs.hop(3)
    feed(mine)
    downs.relay()
    down_grad = ColumnGrad(
        net, at, m.grad_two_t, m.grad_two_all, m.hid, m.hid_all, m.down_total, m.down_got, m.down_grad
    )
    up_grad = ColumnGrad(
        net, at, m.normed_t, m.normed_all, m.grad_pre, m.grad_pre_all, m.up_total, m.up_got, m.up_grad
    )
    out_grad = ColumnGrad(
        net,
        at,
        m.grad_one_t,
        m.grad_one_all,
        m.attn.at[:, rows_at(at.y, local_width)],
        m.attn_all,
        m.out_total,
        m.out_got,

        m.out_grad,
    )
    down_grad.send_wide()
    downs.finish()
    late = []
    for k in range(1, nz):
        for j in range(1, nz):
            g = at.z_at(k + j)
            target = qkv_slot(g, at.dp, at.z)
            late.append((net.put(m.wq.at[g], target, at.z_to(k)), k, j))
    late_own = [
        net.keep(m.wq.at[at.z_at(j)], qkv_slot(at.z_at(j), at.dp, at.z)) for j in range(1, nz)
    ]
    last_by_tiles(m.part_a, [lambda: m.hid[other, :]], [lambda at_rows: m.down[at_rows, :]])
    part_a = net.put(m.part_a, m.got_a, at.y_to)
    last_by_tiles(m.kept, [lambda: m.hid[mine, :]], [lambda at_rows: m.down[at_rows, :]])
    net.arrive(part_a, m.got_a)
    second_sum = m.normed[...] + (m.kept[...] + m.got_a[...]) + shift[2]
    result, z_two, rstd_two = layer_norm(second_sum, gain_two, shift[3])
    grad_out = m.cot[mine, :].astype(f32)
    grad_two = norm_back_rows(grad_out, z_two, rstd_two, gain_two)
    m.grad_two[...] = grad_two
    m.grad_two_low[mine, :] = grad_two.astype(bf16)
    two_y = net.put(m.grad_two_low.at[mine], m.grad_two_low.at[mine], at.y_to)
    m.output[mine, :] = result.astype(bf16)
    sums = {1: row_sum(grad_out * z_two), 5: row_sum(grad_out), 4: row_sum(grad_two)}

    m.hidden_sum[...] = jnp.zeros_like(m.hidden_sum)

    def feed_back(place):
        def step(number, carry):
            columns = rows_at(number, tile)
            grad_hidden = dot_nn(m.grad_two_low[place, :], m.down[:, columns])
            grad_pre = grad_hidden * m.slope[place, columns]
            m.grad_pre[place, columns] = grad_pre.astype(bf16)
            m.hidden_sum[:, columns] += row_sum(grad_pre)
            return carry

        lax.fori_loop(0, hidden // tile, step, 0)

    feed_back(mine)
    net.arrive(two_y, m.grad_two_low.at[other])
    m.grad_two_t[...] = m.grad_two_low[...].T
    down_grad.send_turned()
    feed_back(other)
    up_grad.send_wide()
    net.sent_all(part_a)
    last_by_tiles(m.part_a, [lambda: m.grad_pre[other, :]], [lambda at_rows: m.up[at_rows, :]])
    part_b = net.put(m.part_a, m.got_a, at.y_to)
    last_by_tiles(m.kept, [lambda: m.grad_pre[mine, :]], [lambda at_rows: m.up[at_rows, :]])
    down_grad.hand_on()
    down_grad.multiply()
    down_grad.spread()
    net.arrive(part_b, m.got_a)
    grad_normed = m.kept[...] + m.got_a[...] + m.grad_two[...]
    z_mine = m.z_one[...]
    grad_one = norm_back_rows(grad_normed, z_mine, m.rstd[...], gain_one)
    m.grad_one[...] = grad_one
    m.grad_one_low[mine, :] = grad_one.astype(bf16)
    sums[0] = row_sum(grad_normed * z_mine)
    sums[3] = row_sum(grad_normed)
    sums[2] = row_sum(grad_one)
    def back_step(y, carry):
        value = dot_nn(m.grad_one_low[mine, :], m.outf[y])
        m.grad_attn[:, rows_at(y, local_width)] = value.astype(bf16)
        return carry

    lax.fori_loop(0, 2, back_step, 0)

    def attn_part(y, z):
        return m.grad_attn.at[:, rows_at(y * nz + z, group)]

    my_slot = m.grad_mixed.at[rows_at(at.z * 2 + at.y, half)]
    grad_along = []
    for k in range(1, nz):
        grad_along.append((net.put(attn_part(at.y, at.z_at(k)), my_slot, at.z_to(k)), at.z_from(k), at.y))
        grad_along.append(
            (net.put(attn_part(1 - at.y, at.z_at(k)), my_slot, at.zy_to(k)), at.z_from(k), 1 - at.y)
        )
    grad_along.append((net.put(attn_part(1 - at.y, at.z), my_slot, at.y_to), at.z, 1 - at.y))
    own_grad = net.keep(attn_part(at.y, at.z), my_slot)
    one_y = net.put(m.grad_one_low.at[mine], m.grad_one_low.at[mine], at.y_to)
    up_grad.send_turned()
    out_grad.send_wide()

    for number, origin, y in grad_along:
        net.arrive(number, m.grad_mixed.at[rows_at(origin * 2 + y, half)])
    own_grad.wait()
    net.arrive(one_y, m.grad_one_low.at[other])
    output_y = net.put(m.output.at[mine], m.output.at[mine], at.y_to)
    m.grad_one_t[...] = m.grad_one_low[...].T
    out_grad.send_turned()
    down_grad.pass_on(0)

    m.acc_keys[...] = jnp.zeros_like(m.acc_keys)
    m.acc_values[...] = jnp.zeros_like(m.acc_values)
    ones_row = jnp.ones((8, group), f32)

    def attend_back(block, carry):
        place = rows_at(block, rows)
        query = m.queries[place, :]
        grad = m.grad_mixed[place, :]
        product = grad.astype(f32) * m.mixed[place, :].astype(f32)
        turned = product.T
        grad_query = jnp.zeros((group, rows), f32)
        grad_keys = jnp.zeros((total_len, group), f32)
        grad_values = jnp.zeros((total_len, group), f32)
        for h in range(heads):
            query_h = head_of(query, h)
            grad_h = head_of(grad, h)
            probs = jnp.exp(scores_of(query_h) - m.log_total[h : h + 1, place])
            grad_values += dot_nn(probs.astype(bf16), grad_h)
            inner = row_sum(turned[h * head_size : (h + 1) * head_size, :])
            grad_probs = contract_last(m.values[...], grad_h)
            grad_scores = (probs * (grad_probs - inner)).astype(bf16)
            grad_keys += dot_nn(grad_scores, query_h)
            grad_query = jnp.where(row_head == h, dot_nn(m.keys_t[...], grad_scores), grad_query)
        m.acc_keys[...] += grad_keys
        m.acc_values[...] += grad_values
        grad_query = grad_query.T * SCALE
        m.grad_proj[place, :group] = grad_query.astype(bf16)
        return carry + row_sum(grad_query)

    query_sum = lax.fori_loop(0, nz // 2, attend_back, jnp.zeros((1, group), f32))
    down_grad.pass_on(1)
    query_sum = lax.fori_loop(nz // 2, nz, attend_back, query_sum)
    m.grad_proj[:, group : 2 * group] = (m.acc_keys[...] * SCALE).astype(bf16)
    m.grad_proj[:, 2 * group :] = m.acc_values[...].astype(bf16)
    value_sum = row_sum(m.acc_values[...])
    proj_along = [
        net.put(m.grad_proj.at[rows_at(at.z_at(k), rows)], m.proj_rows.at[at.z], at.z_to(k))
        for k in range(1, nz)
    ]
    own_proj = net.keep(m.grad_proj.at[rows_at(at.z, rows)], m.proj_rows.at[at.z])

    m.small_sum[...] = jnp.zeros_like(m.small_sum)
    for row in range(6):
        for j in range(groups_wide):
            at_row = row * groups_wide + j
            m.small_sum[at_row : at_row + 1, :] = sums[row][:, j * 128 : (j + 1) * 128]
    m.small_sum[pl.ds(query_row + at.z, 1), :] = query_sum
    m.small_sum[pl.ds(value_row + at.z, 1), :] = value_sum
    for j in range(hidden // 128):
        m.small_sum[hidden_row + j : hidden_row + j + 1, :] = m.hidden_sum[:, j * 128 : (j + 1) * 128]
    small_along = [net.put(m.small_sum, m.small_got.at[k - 1], at.z_to(k)) for k in range(1, nz)]

    up_grad.hand_on()
    up_grad.multiply()
    up_grad.spread()
    late_x = []
    for number, k, j in late:
        got = qkv_slot(at.z_at(j), at.dp, at.z_from(k))
        net.arrive(number, got)
    for copy in late_own:
        copy.wait()
    for j in range(1, nz):
        block = qkv_block(at.z_at(j), at.dp)
        late_x.append((net.put(block, block, at.x_to), net.put(block, block, at.c_to), j))
    def qkv_step(block, carry):
        place = rows_at(block, rows)
        m.qkv_total[place, :] = dot_nn(m.xall_t[place, :], m.grad_proj[...])
        return carry

    lax.fori_loop(0, width // rows, qkv_step, 0)
    core_waits = []
    for x in range(2):
        part = m.qkv_total.at[rows_at(x * 2 + 1 - at.c, part_rows)]
        core_waits.append(net.put(part, m.qkv_core.at[x], at.c_to))
    for x in range(2):
        net.arrive(core_waits[x], m.qkv_core.at[x])
    across_rows, kept_rows = rows_at(at.x_dp, part_rows), rows_at(at.dp, part_rows)
    m.qkv_total[across_rows, :] += m.qkv_core[1 - at.x]
    qkv_x = net.put(m.qkv_total.at[across_rows], m.qkv_got, at.x_to)
    out_grad.hand_on()
    out_grad.multiply()
    out_grad.spread()
    up_grad.pass_on(0)
    for k in range(1, nz):
        net.arrive(small_along[k - 1], m.small_got.at[k - 1])
    value = m.small_sum[...]
    for k in range(1, nz):
        value += m.small_got[k - 1]
    m.small_two[...] = value
    small_x = net.put(m.small_two, m.small_got.at[nz - 1], at.x_to)
    late_c = []
    for across, near, j in late_x:
        block = qkv_block(at.z_at(j), at.x_dp)
        net.arrive(across, block)
        late_c.append((net.put(block, block, at.c_to), near, j))
    for across, near, j in late_c:
        net.arrive(near, qkv_block(at.z_at(j), at.c_dp))
        net.arrive(across, qkv_block(at.z_at(j), at.xc_dp))
    own_proj.wait()
    for k in range(1, nz):
        net.arrive(proj_along[k - 1], m.proj_rows.at[at.z_from(k)])

    def input_part(target, place):
        last_by_tiles(
            target,
            [lambda g=g: m.proj_rows[g, place, :] for g in range(nz)],
            [lambda at_rows, g=g: m.wfull[g, at_rows, :] for g in range(nz)],
        )

    net.sent_all(part_b)
    input_part(m.part_a, other)
    part_c = net.put(m.part_a, m.got_a, at.y_to)
    input_part(m.kept, mine)
    up_grad.pass_on(1)
    out_grad.pass_on(0)
    net.arrive(qkv_x, m.qkv_got)
    m.qkv_total[kept_rows, :] += m.qkv_core[at.x] + m.qkv_got[...]
    qkv_z = [
        net.put(
            m.qkv_total.at[rows_at(at.dp * nz + at.z_at(k), shard)], m.qkv_grad.at[at.z], at.z_to(k)
        )
        for k in range(1, nz)
    ]
    m.qkv_grad[at.z] = m.qkv_total[rows_at(at.dp * nz + at.z, shard), :]
    net.arrive(small_x, m.small_got.at[nz - 1])
    m.small_three[...] = m.small_two[...] + m.small_got[nz - 1]
    small_c = net.put(m.small_three, m.small_got.at[nz], at.c_to)
    net.arrive(part_c, m.got_a)
    m.input_grad[mine, :] = m.kept[...] + m.got_a[...] + m.grad_one[...]
    input_y = net.put(m.input_grad.at[mine], m.input_grad.at[mine], at.y_to)
    net.arrive(small_c, m.small_got.at[nz])
    m.small_four[...] = m.small_three[...] + m.small_got[nz]
    small_y = net.put(m.small_four, m.small_got.at[nz + 1], at.y_to)
    out_grad.pass_on(1)
    down_grad.swap_cores()
    up_grad.swap_cores()
    out_grad.swap_cores()
    net.arrive(small_y, m.small_got.at[nz + 1])
    shared = lax.broadcasted_iota(jnp.int32, (small_rows, 1), 0) < query_row
    m.small_grad[...] = m.small_four[...] + jnp.where(shared, m.small_got[nz + 1], 0.0)
    for k in range(1, nz):
        net.arrive(qkv_z[k - 1], m.qkv_grad.at[at.z_from(k)])
    net.arrive(output_y, m.output.at[other])
    net.arrive(input_y, m.input_grad.at[other])
    for item in (down_grad, up_grad, out_grad):
        item.finish()
    net.close()


def fused(
    sizes,
    tokens,
    seq_lengths,
    qkv_weight,
    out_weight,
    up_weight,
    down_weight,
    head_bias,
    hidden_bias,
    norm_gains,
    out_biases,
    cotangent,
):
    n_outer, n_core, nz, n_tensor = sizes
    n_dp = n_outer * n_core
    shards = n_dp * nz
    _, rows, width = tokens.shape
    shard, _, local_width = qkv_weight.shape
    hidden = up_weight.shape[1]
    head_size = head_bias.shape[1] * shards // 2
    group = local_width // nz
    total_len = rows * nz
    bf16, f32 = jnp.bfloat16, jnp.float32
    place = lax.axis_index("dp") * nz + lax.axis_index("ctx")

    def spread(part):
        wide = part.shape[1] * shards
        return lax.dynamic_update_slice(
            jnp.zeros((part.shape[0], wide), bf16), part, (0, place * part.shape[1])
        )

    head_wide = spread(head_bias)
    pieces = [
        spread(norm_gains),
        spread(out_biases),
        head_wide[:, :head_size],
        head_wide[:, head_size:],
        spread(hidden_bias),
    ]
    small = jnp.concatenate([piece.reshape(-1, 128) for piece in pieces], axis=0)
    used = small.shape[0]
    small_rows = -(-used // 16) * 16
    small = jnp.pad(small, ((0, small_rows - used), (0, 0)))
    wq = qkv_weight.reshape(shard, 3, nz, group).transpose(2, 0, 1, 3).reshape(nz, shard, 3 * group)
    tok = tokens.reshape(rows, width)
    cot = cotangent.reshape(rows, width)
    half = rows // 2
    ins = dict(
        lens=seq_lengths, tok=tok, cot=cot, wq=wq, outw=out_weight, upw=up_weight, downw=down_weight, small=small
    )
    outs = dict(
        output=((rows, width), bf16),
        input_grad=((rows, width), f32),
        qkv_grad=((nz, shard, 3 * group), f32),
        out_grad=((shard, local_width), f32),
        up_grad=((shard, hidden), f32),
        down_grad=((shard, hidden), f32),
        small_grad=((small_rows, 128), f32),
    )
    block = 2 * nz * shard
    part_rows = nz * shard
    scratch = dict(
        small_all=((shards * small_rows, 128), bf16),
        smalls=((small_rows, 128), f32),
        norms=((8, width), f32),
        hbias=((1, hidden), f32),
        wfull=((nz, width, 3 * group), bf16),
        xall=((total_len, width), bf16),
        xall_t=((width, total_len), bf16),
        outf=((2, width, local_width), bf16),
        up=((width, hidden), bf16),
        down=((width, hidden), bf16),
        queries=((total_len, group), bf16),
        keys=((total_len, group), bf16),
        values=((total_len, group), bf16),
        keys_t=((group, total_len), bf16),
        values_t=((group, total_len), bf16),
        mixed=((total_len, group), bf16),
        log_total=((max(8, group // head_size), total_len), f32),
        attn=((rows, width), bf16),
        normed=((half, width), f32),
        z_one=((half, width), f32),
        rstd=((half, 1), f32),
        normed_low=((rows, width), bf16),
        normed_t=((width, rows), bf16),
        hid=((rows, hidden), bf16),
        slope=((rows, hidden), f32),
        part_a=((half, width), f32),
        got_a=((half, width), f32),
        kept=((half, width), f32),
        grad_two=((half, width), f32),
        grad_two_low=((rows, width), bf16),
        grad_two_t=((width, rows), bf16),
        grad_pre=((rows, hidden), bf16),
        hidden_sum=((1, hidden), f32),
        grad_one=((half, width), f32),
        grad_one_low=((rows, width), bf16),
        grad_one_t=((width, rows), bf16),
        grad_attn=((half, width), bf16),
        grad_mixed=((total_len, group), bf16),
        acc_keys=((total_len, group), f32),
        acc_values=((total_len, group), f32),
        grad_proj=((total_len, 3 * group), bf16),
        proj_rows=((nz, rows, 3 * group), bf16),
        small_sum=((small_rows, 128), f32),
        small_two=((small_rows, 128), f32),
        small_three=((small_rows, 128), f32),
        small_four=((small_rows, 128), f32),
        small_got=((nz + 2, small_rows, 128), f32),
        qkv_total=((width, 3 * group), f32),
        qkv_core=((2, part_rows, 3 * group), f32),
        qkv_got=((part_rows, 3 * group), f32),
        hid_all=((n_dp, rows, hidden // 2), bf16),
        grad_two_all=((block, n_dp * rows), bf16),
        down_total=((2, part_rows, hidden // 2), f32),
        down_got=((4, 2, shard, hidden // 2), f32),
        grad_pre_all=((n_dp, rows, hidden // 2), bf16),
        normed_all=((block, n_dp * rows), bf16),
        up_total=((2, part_rows, hidden // 2), f32),
        up_got=((4, 2, shard, hidden // 2), f32),
        attn_all=((n_dp, rows, local_width // 2), bf16),
        grad_one_all=((block, n_dp * rows), bf16),
        out_total=((2, part_rows, local_width // 2), f32),
        out_got=((4, 2, shard, local_width // 2), f32),
    )
    names = tuple(ins) + tuple(outs) + tuple(scratch) + ("send_sem", "recv_sem", "own_sem")
    vmem = pl.BlockSpec(memory_space=pltpu.VMEM)
    copies = 256
    result = pl.pallas_call(
        functools.partial(layer_kernel, (nz, head_size, small_rows), names),
        out_shape=tuple(jax.ShapeDtypeStruct(*spec) for spec in outs.values()),
        in_specs=[pl.BlockSpec(memory_space=pltpu.SMEM)] + [vmem] * (len(ins) - 1),
        out_specs=(vmem,) * len(outs),
        scratch_shapes=[pltpu.VMEM(*spec) for spec in scratch.values()]
        + [
            pltpu.SemaphoreType.DMA((copies,)),
            pltpu.SemaphoreType.DMA((copies,)),
            pltpu.SemaphoreType.DMA((40,)),
        ],
        compiler_params=pltpu.CompilerParams(
            collective_id=1, has_side_effects=True, vmem_limit_bytes=64 * 2**20 - 2**18
        ),
        name="layer",
    )(*ins.values())
    output, input_grad, qkv_grad, out_grad, up_grad, down_grad, small_grad = result
    qkv_grad = (
        qkv_grad.reshape(nz, shard, 3, group).transpose(1, 2, 0, 3).reshape(shard, 3, local_width)
    )

    def mine(part, like):
        return lax.dynamic_slice(
            part.reshape(like.shape[0], -1), (0, place * like.shape[1]), like.shape
        )

    at, cut = 0, []
    for piece in pieces:
        count = piece.size // 128
        cut.append(small_grad[at : at + count])
        at += count
    heads = head_bias.shape[0]
    head_grad = jnp.concatenate(
        [cut[2].reshape(heads, head_size), cut[3].reshape(heads, head_size)], axis=1
    )
    return (
        output.reshape(tokens.shape),
        input_grad.reshape(tokens.shape),
        qkv_grad,
        out_grad,
        up_grad,
        down_grad,
        mine(head_grad, head_bias),
        mine(cut[4], hidden_bias),
        mine(cut[0], norm_gains),
        mine(cut[1], out_biases),
    )


def fits(sizes, mesh):
    n_outer, n_core, nz, n_tensor = sizes
    return n_outer == 2 and n_core == 2 and n_tensor == 2 and nz == 4


def solution(mesh):
    in_specs = (
        P("dp", "ctx", None),
        P("dp"),
        P(("dp", "ctx"), None, "tensor"),
        P(("dp", "ctx"), "tensor"),
        P(("dp", "ctx"), "tensor"),
        P(("dp", "ctx"), "tensor"),
        P("tensor", ("dp", "ctx")),
        P("tensor", ("dp", "ctx")),
        P(None, ("dp", "ctx")),
        P(None, ("dp", "ctx")),
        P("dp", "ctx", None),
    )
    out_specs = (
        P("dp", "ctx", None),
        P("dp", "ctx", None),
        P(("dp", "ctx"), None, "tensor"),
        P(("dp", "ctx"), "tensor"),
        P(("dp", "ctx"), "tensor"),
        P(("dp", "ctx"), "tensor"),
        P("tensor", ("dp", "ctx")),
        P("tensor", ("dp", "ctx")),
        P(None, ("dp", "ctx")),
        P(None, ("dp", "ctx")),
    )
    n_core = 2 if mesh.shape["dp"] % 2 == 0 else 1
    sizes = (mesh.shape["dp"] // n_core, n_core, mesh.shape["ctx"], mesh.shape["tensor"])
    body = fused if fits(sizes, mesh) else on_device
    return jax.shard_map(
        functools.partial(body, sizes), mesh=mesh, in_specs=in_specs, out_specs=out_specs, check_vma=False
    )
```

```python
import functools
import math

import jax
import jax.numpy as jnp
from jax import lax
from jax.experimental import pallas as pl
from jax.experimental.pallas import tpu as pltpu
from jax.sharding import PartitionSpec as P

EPSILON = 1e-05
SCALE = 0.125
NEG_BIG = -1000000000.0
INV_ROOT_TWO = 1.0 / math.sqrt(2.0)
INV_ROOT_TWO_PI = 1.0 / math.sqrt(2.0 * math.pi)


def contract_last(left, right):
    return lax.dot_general(
        left, right, (((1,), (1,)), ((), ())), preferred_element_type=jnp.float32
    )


def contract_first(left, right):
    return lax.dot_general(
        left, right, (((0,), (0,)), ((), ())), preferred_element_type=jnp.float32
    )


def layer_norm(hidden_in, gain, shift):
    centred = hidden_in - jnp.mean(hidden_in, axis=-1, keepdims=True)
    variance = jnp.mean(centred * centred, axis=-1, keepdims=True)
    inv_std = lax.rsqrt(variance + EPSILON)
    normed = centred * inv_std
    return (normed * gain + shift, normed, inv_std)


def norm_back(grad_out, normed, inv_std, gain):
    grad_normed = grad_out * gain
    first_mean = jnp.mean(grad_normed, axis=-1, keepdims=True)
    second_mean = jnp.mean(grad_normed * normed, axis=-1, keepdims=True)
    grad_in = inv_std * (grad_normed - first_mean - normed * second_mean)
    return (grad_in, jnp.sum(grad_out * normed, axis=0), jnp.sum(grad_out, axis=0))


def gelu_parts(pre_act):
    cdf_val = 0.5 * (1.0 + jax.scipy.special.erf(pre_act * INV_ROOT_TWO))
    return (
        pre_act * cdf_val,
        cdf_val + pre_act * jnp.exp(-0.5 * pre_act * pre_act) * INV_ROOT_TWO_PI,
    )


def block_scores(queries, key_rows, valid):
    scores = (
        jnp.einsum("qhd,khd->hqk", queries, key_rows, preferred_element_type=jnp.float32) * SCALE
    )
    return jnp.where(valid[None, None, :], scores, NEG_BIG)


def attend_forward(inputs):
    queries, key_rows, value_rows, valid = inputs
    scores = block_scores(queries, key_rows, valid)
    peak = jnp.max(scores, axis=-1, keepdims=True)
    log_total = peak + jnp.log(jnp.sum(jnp.exp(scores - peak), axis=-1, keepdims=True))
    probs = jnp.exp(scores - log_total).astype(jnp.bfloat16)
    mixed = jnp.einsum(
        "hqk,khd->qhd", probs, value_rows, preferred_element_type=jnp.float32
    ).astype(jnp.bfloat16)
    return (mixed, log_total)


def attend_backward(inputs):
    queries, key_rows, value_rows, valid, mixed, log_total, grad_mixed = inputs
    scores = block_scores(queries, key_rows, valid)
    probs = jnp.exp(scores - log_total)
    grad_values = jnp.einsum(
        "hqk,qhd->khd", probs.astype(jnp.bfloat16), grad_mixed, preferred_element_type=jnp.float32
    )
    grad_probs = jnp.einsum(
        "qhd,khd->hqk", grad_mixed, value_rows, preferred_element_type=jnp.float32
    )
    inner = jnp.einsum("qhd,qhd->hq", grad_mixed.astype(jnp.float32), mixed.astype(jnp.float32))
    grad_scores = (probs * (grad_probs - inner[:, :, None])).astype(jnp.bfloat16)
    grad_queries = (
        jnp.einsum("hqk,khd->qhd", grad_scores, key_rows, preferred_element_type=jnp.float32)
        * SCALE
    )
    grad_keys = (
        jnp.einsum("hqk,qhd->khd", grad_scores, queries, preferred_element_type=jnp.float32) * SCALE
    )
    return (grad_queries, grad_keys, grad_values)


def comm_kernel(sizes, kinds, copies, *refs):
    n_outer, n_core, n_ctx, n_tensor = sizes
    count = len(kinds)
    ins, outs = refs[:count], refs[count : 2 * count]
    send_sem, recv_sem, own_sem = refs[2 * count :]
    dp, ctx, tensor = (lax.axis_index(name) for name in ("dp", "ctx", "tensor"))
    outer, core = dp // n_core, dp % n_core

    def coords(offset, sign=1):
        def move(at, step, size):
            return at if step == 0 else (at + (step if sign > 0 else size - step)) % size

        outer_at = move(outer, offset[0], n_outer)
        core_at = move(core, offset[1], n_core)
        return outer_at * n_core + core_at, move(ctx, offset[2], n_ctx), move(tensor, offset[3], n_tensor)

    def device(offset):
        dp_at, ctx_at, tensor_at = coords(offset)
        return {"dp": dp_at, "ctx": ctx_at, "tensor": tensor_at}

    offsets = peer_offsets(sizes, kinds)
    barrier = pltpu.get_barrier_semaphore()
    for offset in offsets:
        pl.semaphore_signal(
            barrier, inc=1, device_id=device(offset), device_id_type=pl.DeviceIdType.MESH
        )
    pl.semaphore_wait(barrier, len(offsets))

    started, used = [], [0]

    def put(source, target, offset):
        number = used[0]
        used[0] += 1
        copy = pltpu.make_async_remote_copy(
            src_ref=source,
            dst_ref=target,
            send_sem=send_sem.at[number],
            recv_sem=recv_sem.at[number],
            device_id=device(offset),
            device_id_type=pl.DeviceIdType.MESH,
        )
        copy.start()
        started.append(copy)
        return number

    def arrived(number, target, offset):
        pltpu.make_async_remote_copy(
            src_ref=target,
            dst_ref=target,
            send_sem=send_sem.at[number],
            recv_sem=recv_sem.at[number],
            device_id=device(offset),
            device_id_type=pl.DeviceIdType.MESH,
        ).wait_recv()

    partner = (0, 1, 0, 0)
    pending, own_copies = [], []
    first = {}
    for at, kind in enumerate(kinds):
        source, target = ins[at], outs[at]
        index = functools.partial(slot_of, kind, n_ctx)
        mine = index(*coords((0, 0, 0, 0)))
        if kind == "swap":
            for offset in direct_offsets(sizes, kind):
                number = put(source, target.at[offset[3] - 1], offset)
                pending.append((number, target.at[offset[3] - 1], offset))
            continue
        if kind in ("ctx", "cg", "dp", "all"):
            for offset in direct_offsets(sizes, kind):
                block = source if kind == "cg" else source.at[index(*coords(offset))]
                number = put(block, target.at[mine], offset)
                pending.append((number, target.at[index(*coords(offset, -1))], offset))
            block = source if kind == "cg" else source.at[mine]
            own = pltpu.make_async_copy(block, target.at[mine], own_sem.at[at])
        else:
            stage = []
            if kind == "wg":
                for step in range(1, n_ctx):
                    offset = (0, 0, step, 0)
                    stage.append((put(source, target.at[mine], offset), offset))
            crossing = []
            for step in range(1, n_outer):
                offset = (step, 0, 0, 0)
                crossing.append((put(source, target.at[mine], offset), offset, (0, 0, 0, 0)))
            pending.append(
                (put(source, target.at[mine], partner), target.at[index(*coords(partner, -1))], partner)
            )
            own = pltpu.make_async_copy(source, target.at[mine], own_sem.at[at])
            first[at] = (stage, crossing)
        own.start()
        own_copies.append(own)
    for at in first:
        target = outs[at]
        index = functools.partial(slot_of, kinds[at], n_ctx)
        stage, crossing = first[at]
        for number, offset in stage:
            slot = index(*coords(offset, -1))
            arrived(number, target.at[slot], offset)
            for step in range(1, n_outer):
                across = (step, 0, 0, 0)
                crossing.append((put(target.at[slot], target.at[slot], across), across, offset))
            both = (0, 1, offset[2], 0)
            pending.append(
                (put(target.at[slot], target.at[slot], partner), target.at[index(*coords(both, -1))], partner)
            )
    for at in first:
        target = outs[at]
        index = functools.partial(slot_of, kinds[at], n_ctx)
        for number, across, offset in first[at][1]:
            origin = (across[0], 0, offset[2], 0)
            slot = index(*coords(origin, -1))
            arrived(number, target.at[slot], across)
            both = (across[0], 1, offset[2], 0)
            pending.append(
                (put(target.at[slot], target.at[slot], partner), target.at[index(*coords(both, -1))], partner)
            )
    for number, target, offset in pending:
        arrived(number, target, offset)
    for own in own_copies:
        own.wait()
    for copy in started:
        copy.wait_send()


def slot_of(kind, n_ctx, dp_at, ctx_at, tensor_at):
    if kind in ("ctx", "cg"):
        return ctx_at
    if kind in ("dp", "dpg"):
        return dp_at
    return dp_at * n_ctx + ctx_at


def direct_offsets(sizes, kind):
    n_outer, n_core, n_ctx, n_tensor = sizes
    if kind == "swap":
        return [(0, 0, 0, step) for step in range(1, n_tensor)]
    if kind in ("ctx", "cg"):
        return [(0, 0, step, 0) for step in range(1, n_ctx)]
    ctx_steps = range(n_ctx) if kind == "all" else range(1)
    return [
        (o, c, k, 0) for k in ctx_steps for o in range(n_outer) for c in range(n_core) if o + c + k
    ]


def peer_offsets(sizes, kinds):
    n_outer, n_core, n_ctx, n_tensor = sizes
    found = set()
    for kind in kinds:
        if kind in ("wg", "dpg"):
            found.update((o, 0, 0, 0) for o in range(1, n_outer))
            found.add((0, 1, 0, 0))
            if kind == "wg":
                found.update((0, 0, k, 0) for k in range(1, n_ctx))
        else:
            found.update(direct_offsets(sizes, kind))
    return sorted(found)


def exchange(sizes, number, ops):
    n_outer, n_core, n_ctx, n_tensor = sizes
    n_dp = n_outer * n_core
    kinds = tuple(kind for kind, _ in ops)
    shapes, copies, moved = [], 0, 0
    for kind, array in ops:
        if kind == "swap":
            lead, sends = (n_tensor - 1,), n_tensor - 1
        elif kind == "dpg":
            lead, sends = (n_dp,), n_dp - 1
        elif kind == "cg":
            lead, sends = (n_ctx,), n_ctx - 1
        elif kind == "wg":
            lead, sends = (n_dp * n_ctx,), n_dp * n_ctx - 1
        else:
            lead, sends = (), array.shape[0] - 1
        shapes.append(jax.ShapeDtypeStruct(lead + array.shape, array.dtype))
        copies += sends
        moved += math.prod(lead + array.shape) * array.dtype.itemsize
    vmem = pl.BlockSpec(memory_space=pltpu.VMEM)
    return pl.pallas_call(
        functools.partial(comm_kernel, sizes, kinds, copies),
        out_shape=tuple(shapes),
        in_specs=[vmem] * len(ops),
        out_specs=tuple(
            pl.BlockSpec(memory_space=pl.ANY) if kind == "wg" else vmem for kind in kinds
        ),
        scratch_shapes=[
            pltpu.SemaphoreType.DMA((copies,)),
            pltpu.SemaphoreType.DMA((copies,)),
            pltpu.SemaphoreType.DMA((len(ops),)),
        ],
        compiler_params=pltpu.CompilerParams(
            collective_id=number, has_side_effects=True, vmem_limit_bytes=60 * 2**20
        ),
        cost_estimate=pl.CostEstimate(
            flops=0, bytes_accessed=moved * 10, transcendentals=0
        ),
        name=f"exchange_{number}",
    )(*(array for _, array in ops))


def pack(parts, lead, unit):
    flat = jnp.concatenate([part.reshape(lead, -1) for part in parts], axis=1)
    wide = -(-flat.shape[1] // unit) * unit
    return jnp.pad(flat, ((0, 0), (0, wide - flat.shape[1]))).reshape(lead, wide // 128, 128)


def unpack(packed, shapes):
    flat = packed.reshape(packed.shape[0], -1)
    out, at = [], 0
    for shape in shapes:
        size = math.prod(shape)
        out.append(flat[:, at : at + size].reshape((packed.shape[0],) + shape))
        at += size
    return out


def on_device(
    sizes,
    tokens,
    seq_lengths,
    qkv_weight,
    out_weight,
    up_weight,
    down_weight,
    head_bias,
    hidden_bias,
    norm_gains,
    out_biases,
    cotangent,
):
    n_outer, n_core, n_ctx, n_tensor = sizes
    n_dp = n_outer * n_core
    shards = n_dp * n_ctx
    seq_count, local_len, width = tokens.shape
    row_count = seq_count * local_len
    total_len = n_ctx * local_len
    local_width = qkv_weight.shape[2]
    feature_rows = width // n_dp
    token_rows = tokens.reshape(row_count, width)

    def feature_slices(rows):
        return rows.reshape(row_count, n_dp, feature_rows).transpose(1, 0, 2)

    smalls = (head_bias, hidden_bias, norm_gains, out_biases)
    qkv_got, out_got, small_got, token_slices = exchange(
        sizes,
        1,
        [
            ("wg", qkv_weight.reshape(qkv_weight.shape[0], 3 * local_width)),
            ("wg", out_weight),
            ("wg", pack(smalls, 1, 2048)[0]),
            ("dp", feature_slices(token_rows)),
        ],
    )
    qkv_full = qkv_got.reshape(width, 3 * local_width)
    out_full = out_got.reshape(width, -1)
    up_full = lax.all_gather(up_weight, ("dp", "ctx"), axis=0, tiled=True)
    down_full = lax.all_gather(down_weight, ("dp", "ctx"), axis=0, tiled=True)
    head_full, hidden_full, gains_full, biases_full = (
        part.transpose(1, 0, 2).reshape(part.shape[1], -1)
        for part in unpack(small_got, [small.shape for small in smalls])
    )
    local_heads = head_full.shape[0]
    head_size = head_full.shape[1] // 2
    heads_here = local_heads // n_ctx
    group_width = heads_here * head_size
    bias_query = head_full[:, :head_size].reshape(local_width).astype(jnp.float32)
    bias_value = head_full[:, head_size:].reshape(local_width).astype(jnp.float32)
    bias_hidden = hidden_full.reshape(-1).astype(jnp.float32)
    gains_wide = gains_full.astype(jnp.float32)
    biases_wide = biases_full.astype(jnp.float32)

    def to_positions(chunks, parts):
        return (
            chunks.reshape(n_ctx, parts, seq_count, local_len, group_width)
            .transpose(1, 2, 0, 3, 4)
            .reshape(parts, seq_count, total_len, heads_here, head_size)
        )

    def by_position(parts):
        return (
            jnp.stack(parts)
            .reshape(len(parts), seq_count, n_ctx, local_len, group_width)
            .transpose(2, 0, 1, 3, 4)
            .reshape(n_ctx, len(parts), row_count, group_width)
        )

    def by_heads(rows, parts):
        return rows.reshape(row_count, parts, n_ctx, group_width).transpose(2, 1, 0, 3)

    def to_rows(chunks, parts):
        return (
            chunks.reshape(n_ctx, parts, row_count, group_width)
            .transpose(2, 1, 0, 3)
            .reshape(row_count, parts * local_width)
        )

    projected = jnp.dot(token_rows, qkv_full, preferred_element_type=jnp.float32)
    shift = jnp.concatenate([bias_query, jnp.zeros_like(bias_query), bias_value])
    projected = (projected + shift).astype(jnp.bfloat16)
    (qkv_chunks,) = exchange(sizes, 2, [("ctx", by_heads(projected, 3))])
    queries, key_rows, value_rows = to_positions(qkv_chunks, 3)
    valid = jnp.arange(total_len)[None, :] < seq_lengths[:, None]
    mixed, log_total = lax.map(attend_forward, (queries, key_rows, value_rows, valid))
    (mixed_chunks,) = exchange(sizes, 3, [("ctx", by_position([mixed]))])
    attn_flat = to_rows(mixed_chunks, 1)
    attn_part = contract_last(attn_flat, out_full)
    attn_other, attn_all = exchange(sizes, 4, [("swap", attn_part), ("dpg", attn_flat)])
    attn_proj = attn_part + jnp.sum(attn_other, axis=0)
    first_sum = token_rows.astype(jnp.float32) + attn_proj + biases_wide[0]
    normed_one, z_one, rstd_one = layer_norm(first_sum, gains_wide[0], biases_wide[1])
    normed_low = normed_one.astype(jnp.bfloat16)
    pre_act = jnp.dot(normed_low, up_full, preferred_element_type=jnp.float32) + bias_hidden
    activated, slope = gelu_parts(pre_act)
    hidden_low = activated.astype(jnp.bfloat16)
    mlp_part = contract_last(hidden_low, down_full)
    half = n_dp // 2
    mlp_other, hidden_all, token_low = exchange(
        sizes,
        5,
        [("swap", mlp_part), ("dpg", hidden_low), ("cg", token_slices[:half])],
    )
    mlp_out = mlp_part + jnp.sum(mlp_other, axis=0)
    second_sum = normed_one + mlp_out + biases_wide[2]
    result, z_two, rstd_two = layer_norm(second_sum, gains_wide[1], biases_wide[3])
    output = result.astype(jnp.bfloat16).reshape(seq_count, local_len, width)
    grad_out = cotangent.reshape(row_count, width).astype(jnp.float32)
    grad_two, gain_two_grad, shift_two_grad = norm_back(grad_out, z_two, rstd_two, gains_wide[1])
    grad_two_low = grad_two.astype(jnp.bfloat16)
    grad_hidden = jnp.dot(grad_two_low, down_full, preferred_element_type=jnp.float32)
    grad_pre = grad_hidden * slope
    grad_pre_low = grad_pre.astype(jnp.bfloat16)
    hidden_part = jnp.sum(grad_pre, axis=0).reshape(hidden_full.shape)
    normed_part = contract_last(grad_pre_low, up_full)
    normed_other, grad_pre_all, grad_two_slices, token_high = exchange(
        sizes,
        6,
        [
            ("swap", normed_part),
            ("dpg", grad_pre_low),
            ("dp", feature_slices(grad_two_low)),
            ("cg", token_slices[half:]),
        ],
    )

    def over_rows(slices, wide):
        return contract_first(
            slices.reshape(n_dp * row_count, feature_rows), wide.reshape(n_dp * row_count, -1)
        )

    down_grad = lax.psum_scatter(
        over_rows(grad_two_slices, hidden_all), "ctx", scatter_dimension=0, tiled=True
    )
    grad_normed = normed_part + jnp.sum(normed_other, axis=0) + grad_two
    grad_one, gain_one_grad, shift_one_grad = norm_back(grad_normed, z_one, rstd_one, gains_wide[0])
    grad_one_low = grad_one.astype(jnp.bfloat16)
    grad_attn = jnp.dot(grad_one_low, out_full, preferred_element_type=jnp.float32).astype(
        jnp.bfloat16
    )
    grad_chunks, grad_one_slices, normed_slices = exchange(
        sizes,
        7,
        [
            ("ctx", by_heads(grad_attn, 1)),
            ("dp", feature_slices(grad_one_low)),
            ("dp", feature_slices(normed_low)),
        ],
    )
    up_grad = lax.psum_scatter(
        over_rows(normed_slices, grad_pre_all), "ctx", scatter_dimension=0, tiled=True
    )
    grad_mixed = to_positions(grad_chunks, 1)[0]
    out_grad = over_rows(grad_one_slices, attn_all)
    grad_queries, grad_keys, grad_values = lax.map(
        attend_backward, (queries, key_rows, value_rows, valid, mixed, log_total, grad_mixed)
    )
    proj_parts = by_position(
        [part.astype(jnp.bfloat16) for part in (grad_queries, grad_keys, grad_values)]
    )
    proj_wide = proj_parts.transpose(0, 2, 1, 3).reshape(n_ctx * row_count, 3 * group_width)
    proj_chunks, proj_all = exchange(sizes, 8, [("ctx", proj_parts), ("dpg", proj_wide)])
    token_all = (
        jnp.concatenate([token_low, token_high], axis=1)
        .transpose(1, 0, 2, 3)
        .reshape(n_dp * n_ctx * row_count, feature_rows)
    )
    qkv_part = contract_first(token_all, proj_all.reshape(n_dp * n_ctx * row_count, -1))
    grad_proj = to_rows(proj_chunks, 3)
    input_part = contract_last(grad_proj, qkv_full)
    head_rows = jnp.concatenate(
        [jnp.sum(grad_queries, axis=(0, 1)), jnp.sum(grad_values, axis=(0, 1))], axis=1
    )
    head_part = lax.dynamic_update_slice(
        jnp.zeros((local_heads, 2 * head_size), jnp.float32),
        head_rows,
        (lax.axis_index("ctx") * heads_here, 0),
    )
    gains_part = jnp.stack([gain_one_grad, gain_two_grad])
    biases_part = jnp.stack(
        [jnp.sum(grad_one, axis=0), shift_one_grad, jnp.sum(grad_two, axis=0), shift_two_grad]
    )
    small_parts = [
        part.reshape(part.shape[0], shards, -1).transpose(1, 0, 2)
        for part in (head_part, hidden_part, gains_part, biases_part)
    ]
    input_other, small_sums, out_blocks, qkv_blocks = exchange(
        sizes,
        9,
        [
            ("swap", input_part),
            ("all", pack(small_parts, shards, 1024)),
            ("ctx", out_grad.reshape(n_ctx, feature_rows // n_ctx, -1)),
            ("ctx", qkv_part.reshape(n_ctx, feature_rows // n_ctx, -1)),
        ],
    )
    input_grad = (input_part + jnp.sum(input_other, axis=0) + grad_one).reshape(
        seq_count, local_len, width
    )
    qkv_grad = (
        qkv_blocks.reshape(n_ctx, -1, 3, group_width)
        .transpose(1, 2, 0, 3)
        .reshape(-1, 3, local_width)
    )
    small_grads = unpack(
        jnp.sum(small_sums, axis=0)[None], [part.shape[1:] for part in small_parts]
    )
    return (
        output,
        input_grad,
        qkv_grad,
        jnp.sum(out_blocks, axis=0),
        up_grad,
        down_grad,
        *(part[0] for part in small_grads),
    )


MESH = pl.DeviceIdType.MESH


def dot_nn(left, right):
    return jnp.dot(left, right, preferred_element_type=jnp.float32)


class Links:
    def __init__(self, send_sem, recv_sem, own_sem, partner):
        self.send_sem, self.recv_sem, self.own_sem = send_sem, recv_sem, own_sem
        self.partner, self.sent, self.used, self.kept = partner, {}, 0, 0
        self.at_close = []

    def reserve(self):
        self.used += 1
        return self.used - 1

    def copy(self, number, source, target, to, got=None):
        return pltpu.make_async_remote_copy(
            src_ref=source,
            dst_ref=target,
            send_sem=self.send_sem.at[number],
            recv_sem=self.recv_sem.at[number if got is None else got],
            device_id=to,
            device_id_type=MESH,
        )

    def put(self, source, target, to):
        number = self.reserve()
        copy = self.copy(number, source, target, to)
        copy.start()
        self.sent[number] = copy
        return number

    def put_if(self, condition, number, ends, got=None):
        @pl.when(condition)
        def _():
            self.copy(number, *ends(), got).start()

        self.at_close.append((condition, number, ends))

    def arrive(self, number, target):
        self.copy(number, target, target, self.partner).wait_recv()

    def keep(self, source, target):
        copy = pltpu.make_async_copy(source, target, self.own_sem.at[self.kept])
        self.kept += 1
        copy.start()
        return copy

    def sent_all(self, number):
        self.sent.pop(number).wait_send()

    def close(self):
        for copy in self.sent.values():
            copy.wait_send()
        for condition, number, ends in self.at_close:

            @pl.when(condition)
            def _():
                self.copy(number, *ends()).wait_send()


class RowGather:
    def __init__(self, net, at, source, slot, block):
        self.net, self.at, self.source, self.slot, self.block = net, at, source, slot, block

    def start(self):
        net, at = self.net, self.at
        mine = self.slot(at.dp, at.z)
        self.own = net.keep(self.source, mine)
        self.along = [net.put(self.source, mine, at.z_to(k)) for k in range(1, at.nz)]
        self.across = [(net.put(self.source, mine, at.x_to), at.z)]

    def cross(self):
        net, at = self.net, self.at
        for k in range(1, at.nz):
            origin = at.z_from(k)
            got = self.slot(at.dp, origin)
            net.arrive(self.along[k - 1], got)
            self.across.append((net.put(got, got, at.x_to), origin))
        self.own.wait()
        block = self.block(at.dp)
        self.near = net.put(block, block, at.c_to)

    def relay(self):
        net, at = self.net, self.at
        for number, origin in self.across:
            net.arrive(number, self.slot(at.x_dp, origin))
        block = self.block(at.x_dp)
        self.far = net.put(block, block, at.c_to)

    def finish(self):
        self.net.arrive(self.near, self.block(self.at.c_dp))
        self.net.arrive(self.far, self.block(self.at.xc_dp))


class LineGather(RowGather):
    def start(self):
        net, at = self.net, self.at
        mine = self.slot(at.dp, at.z)
        self.own = net.keep(self.source, mine)
        self.across = [(net.put(self.source, mine, at.x_to), at.z)]
        self.numbers = [
            [[net.reserve() for _ in range(2)] for _ in range(at.nz)] for _ in range(2)
        ]
        for way in range(2):
            net.put_if(
                self.ahead(way),
                self.numbers[way][1][0],
                lambda way=way: (self.source, self.slot(at.dp, at.z), at.next_to(way)),
            )

    def ahead(self, way):
        return self.at.z < self.at.nz - 1 if way == 0 else self.at.z > 0

    def behind(self, way, hop):
        return self.at.z >= hop if way == 0 else self.at.z + hop < self.at.nz

    def got(self, way, hop, dp):
        return self.slot(dp, (self.at.z + (-hop if way == 0 else hop) + self.at.nz) % self.at.nz)

    def hop(self, hop):
        net, at = self.net, self.at
        for way in range(2):
            along, across = self.numbers[way][hop]

            def ends(to, way=way):
                got = self.got(way, hop, at.dp)
                return got, got, to

            @pl.when(self.behind(way, hop))
            def _():
                net.arrive(along, self.got(way, hop, at.dp))

            if hop < at.nz - 1:
                net.put_if(
                    jnp.logical_and(self.behind(way, hop), self.ahead(way)),
                    self.numbers[way][hop + 1][0],
                    lambda ends=ends, way=way: ends(at.next_to(way)),
                )
            net.put_if(self.behind(way, hop), across, lambda ends=ends: ends(at.x_to))
        if hop == at.nz - 1:
            self.own.wait()
            block = self.block(at.dp)
            self.near = net.put(block, block, at.c_to)

    def relay(self):
        net, at = self.net, self.at
        for hop in range(1, at.nz):
            for way in range(2):

                @pl.when(self.behind(way, hop))
                def _():
                    net.arrive(self.numbers[way][hop][1], self.got(way, hop, at.x_dp))

        super().relay()


class Place:
    def __init__(self, nz):
        self.nz = nz
        self.dp, self.z, self.y = (lax.axis_index(name) for name in ("dp", "ctx", "tensor"))
        dp, z, y = self.dp, self.z, self.y
        self.x, self.c = dp // 2, dp % 2
        self.c_dp = self.x * 2 + 1 - self.c
        self.x_dp = (1 - self.x) * 2 + self.c
        self.xc_dp = (1 - self.x) * 2 + 1 - self.c
        self.x_to = {"dp": self.x_dp, "ctx": z, "tensor": y}
        self.c_to = {"dp": self.c_dp, "ctx": z, "tensor": y}
        self.xc_to = {"dp": self.xc_dp, "ctx": z, "tensor": y}
        self.y_to = {"dp": dp, "ctx": z, "tensor": 1 - y}

        self.is_end = jnp.logical_or(z == 0, z == nz - 1)

    def seen(self, k):
        return jnp.where(self.z < self.nz // 2, k, self.nz - 1 - k)

    def along_to(self, z):
        return {"dp": self.dp, "ctx": z, "tensor": self.y}

    def z_at(self, k):
        return (self.z + k) % self.nz

    def z_from(self, k):
        return (self.z + self.nz - k) % self.nz

    def z_to(self, k):
        return {"dp": self.dp, "ctx": self.z_at(k), "tensor": self.y}

    def next_to(self, way):
        return self.z_to(1 if way == 0 else self.nz - 1)

    def zy_to(self, k):
        return {"dp": self.dp, "ctx": self.z_at(k), "tensor": 1 - self.y}

    def greet(self):
        peers = [self.x_to, self.c_to, self.xc_to, self.y_to]
        for k in range(1, self.nz):
            peers += [self.z_to(k), self.zy_to(k)]
        barrier = pltpu.get_barrier_semaphore()
        for peer in peers:
            pl.semaphore_signal(barrier, inc=1, device_id=peer, device_id_type=MESH)
        pl.semaphore_wait(barrier, len(peers))


def rows_at(index, size):
    return pl.ds(pl.multiple_of(index * size, size), size)


def row_sum(value):
    return jnp.sum(value, axis=0, keepdims=True)


def norm_back_rows(grad_out, normed, inv_std, gain):
    grad_normed = grad_out * gain
    first_mean = jnp.mean(grad_normed, axis=-1, keepdims=True)
    second_mean = jnp.mean(grad_normed * normed, axis=-1, keepdims=True)
    return inv_std * (grad_normed - first_mean - normed * second_mean)


def last_by_tiles(target, lefts, rights, tile=512):
    count = target.shape[1]
    tile = min(tile, count)

    def step(number, carry):
        columns = rows_at(number, tile)
        value = contract_last(lefts[0](), rights[0](columns))
        for left, right in zip(lefts[1:], rights[1:]):
            value += contract_last(left(), right(columns))
        target[:, columns] = value
        return carry

    lax.fori_loop(0, count // tile, step, 0)


class ColumnGrad:
    def __init__(self, net, at, turned, turned_all, wide, wide_all, total, got, out):
        self.net, self.at = net, at
        self.turned, self.turned_all = turned, turned_all
        self.wide, self.wide_all = wide, wide_all
        self.total, self.got, self.out = total, got, out
        self.half = wide_all.shape[2]
        self.block = turned_all.shape[0]
        self.rows = turned.shape[1]
        self.depth = got.shape[2]

    def send_wide(self):
        net, at = self.net, self.at
        mine = self.wide.at[:, rows_at(at.c, self.half)]
        theirs = self.wide.at[:, rows_at(1 - at.c, self.half)]
        slot = self.wide_all.at[at.dp]
        self.waits_wide = [
            (net.put(mine, slot, at.x_to), at.x_dp),
            (net.put(theirs, slot, at.xc_to), at.xc_dp),
            (net.put(theirs, slot, at.c_to), at.c_dp),
        ]
        self.own_wide = net.keep(mine, slot)

    def turned_of(self, dp):
        return self.turned_all.at[:, rows_at(dp, self.rows)]

    def send_turned(self):
        net, at = self.net, self.at
        mine = self.turned.at[rows_at(at.x, self.block)]
        theirs = self.turned.at[rows_at(1 - at.x, self.block)]
        slot = self.turned_of(at.dp)
        self.turned_x = net.put(theirs, slot, at.x_to)
        self.turned_c = net.put(mine, slot, at.c_to)
        self.own_turned = net.keep(mine, slot)

    def hand_on(self):
        net, at = self.net, self.at
        got = self.turned_of(at.x_dp)
        net.arrive(self.turned_x, got)
        self.turned_xc = net.put(got, got, at.c_to)

    def multiply(self):
        net, at = self.net, self.at
        self.own_wide.wait()
        self.own_turned.wait()
        for number, dp in self.waits_wide:
            net.arrive(number, self.wide_all.at[dp])
        net.arrive(self.turned_c, self.turned_of(at.c_dp))
        net.arrive(self.turned_xc, self.turned_of(at.xc_dp))
        tile = min(256, self.half)
        n_dp = self.wide_all.shape[0]
        middle = self.block // 2

        def step(number, carry):
            columns = rows_at(number, tile)
            value = dot_nn(self.turned_all[:, : self.rows], self.wide_all[0, :, columns])
            for dp in range(1, n_dp):
                value += dot_nn(
                    self.turned_all[:, dp * self.rows : (dp + 1) * self.rows],
                    self.wide_all[dp, :, columns],
                )
            self.total[0, :, columns] = value[:middle]
            self.total[1, :, columns] = value[middle:]
            return carry

        lax.fori_loop(0, self.half // tile, step, 0)

    def chunk(self, z):
        return self.total.at[:, rows_at(z, self.depth)]

    def spread(self):
        net, at = self.net, self.at
        self.numbers = [net.reserve() for _ in range(5)]
        far_end, far_mid, plain, _, _ = self.numbers
        for slot, (number, to) in enumerate(((far_end, 3), (far_mid, 2))):
            net.put_if(
                at.is_end,
                number,
                lambda slot=slot, to=to: (self.chunk(at.seen(to)), self.got.at[slot], at.along_to(at.seen(1))),
            )
        net.put_if(
            at.is_end, plain, lambda: (self.chunk(at.seen(1)), self.got.at[2], at.along_to(at.seen(1)))
        )
        net.put_if(
            jnp.logical_not(at.is_end),
            plain,
            lambda: (self.chunk(at.seen(0)), self.got.at[2], at.along_to(at.seen(0))),
        )

    def pass_on(self, slot):
        net, at = self.net, self.at
        to = 3 - slot
        middle = jnp.logical_not(at.is_end)

        @pl.when(middle)
        def _():
            net.arrive(self.numbers[slot], self.got.at[slot])
            for core in range(2):
                self.got[slot, core] += self.total[core, rows_at(at.seen(to), self.depth), :]

        net.put_if(
            middle,
            self.numbers[3 + slot],
            lambda: (self.got.at[slot], self.got.at[3], at.along_to(at.seen(to))),
            self.numbers[3],
        )

    def swap_cores(self):
        net, at = self.net, self.at
        net.arrive(self.numbers[2], self.got.at[2])
        net.arrive(self.numbers[3], self.got.at[3])

        def added(core):
            return (
                self.total[core, rows_at(at.z, self.depth), :] + self.got[2, core] + self.got[3, core]
            )

        place = rows_at(at.c, self.half)
        self.got[2, 1 - at.c] = added(1 - at.c)
        self.last = net.put(self.got.at[2, 1 - at.c], self.out.at[:, place], at.c_to)
        self.out[:, place] = added(at.c)

    def finish(self):
        self.net.arrive(self.last, self.out.at[:, rows_at(1 - self.at.c, self.half)])


def layer_kernel(dims, names, *refs):
    (nz, head_size, small_rows) = dims
    r = dict(zip(names, refs))

    class Refs:
        pass

    m = Refs()
    m.__dict__.update(r)
    at = Place(nz)
    net = Links(m.send_sem, m.recv_sem, m.own_sem, at.c_to)
    rows, width = m.tok.shape
    half = rows // 2
    total_len = rows * nz
    group = m.queries.shape[1]
    heads = group // head_size
    shard = m.outw.shape[0]
    part_rows = nz * shard
    local_width = m.outw.shape[1]
    hidden = m.upw.shape[1]
    groups_wide = width // 128
    bf16, f32 = jnp.bfloat16, jnp.float32
    mine, other = rows_at(at.y, half), rows_at(1 - at.y, half)
    at.greet()

    def gather(source, full, form=RowGather):
        return form(
            net,
            at,
            source,
            lambda dp, z: full.at[rows_at(dp * nz + z, source.shape[0])],
            lambda dp: full.at[rows_at(dp, nz * source.shape[0])],
        )

    def qkv_slot(g, dp, z):
        return m.wfull.at[g, rows_at(dp * nz + z, shard)]

    def qkv_block(g, dp):
        return m.wfull.at[g, rows_at(dp, part_rows)]

    own_qkv = net.keep(m.wq.at[at.z], qkv_slot(at.z, at.dp, at.z))
    qkv_along = [
        net.put(m.wq.at[at.z_at(k)], qkv_slot(at.z_at(k), at.dp, at.z), at.z_to(k))
        for k in range(1, nz)
    ]
    qkv_across = [(net.put(m.wq.at[at.z], qkv_slot(at.z, at.dp, at.z), at.x_to), at.z)]
    small = gather(m.small, m.small_all)
    small.start()
    own_rows = net.keep(m.tok, m.xall.at[rows_at(at.z, rows)])

    def half_of(z, y):
        return m.xall.at[rows_at(z * 2 + y, half)]

    token_along = [
        net.put(m.tok.at[mine], half_of(at.z, at.y), at.z_to(k)) for k in range(1, nz)
    ]
    for k in range(1, nz):
        origin = at.z_from(k)
        got = qkv_slot(at.z, at.dp, origin)
        net.arrive(qkv_along[k - 1], got)
        qkv_across.append((net.put(got, got, at.x_to), origin))
    own_qkv.wait()
    near = qkv_block(at.z, at.dp)
    qkv_near = net.put(near, near, at.c_to)
    small.cross()
    token_y = []
    for k in range(1, nz):
        origin = at.z_from(k)
        got = half_of(origin, at.y)
        net.arrive(token_along[k - 1], got)
        token_y.append((net.put(got, got, at.y_to), origin))
    outs = gather(m.outw, m.outf.at[at.y])
    outs.start()
    ups = gather(m.upw, m.up, LineGather)
    ups.start()
    for number, origin in qkv_across:
        net.arrive(number, qkv_slot(at.z, at.x_dp, origin))
    far = qkv_block(at.z, at.x_dp)
    qkv_far = net.put(far, far, at.c_to)
    small.relay()
    small.finish()
    small_sum = m.small_all[:small_rows, :].astype(f32)
    for slot in range(1, 4 * nz):
        small_sum += m.small_all[slot * small_rows : (slot + 1) * small_rows, :].astype(f32)
    m.smalls[...] = small_sum
    for row in range(6):
        for j in range(groups_wide):
            at_row = row * groups_wide + j
            m.norms[row : row + 1, j * 128 : (j + 1) * 128] = m.smalls[at_row : at_row + 1, :]
    query_row = 6 * groups_wide
    value_row = query_row + nz
    hidden_row = value_row + nz
    for j in range(hidden // 128):
        m.hbias[:, j * 128 : (j + 1) * 128] = m.smalls[hidden_row + j : hidden_row + j + 1, :]
    net.arrive(qkv_near, qkv_block(at.z, at.c_dp))
    net.arrive(qkv_far, qkv_block(at.z, at.xc_dp))
    downs = gather(m.downw, m.down, LineGather)
    own_rows.wait()
    for number, origin in token_y:
        net.arrive(number, half_of(origin, 1 - at.y))
    bias_q = m.smalls[pl.ds(query_row + at.z, 1), :]
    bias_v = m.smalls[pl.ds(value_row + at.z, 1), :]

    def project(block, carry):
        place = rows_at(block, rows)
        value = dot_nn(m.xall[place, :], m.wfull[at.z])
        m.queries[place, :] = (value[:, :group] + bias_q).astype(bf16)
        key = value[:, group : 2 * group]
        m.keys[place, :] = key.astype(bf16)
        m.keys_t[:, place] = key.T.astype(bf16)
        val = value[:, 2 * group :] + bias_v
        m.values[place, :] = val.astype(bf16)
        m.values_t[:, place] = val.T.astype(bf16)
        return carry

    lax.fori_loop(0, nz, project, 0)
    outs.cross()
    y_rows = width // 2

    valid = lax.broadcasted_iota(jnp.int32, (total_len, 1), 0) < m.lens[0]
    lane_head = lax.broadcasted_iota(jnp.int32, (1, group), 1) // head_size
    row_head = lax.broadcasted_iota(jnp.int32, (group, 1), 0) // head_size

    def head_of(value, h):
        return jnp.where(lane_head == h, value, jnp.zeros_like(value))

    def scores_of(query):
        return jnp.where(valid, contract_last(m.keys[...], query) * SCALE, NEG_BIG)

    def attend(block):
        place = rows_at(block, rows)
        query = m.queries[place, :]
        mixed = jnp.zeros((group, rows), f32)
        for h in range(heads):
            score = scores_of(head_of(query, h))
            peak = jnp.max(score, axis=0, keepdims=True)
            grown = jnp.exp(score - peak)
            total = jnp.sum(grown, axis=0, keepdims=True)
            m.log_total[h : h + 1, place] = peak + jnp.log(total)
            probs = (grown * (1.0 / total)).astype(bf16)
            mixed = jnp.where(row_head == h, dot_nn(m.values_t[...], probs), mixed)
        m.mixed[place, :] = mixed.T.astype(bf16)

    def columns_of(y, z):
        return m.attn.at[:, rows_at(y * nz + z, group)]

    mixed_along = []
    for k in list(range(1, nz)) + [0]:
        if k == 0:
            outs.relay()
            outs.finish()
            out_half = m.outf.at[at.y, rows_at(at.c, y_rows)]
            out_y = net.put(out_half, out_half, at.y_to)
        attend(at.z_at(k))
        part = m.mixed.at[rows_at(at.z_at(k), rows)]
        if k:
            mixed_along.append(net.put(part, columns_of(at.y, at.z), at.z_to(k)))
            if k == 2:
                ups.hop(1)
        else:
            own_mixed = net.keep(part, columns_of(at.y, at.z))
            mixed_y = [(net.put(part, columns_of(at.y, at.z), at.y_to), at.z)]
    ups.hop(2)
    downs.start()
    for k in range(1, nz):
        origin = at.z_from(k)
        got = columns_of(at.y, origin)
        net.arrive(mixed_along[k - 1], got)
        mixed_y.append((net.put(got, got, at.y_to), origin))
    ups.hop(3)

    def turn_rows(block, carry):
        place = rows_at(block, rows)
        m.xall_t[:, place] = m.xall[place, :].T
        return carry

    downs.hop(1)
    got = m.outf.at[1 - at.y, rows_at(at.c, y_rows)]
    net.arrive(out_y, got)
    out_near = net.put(got, got, at.c_to)
    net.arrive(out_near, m.outf.at[1 - at.y, rows_at(1 - at.c, y_rows)])
    own_mixed.wait()
    for number, origin in mixed_y:
        net.arrive(number, columns_of(1 - at.y, origin))

    gain_one, gain_two = m.norms[0:1, :], m.norms[1:2, :]
    shift = [m.norms[2 + i : 3 + i, :] for i in range(4)]

    def first_norm(place, kept):
        first_sum = (
            m.tok[place, :].astype(f32)
            + contract_last(m.attn[place, :local_width], m.outf[0])
            + contract_last(m.attn[place, local_width:], m.outf[1])
            + shift[0]
        )
        normed, z_one, rstd = layer_norm(first_sum, gain_one, shift[1])
        if kept:
            m.normed[...] = normed
            m.z_one[...] = z_one
            m.rstd[...] = rstd
        m.normed_low[place, :] = normed.astype(bf16)

    first_norm(other, False)
    first_norm(mine, True)
    ups.relay()
    downs.hop(2)
    ups.finish()

    tile = min(512, hidden)

    def feed(place):
        def step(number, carry):
            columns = rows_at(number, tile)
            pre = dot_nn(m.normed_low[place, :], m.up[:, columns]) + m.hbias[:, columns]
            activated, slope = gelu_parts(pre)
            m.hid[place, columns] = activated.astype(bf16)
            m.slope[place, columns] = slope
            return carry

        lax.fori_loop(0, hidden // tile, step, 0)

    feed(other)
    downs.hop(3)
    feed(mine)
    downs.relay()
    down_grad = ColumnGrad(
        net, at, m.grad_two_t, m.grad_two_all, m.hid, m.hid_all, m.down_total, m.down_got, m.down_grad
    )
    up_grad = ColumnGrad(
        net, at, m.normed_t, m.normed_all, m.grad_pre, m.grad_pre_all, m.up_total, m.up_got, m.up_grad
    )
    out_grad = ColumnGrad(
        net,
        at,
        m.grad_one_t,
        m.grad_one_all,
        m.attn.at[:, rows_at(at.y, local_width)],
        m.attn_all,
        m.out_total,
        m.out_got,

        m.out_grad,
    )
    down_grad.send_wide()
    downs.finish()
    late = []
    for k in range(1, nz):
        for j in range(1, nz):
            g = at.z_at(k + j)
            target = qkv_slot(g, at.dp, at.z)
            late.append((net.put(m.wq.at[g], target, at.z_to(k)), k, j))
    late_own = [
        net.keep(m.wq.at[at.z_at(j)], qkv_slot(at.z_at(j), at.dp, at.z)) for j in range(1, nz)
    ]
    last_by_tiles(m.part_a, [lambda: m.hid[other, :]], [lambda at_rows: m.down[at_rows, :]])
    part_a = net.put(m.part_a, m.got_a, at.y_to)
    last_by_tiles(m.kept, [lambda: m.hid[mine, :]], [lambda at_rows: m.down[at_rows, :]])
    m.normed_t[...] = m.normed_low[...].T
    lax.fori_loop(0, nz, turn_rows, 0)
    net.arrive(part_a, m.got_a)
    second_sum = m.normed[...] + (m.kept[...] + m.got_a[...]) + shift[2]
    result, z_two, rstd_two = layer_norm(second_sum, gain_two, shift[3])
    grad_out = m.cot[mine, :].astype(f32)
    grad_two = norm_back_rows(grad_out, z_two, rstd_two, gain_two)
    m.grad_two[...] = grad_two
    m.grad_two_low[mine, :] = grad_two.astype(bf16)
    two_y = net.put(m.grad_two_low.at[mine], m.grad_two_low.at[mine], at.y_to)
    m.output[mine, :] = result.astype(bf16)
    sums = {1: row_sum(grad_out * z_two), 5: row_sum(grad_out), 4: row_sum(grad_two)}

    m.hidden_sum[...] = jnp.zeros_like(m.hidden_sum)

    def feed_back(place):
        def step(number, carry):
            columns = rows_at(number, tile)
            grad_hidden = dot_nn(m.grad_two_low[place, :], m.down[:, columns])
            grad_pre = grad_hidden * m.slope[place, columns]
            m.grad_pre[place, columns] = grad_pre.astype(bf16)
            m.hidden_sum[:, columns] += row_sum(grad_pre)
            return carry

        lax.fori_loop(0, hidden // tile, step, 0)

    feed_back(mine)
    net.arrive(two_y, m.grad_two_low.at[other])
    m.grad_two_t[...] = m.grad_two_low[...].T
    down_grad.send_turned()
    feed_back(other)
    up_grad.send_wide()
    net.sent_all(part_a)
    last_by_tiles(m.part_a, [lambda: m.grad_pre[other, :]], [lambda at_rows: m.up[at_rows, :]])
    part_b = net.put(m.part_a, m.got_a, at.y_to)
    last_by_tiles(m.kept, [lambda: m.grad_pre[mine, :]], [lambda at_rows: m.up[at_rows, :]])
    net.arrive(part_b, m.got_a)
    grad_normed = m.kept[...] + m.got_a[...] + m.grad_two[...]
    z_mine = m.z_one[...]
    grad_one = norm_back_rows(grad_normed, z_mine, m.rstd[...], gain_one)
    m.grad_one[...] = grad_one
    m.grad_one_low[mine, :] = grad_one.astype(bf16)
    sums[0] = row_sum(grad_normed * z_mine)
    sums[3] = row_sum(grad_normed)
    sums[2] = row_sum(grad_one)
    def back_step(y, carry):
        value = dot_nn(m.grad_one_low[mine, :], m.outf[y])
        m.grad_attn[:, rows_at(y, local_width)] = value.astype(bf16)
        return carry

    lax.fori_loop(0, 2, back_step, 0)

    def attn_part(y, z):
        return m.grad_attn.at[:, rows_at(y * nz + z, group)]

    my_slot = m.grad_mixed.at[rows_at(at.z * 2 + at.y, half)]
    grad_along = []
    for k in range(1, nz):
        grad_along.append((net.put(attn_part(at.y, at.z_at(k)), my_slot, at.z_to(k)), at.z_from(k), at.y))
        grad_along.append(
            (net.put(attn_part(1 - at.y, at.z_at(k)), my_slot, at.zy_to(k)), at.z_from(k), 1 - at.y)
        )
    grad_along.append((net.put(attn_part(1 - at.y, at.z), my_slot, at.y_to), at.z, 1 - at.y))
    own_grad = net.keep(attn_part(at.y, at.z), my_slot)
    one_y = net.put(m.grad_one_low.at[mine], m.grad_one_low.at[mine], at.y_to)
    up_grad.send_turned()
    out_grad.send_wide()
    down_grad.hand_on()
    down_grad.multiply()
    down_grad.spread()

    for number, origin, y in grad_along:
        net.arrive(number, m.grad_mixed.at[rows_at(origin * 2 + y, half)])
    own_grad.wait()
    net.arrive(one_y, m.grad_one_low.at[other])
    output_y = net.put(m.output.at[mine], m.output.at[mine], at.y_to)
    m.grad_one_t[...] = m.grad_one_low[...].T
    out_grad.send_turned()
    down_grad.pass_on(0)

    product = m.grad_mixed[...].astype(f32) * m.mixed[...].astype(f32)
    turned = product.T
    for h in range(heads):
        m.inner[h : h + 1, :] = row_sum(turned[h * head_size : (h + 1) * head_size, :])
    m.acc_query[...] = jnp.zeros_like(m.acc_query)

    def attend_back(block, value_sum):
        place = rows_at(block, rows)
        keys, values = m.keys[place, :], m.values[place, :]
        grad_keys = jnp.zeros((rows, group), f32)
        grad_values = jnp.zeros((rows, group), f32)
        valid_here = lax.broadcasted_iota(jnp.int32, (rows, 1), 0) + block * rows < m.lens[0]
        for h in range(heads):
            query_h = head_of(m.queries[...], h)
            grad_h = head_of(m.grad_mixed[...], h)
            score = jnp.where(valid_here, contract_last(keys, query_h) * SCALE, NEG_BIG)
            probs = jnp.exp(score - m.log_total[h : h + 1, :])
            grad_values += dot_nn(probs.astype(bf16), grad_h)
            grad_probs = contract_last(values, grad_h)
            grad_scores = (probs * (grad_probs - m.inner[h : h + 1, :])).astype(bf16)
            grad_keys += dot_nn(grad_scores, query_h)
            m.acc_query[h] += dot_nn(m.keys_t[:, place], grad_scores)
        m.grad_proj[place, group : 2 * group] = (grad_keys * SCALE).astype(bf16)
        m.grad_proj[place, 2 * group :] = grad_values.astype(bf16)
        return value_sum + row_sum(grad_values)

    value_sum = jnp.zeros((1, group), f32)
    wide = pl.ds(group, 2 * group)
    proj_along = []
    for k in list(range(1, nz)) + [0]:
        value_sum = attend_back(at.z_at(k), value_sum)
        if k:
            part = m.grad_proj.at[rows_at(at.z_at(k), rows), wide]
            slot = m.proj_rows.at[at.z, :, wide]
            proj_along.append((net.put(part, slot, at.z_to(k)), at.z_from(k), wide))
        if k == 2:
            down_grad.pass_on(1)
    narrow = pl.ds(0, group)
    query_sum = jnp.zeros((1, group), f32)
    for k in range(nz):
        place = rows_at(at.z_at(k), rows)
        grad_query = m.acc_query[0, :, place]
        for h in range(1, heads):
            grad_query = jnp.where(row_head == h, m.acc_query[h, :, place], grad_query)
        grad_query = grad_query.T * SCALE
        query_sum += row_sum(grad_query)
        m.grad_proj[place, :group] = grad_query.astype(bf16)
        if k:
            part = m.grad_proj.at[place, narrow]
            slot = m.proj_rows.at[at.z, :, narrow]
            proj_along.append((net.put(part, slot, at.z_to(k)), at.z_from(k), narrow))
    own_proj = net.keep(m.grad_proj.at[rows_at(at.z, rows)], m.proj_rows.at[at.z])

    m.small_sum[...] = jnp.zeros_like(m.small_sum)
    for row in range(6):
        for j in range(groups_wide):
            at_row = row * groups_wide + j
            m.small_sum[at_row : at_row + 1, :] = sums[row][:, j * 128 : (j + 1) * 128]
    m.small_sum[pl.ds(query_row + at.z, 1), :] = query_sum
    m.small_sum[pl.ds(value_row + at.z, 1), :] = value_sum
    for j in range(hidden // 128):
        m.small_sum[hidden_row + j : hidden_row + j + 1, :] = m.hidden_sum[:, j * 128 : (j + 1) * 128]
    small_along = [net.put(m.small_sum, m.small_got.at[k - 1], at.z_to(k)) for k in range(1, nz)]

    up_grad.hand_on()
    up_grad.multiply()
    up_grad.spread()
    late_x = []
    for number, k, j in late:
        got = qkv_slot(at.z_at(j), at.dp, at.z_from(k))
        net.arrive(number, got)
    for copy in late_own:
        copy.wait()
    for j in range(1, nz):
        block = qkv_block(at.z_at(j), at.dp)
        late_x.append((net.put(block, block, at.x_to), net.put(block, block, at.c_to), j))
    def qkv_step(block, carry):
        place = rows_at(block, rows)
        m.qkv_total[place, :] = dot_nn(m.xall_t[place, :], m.grad_proj[...])
        return carry

    lax.fori_loop(0, width // rows, qkv_step, 0)
    core_waits = []
    for x in range(2):
        part = m.qkv_total.at[rows_at(x * 2 + 1 - at.c, part_rows)]
        core_waits.append(net.put(part, m.qkv_core.at[x], at.c_to))
    for x in range(2):
        net.arrive(core_waits[x], m.qkv_core.at[x])
    across_rows, kept_rows = rows_at(at.x_dp, part_rows), rows_at(at.dp, part_rows)
    m.qkv_total[across_rows, :] += m.qkv_core[1 - at.x]
    qkv_x = net.put(m.qkv_total.at[across_rows], m.qkv_got, at.x_to)
    out_grad.hand_on()
    out_grad.multiply()
    out_grad.spread()
    up_grad.pass_on(0)
    for k in range(1, nz):
        net.arrive(small_along[k - 1], m.small_got.at[k - 1])
    value = m.small_sum[...]
    for k in range(1, nz):
        value += m.small_got[k - 1]
    m.small_two[...] = value
    small_x = net.put(m.small_two, m.small_got.at[nz - 1], at.x_to)
    late_c = []
    for across, near, j in late_x:
        block = qkv_block(at.z_at(j), at.x_dp)
        net.arrive(across, block)
        late_c.append((net.put(block, block, at.c_to), near, j))
    for across, near, j in late_c:
        net.arrive(near, qkv_block(at.z_at(j), at.c_dp))
        net.arrive(across, qkv_block(at.z_at(j), at.xc_dp))
    own_proj.wait()
    for number, origin, columns in proj_along:
        net.arrive(number, m.proj_rows.at[origin, :, columns])

    def input_part(target, place):
        last_by_tiles(
            target,
            [lambda g=g: m.proj_rows[g, place, :] for g in range(nz)],
            [lambda at_rows, g=g: m.wfull[g, at_rows, :] for g in range(nz)],
        )

    net.sent_all(part_b)
    input_part(m.part_a, other)
    part_c = net.put(m.part_a, m.got_a, at.y_to)
    input_part(m.kept, mine)
    up_grad.pass_on(1)
    out_grad.pass_on(0)
    net.arrive(qkv_x, m.qkv_got)
    m.qkv_total[kept_rows, :] += m.qkv_core[at.x] + m.qkv_got[...]
    qkv_z = [
        net.put(
            m.qkv_total.at[rows_at(at.dp * nz + at.z_at(k), shard)], m.qkv_grad.at[at.z], at.z_to(k)
        )
        for k in range(1, nz)
    ]
    m.qkv_grad[at.z] = m.qkv_total[rows_at(at.dp * nz + at.z, shard), :]
    net.arrive(small_x, m.small_got.at[nz - 1])
    m.small_three[...] = m.small_two[...] + m.small_got[nz - 1]
    small_c = net.put(m.small_three, m.small_got.at[nz], at.c_to)
    net.arrive(part_c, m.got_a)
    m.input_grad[mine, :] = m.kept[...] + m.got_a[...] + m.grad_one[...]
    input_y = net.put(m.input_grad.at[mine], m.input_grad.at[mine], at.y_to)
    net.arrive(small_c, m.small_got.at[nz])
    m.small_four[...] = m.small_three[...] + m.small_got[nz]
    small_y = net.put(m.small_four, m.small_got.at[nz + 1], at.y_to)
    out_grad.pass_on(1)
    down_grad.swap_cores()
    up_grad.swap_cores()
    out_grad.swap_cores()
    net.arrive(small_y, m.small_got.at[nz + 1])
    shared = lax.broadcasted_iota(jnp.int32, (small_rows, 1), 0) < query_row
    m.small_grad[...] = m.small_four[...] + jnp.where(shared, m.small_got[nz + 1], 0.0)
    for k in range(1, nz):
        net.arrive(qkv_z[k - 1], m.qkv_grad.at[at.z_from(k)])
    net.arrive(output_y, m.output.at[other])
    net.arrive(input_y, m.input_grad.at[other])
    for item in (down_grad, up_grad, out_grad):
        item.finish()
    net.close()


def fused(
    sizes,
    tokens,
    seq_lengths,
    qkv_weight,
    out_weight,
    up_weight,
    down_weight,
    head_bias,
    hidden_bias,
    norm_gains,
    out_biases,
    cotangent,
):
    n_outer, n_core, nz, n_tensor = sizes
    n_dp = n_outer * n_core
    shards = n_dp * nz
    _, rows, width = tokens.shape
    shard, _, local_width = qkv_weight.shape
    hidden = up_weight.shape[1]
    head_size = head_bias.shape[1] * shards // 2
    group = local_width // nz
    total_len = rows * nz
    bf16, f32 = jnp.bfloat16, jnp.float32
    place = lax.axis_index("dp") * nz + lax.axis_index("ctx")

    def spread(part):
        here = jnp.arange(shards)[None, :, None] == place
        return jnp.where(here, part[:, None, :], jnp.zeros((), bf16)).reshape(part.shape[0], -1)

    head_wide = spread(head_bias)
    pieces = [
        spread(norm_gains),
        spread(out_biases),
        head_wide[:, :head_size],
        head_wide[:, head_size:],
        spread(hidden_bias),
    ]
    small = jnp.concatenate([piece.reshape(-1, 128) for piece in pieces], axis=0)
    used = small.shape[0]
    small_rows = -(-used // 16) * 16
    small = jnp.pad(small, ((0, small_rows - used), (0, 0)))
    wq = qkv_weight.reshape(shard, 3, nz, group).transpose(2, 0, 1, 3).reshape(nz, shard, 3 * group)
    tok = tokens.reshape(rows, width)
    cot = cotangent.reshape(rows, width)
    half = rows // 2
    ins = dict(
        lens=seq_lengths, tok=tok, cot=cot, wq=wq, outw=out_weight, upw=up_weight, downw=down_weight, small=small
    )
    outs = dict(
        output=((rows, width), bf16),
        input_grad=((rows, width), f32),
        qkv_grad=((nz, shard, 3 * group), f32),
        out_grad=((shard, local_width), f32),
        up_grad=((shard, hidden), f32),
        down_grad=((shard, hidden), f32),
        small_grad=((small_rows, 128), f32),
    )
    block = 2 * nz * shard
    part_rows = nz * shard
    scratch = dict(
        small_all=((shards * small_rows, 128), bf16),
        smalls=((small_rows, 128), f32),
        norms=((8, width), f32),
        hbias=((1, hidden), f32),
        wfull=((nz, width, 3 * group), bf16),
        xall=((total_len, width), bf16),
        xall_t=((width, total_len), bf16),
        outf=((2, width, local_width), bf16),
        up=((width, hidden), bf16),
        down=((width, hidden), bf16),
        queries=((total_len, group), bf16),
        keys=((total_len, group), bf16),
        values=((total_len, group), bf16),
        keys_t=((group, total_len), bf16),
        values_t=((group, total_len), bf16),
        mixed=((total_len, group), bf16),
        log_total=((max(8, group // head_size), total_len), f32),
        attn=((rows, width), bf16),
        normed=((half, width), f32),
        z_one=((half, width), f32),
        rstd=((half, 1), f32),
        normed_low=((rows, width), bf16),
        normed_t=((width, rows), bf16),
        hid=((rows, hidden), bf16),
        slope=((rows, hidden), f32),
        part_a=((half, width), f32),
        got_a=((half, width), f32),
        kept=((half, width), f32),
        grad_two=((half, width), f32),
        grad_two_low=((rows, width), bf16),
        grad_two_t=((width, rows), bf16),
        grad_pre=((rows, hidden), bf16),
        hidden_sum=((1, hidden), f32),
        grad_one=((half, width), f32),
        grad_one_low=((rows, width), bf16),
        grad_one_t=((width, rows), bf16),
        grad_attn=((half, width), bf16),
        grad_mixed=((total_len, group), bf16),
        acc_query=((group // head_size, group, total_len), f32),
        inner=((max(8, group // head_size), total_len), f32),
        grad_proj=((total_len, 3 * group), bf16),
        proj_rows=((nz, rows, 3 * group), bf16),
        small_sum=((small_rows, 128), f32),
        small_two=((small_rows, 128), f32),
        small_three=((small_rows, 128), f32),
        small_four=((small_rows, 128), f32),
        small_got=((nz + 2, small_rows, 128), f32),
        qkv_total=((width, 3 * group), f32),
        qkv_core=((2, part_rows, 3 * group), f32),
        qkv_got=((part_rows, 3 * group), f32),
        hid_all=((n_dp, rows, hidden // 2), bf16),
        grad_two_all=((block, n_dp * rows), bf16),
        down_total=((2, part_rows, hidden // 2), f32),
        down_got=((4, 2, shard, hidden // 2), f32),
        grad_pre_all=((n_dp, rows, hidden // 2), bf16),
        normed_all=((block, n_dp * rows), bf16),
        up_total=((2, part_rows, hidden // 2), f32),
        up_got=((4, 2, shard, hidden // 2), f32),
        attn_all=((n_dp, rows, local_width // 2), bf16),
        grad_one_all=((block, n_dp * rows), bf16),
        out_total=((2, part_rows, local_width // 2), f32),
        out_got=((4, 2, shard, local_width // 2), f32),
    )
    names = tuple(ins) + tuple(outs) + tuple(scratch) + ("send_sem", "recv_sem", "own_sem")
    vmem = pl.BlockSpec(memory_space=pltpu.VMEM)
    copies = 256
    result = pl.pallas_call(
        functools.partial(layer_kernel, (nz, head_size, small_rows), names),
        out_shape=tuple(jax.ShapeDtypeStruct(*spec) for spec in outs.values()),
        in_specs=[pl.BlockSpec(memory_space=pltpu.SMEM)] + [vmem] * (len(ins) - 1),
        out_specs=(vmem,) * len(outs),
        scratch_shapes=[pltpu.VMEM(*spec) for spec in scratch.values()]
        + [
            pltpu.SemaphoreType.DMA((copies,)),
            pltpu.SemaphoreType.DMA((copies,)),
            pltpu.SemaphoreType.DMA((40,)),
        ],
        compiler_params=pltpu.CompilerParams(
            collective_id=1, has_side_effects=True, vmem_limit_bytes=64 * 2**20 - 2**18
        ),
        name="layer",
    )(*ins.values())
    output, input_grad, qkv_grad, out_grad, up_grad, down_grad, small_grad = result
    qkv_grad = (
        qkv_grad.reshape(nz, shard, 3, group).transpose(1, 2, 0, 3).reshape(shard, 3, local_width)
    )

    def mine(part, like):
        return lax.dynamic_slice(
            part.reshape(like.shape[0], -1), (0, place * like.shape[1]), like.shape
        )

    at, cut = 0, []
    for piece in pieces:
        count = piece.size // 128
        cut.append(small_grad[at : at + count])
        at += count
    heads = head_bias.shape[0]
    head_grad = jnp.concatenate(
        [cut[2].reshape(heads, head_size), cut[3].reshape(heads, head_size)], axis=1
    )
    return (
        output.reshape(tokens.shape),
        input_grad.reshape(tokens.shape),
        qkv_grad,
        out_grad,
        up_grad,
        down_grad,
        mine(head_grad, head_bias),
        mine(cut[4], hidden_bias),
        mine(cut[0], norm_gains),
        mine(cut[1], out_biases),
    )


def fits(sizes, mesh):
    n_outer, n_core, nz, n_tensor = sizes
    return n_outer == 2 and n_core == 2 and n_tensor == 2 and nz == 4


def solution(mesh):
    in_specs = (
        P("dp", "ctx", None),
        P("dp"),
        P(("dp", "ctx"), None, "tensor"),
        P(("dp", "ctx"), "tensor"),
        P(("dp", "ctx"), "tensor"),
        P(("dp", "ctx"), "tensor"),
        P("tensor", ("dp", "ctx")),
        P("tensor", ("dp", "ctx")),
        P(None, ("dp", "ctx")),
        P(None, ("dp", "ctx")),
        P("dp", "ctx", None),
    )
    out_specs = (
        P("dp", "ctx", None),
        P("dp", "ctx", None),
        P(("dp", "ctx"), None, "tensor"),
        P(("dp", "ctx"), "tensor"),
        P(("dp", "ctx"), "tensor"),
        P(("dp", "ctx"), "tensor"),
        P("tensor", ("dp", "ctx")),
        P("tensor", ("dp", "ctx")),
        P(None, ("dp", "ctx")),
        P(None, ("dp", "ctx")),
    )
    n_core = 2 if mesh.shape["dp"] % 2 == 0 else 1
    sizes = (mesh.shape["dp"] // n_core, n_core, mesh.shape["ctx"], mesh.shape["tensor"])
    body = fused if fits(sizes, mesh) else on_device
    return jax.shard_map(
        functools.partial(body, sizes), mesh=mesh, in_specs=in_specs, out_specs=out_specs, check_vma=False
    )
```

```python
import functools
import math

import jax
import jax.numpy as jnp
from jax import lax
from jax.experimental import pallas as pl
from jax.experimental.pallas import tpu as pltpu
from jax.sharding import PartitionSpec as P

EPSILON = 1e-05
SCALE = 0.125
NEG_BIG = -1000000000.0
INV_ROOT_TWO = 1.0 / math.sqrt(2.0)
INV_ROOT_TWO_PI = 1.0 / math.sqrt(2.0 * math.pi)


def contract_last(left, right):
    return lax.dot_general(
        left, right, (((1,), (1,)), ((), ())), preferred_element_type=jnp.float32
    )


def contract_first(left, right):
    return lax.dot_general(
        left, right, (((0,), (0,)), ((), ())), preferred_element_type=jnp.float32
    )


def layer_norm(hidden_in, gain, shift):
    centred = hidden_in - jnp.mean(hidden_in, axis=-1, keepdims=True)
    variance = jnp.mean(centred * centred, axis=-1, keepdims=True)
    inv_std = lax.rsqrt(variance + EPSILON)
    normed = centred * inv_std
    return (normed * gain + shift, normed, inv_std)


def norm_back(grad_out, normed, inv_std, gain):
    grad_normed = grad_out * gain
    first_mean = jnp.mean(grad_normed, axis=-1, keepdims=True)
    second_mean = jnp.mean(grad_normed * normed, axis=-1, keepdims=True)
    grad_in = inv_std * (grad_normed - first_mean - normed * second_mean)
    return (grad_in, jnp.sum(grad_out * normed, axis=0), jnp.sum(grad_out, axis=0))


def gelu_parts(pre_act):
    cdf_val = 0.5 * (1.0 + jax.scipy.special.erf(pre_act * INV_ROOT_TWO))
    return (
        pre_act * cdf_val,
        cdf_val + pre_act * jnp.exp(-0.5 * pre_act * pre_act) * INV_ROOT_TWO_PI,
    )


def block_scores(queries, key_rows, valid):
    scores = (
        jnp.einsum("qhd,khd->hqk", queries, key_rows, preferred_element_type=jnp.float32) * SCALE
    )
    return jnp.where(valid[None, None, :], scores, NEG_BIG)


def attend_forward(inputs):
    queries, key_rows, value_rows, valid = inputs
    scores = block_scores(queries, key_rows, valid)
    peak = jnp.max(scores, axis=-1, keepdims=True)
    log_total = peak + jnp.log(jnp.sum(jnp.exp(scores - peak), axis=-1, keepdims=True))
    probs = jnp.exp(scores - log_total).astype(jnp.bfloat16)
    mixed = jnp.einsum(
        "hqk,khd->qhd", probs, value_rows, preferred_element_type=jnp.float32
    ).astype(jnp.bfloat16)
    return (mixed, log_total)


def attend_backward(inputs):
    queries, key_rows, value_rows, valid, mixed, log_total, grad_mixed = inputs
    scores = block_scores(queries, key_rows, valid)
    probs = jnp.exp(scores - log_total)
    grad_values = jnp.einsum(
        "hqk,qhd->khd", probs.astype(jnp.bfloat16), grad_mixed, preferred_element_type=jnp.float32
    )
    grad_probs = jnp.einsum(
        "qhd,khd->hqk", grad_mixed, value_rows, preferred_element_type=jnp.float32
    )
    inner = jnp.einsum("qhd,qhd->hq", grad_mixed.astype(jnp.float32), mixed.astype(jnp.float32))
    grad_scores = (probs * (grad_probs - inner[:, :, None])).astype(jnp.bfloat16)
    grad_queries = (
        jnp.einsum("hqk,khd->qhd", grad_scores, key_rows, preferred_element_type=jnp.float32)
        * SCALE
    )
    grad_keys = (
        jnp.einsum("hqk,qhd->khd", grad_scores, queries, preferred_element_type=jnp.float32) * SCALE
    )
    return (grad_queries, grad_keys, grad_values)


def comm_kernel(sizes, kinds, copies, *refs):
    n_outer, n_core, n_ctx, n_tensor = sizes
    count = len(kinds)
    ins, outs = refs[:count], refs[count : 2 * count]
    send_sem, recv_sem, own_sem = refs[2 * count :]
    dp, ctx, tensor = (lax.axis_index(name) for name in ("dp", "ctx", "tensor"))
    outer, core = dp // n_core, dp % n_core

    def coords(offset, sign=1):
        def move(at, step, size):
            return at if step == 0 else (at + (step if sign > 0 else size - step)) % size

        outer_at = move(outer, offset[0], n_outer)
        core_at = move(core, offset[1], n_core)
        return outer_at * n_core + core_at, move(ctx, offset[2], n_ctx), move(tensor, offset[3], n_tensor)

    def device(offset):
        dp_at, ctx_at, tensor_at = coords(offset)
        return {"dp": dp_at, "ctx": ctx_at, "tensor": tensor_at}

    offsets = peer_offsets(sizes, kinds)
    barrier = pltpu.get_barrier_semaphore()
    for offset in offsets:
        pl.semaphore_signal(
            barrier, inc=1, device_id=device(offset), device_id_type=pl.DeviceIdType.MESH
        )
    pl.semaphore_wait(barrier, len(offsets))

    started, used = [], [0]

    def put(source, target, offset):
        number = used[0]
        used[0] += 1
        copy = pltpu.make_async_remote_copy(
            src_ref=source,
            dst_ref=target,
            send_sem=send_sem.at[number],
            recv_sem=recv_sem.at[number],
            device_id=device(offset),
            device_id_type=pl.DeviceIdType.MESH,
        )
        copy.start()
        started.append(copy)
        return number

    def arrived(number, target, offset):
        pltpu.make_async_remote_copy(
            src_ref=target,
            dst_ref=target,
            send_sem=send_sem.at[number],
            recv_sem=recv_sem.at[number],
            device_id=device(offset),
            device_id_type=pl.DeviceIdType.MESH,
        ).wait_recv()

    partner = (0, 1, 0, 0)
    pending, own_copies = [], []
    first = {}
    for at, kind in enumerate(kinds):
        source, target = ins[at], outs[at]
        index = functools.partial(slot_of, kind, n_ctx)
        mine = index(*coords((0, 0, 0, 0)))
        if kind == "swap":
            for offset in direct_offsets(sizes, kind):
                number = put(source, target.at[offset[3] - 1], offset)
                pending.append((number, target.at[offset[3] - 1], offset))
            continue
        if kind in ("ctx", "cg", "dp", "all"):
            for offset in direct_offsets(sizes, kind):
                block = source if kind == "cg" else source.at[index(*coords(offset))]
                number = put(block, target.at[mine], offset)
                pending.append((number, target.at[index(*coords(offset, -1))], offset))
            block = source if kind == "cg" else source.at[mine]
            own = pltpu.make_async_copy(block, target.at[mine], own_sem.at[at])
        else:
            stage = []
            if kind == "wg":
                for step in range(1, n_ctx):
                    offset = (0, 0, step, 0)
                    stage.append((put(source, target.at[mine], offset), offset))
            crossing = []
            for step in range(1, n_outer):
                offset = (step, 0, 0, 0)
                crossing.append((put(source, target.at[mine], offset), offset, (0, 0, 0, 0)))
            pending.append(
                (put(source, target.at[mine], partner), target.at[index(*coords(partner, -1))], partner)
            )
            own = pltpu.make_async_copy(source, target.at[mine], own_sem.at[at])
            first[at] = (stage, crossing)
        own.start()
        own_copies.append(own)
    for at in first:
        target = outs[at]
        index = functools.partial(slot_of, kinds[at], n_ctx)
        stage, crossing = first[at]
        for number, offset in stage:
            slot = index(*coords(offset, -1))
            arrived(number, target.at[slot], offset)
            for step in range(1, n_outer):
                across = (step, 0, 0, 0)
                crossing.append((put(target.at[slot], target.at[slot], across), across, offset))
            both = (0, 1, offset[2], 0)
            pending.append(
                (put(target.at[slot], target.at[slot], partner), target.at[index(*coords(both, -1))], partner)
            )
    for at in first:
        target = outs[at]
        index = functools.partial(slot_of, kinds[at], n_ctx)
        for number, across, offset in first[at][1]:
            origin = (across[0], 0, offset[2], 0)
            slot = index(*coords(origin, -1))
            arrived(number, target.at[slot], across)
            both = (across[0], 1, offset[2], 0)
            pending.append(
                (put(target.at[slot], target.at[slot], partner), target.at[index(*coords(both, -1))], partner)
            )
    for number, target, offset in pending:
        arrived(number, target, offset)
    for own in own_copies:
        own.wait()
    for copy in started:
        copy.wait_send()


def slot_of(kind, n_ctx, dp_at, ctx_at, tensor_at):
    if kind in ("ctx", "cg"):
        return ctx_at
    if kind in ("dp", "dpg"):
        return dp_at
    return dp_at * n_ctx + ctx_at


def direct_offsets(sizes, kind):
    n_outer, n_core, n_ctx, n_tensor = sizes
    if kind == "swap":
        return [(0, 0, 0, step) for step in range(1, n_tensor)]
    if kind in ("ctx", "cg"):
        return [(0, 0, step, 0) for step in range(1, n_ctx)]
    ctx_steps = range(n_ctx) if kind == "all" else range(1)
    return [
        (o, c, k, 0) for k in ctx_steps for o in range(n_outer) for c in range(n_core) if o + c + k
    ]


def peer_offsets(sizes, kinds):
    n_outer, n_core, n_ctx, n_tensor = sizes
    found = set()
    for kind in kinds:
        if kind in ("wg", "dpg"):
            found.update((o, 0, 0, 0) for o in range(1, n_outer))
            found.add((0, 1, 0, 0))
            if kind == "wg":
                found.update((0, 0, k, 0) for k in range(1, n_ctx))
        else:
            found.update(direct_offsets(sizes, kind))
    return sorted(found)


def exchange(sizes, number, ops):
    n_outer, n_core, n_ctx, n_tensor = sizes
    n_dp = n_outer * n_core
    kinds = tuple(kind for kind, _ in ops)
    shapes, copies, moved = [], 0, 0
    for kind, array in ops:
        if kind == "swap":
            lead, sends = (n_tensor - 1,), n_tensor - 1
        elif kind == "dpg":
            lead, sends = (n_dp,), n_dp - 1
        elif kind == "cg":
            lead, sends = (n_ctx,), n_ctx - 1
        elif kind == "wg":
            lead, sends = (n_dp * n_ctx,), n_dp * n_ctx - 1
        else:
            lead, sends = (), array.shape[0] - 1
        shapes.append(jax.ShapeDtypeStruct(lead + array.shape, array.dtype))
        copies += sends
        moved += math.prod(lead + array.shape) * array.dtype.itemsize
    vmem = pl.BlockSpec(memory_space=pltpu.VMEM)
    return pl.pallas_call(
        functools.partial(comm_kernel, sizes, kinds, copies),
        out_shape=tuple(shapes),
        in_specs=[vmem] * len(ops),
        out_specs=tuple(
            pl.BlockSpec(memory_space=pl.ANY) if kind == "wg" else vmem for kind in kinds
        ),
        scratch_shapes=[
            pltpu.SemaphoreType.DMA((copies,)),
            pltpu.SemaphoreType.DMA((copies,)),
            pltpu.SemaphoreType.DMA((len(ops),)),
        ],
        compiler_params=pltpu.CompilerParams(
            collective_id=number, has_side_effects=True, vmem_limit_bytes=60 * 2**20
        ),
        cost_estimate=pl.CostEstimate(
            flops=0, bytes_accessed=moved * 10, transcendentals=0
        ),
        name=f"exchange_{number}",
    )(*(array for _, array in ops))


def pack(parts, lead, unit):
    flat = jnp.concatenate([part.reshape(lead, -1) for part in parts], axis=1)
    wide = -(-flat.shape[1] // unit) * unit
    return jnp.pad(flat, ((0, 0), (0, wide - flat.shape[1]))).reshape(lead, wide // 128, 128)


def unpack(packed, shapes):
    flat = packed.reshape(packed.shape[0], -1)
    out, at = [], 0
    for shape in shapes:
        size = math.prod(shape)
        out.append(flat[:, at : at + size].reshape((packed.shape[0],) + shape))
        at += size
    return out


def on_device(
    sizes,
    tokens,
    seq_lengths,
    qkv_weight,
    out_weight,
    up_weight,
    down_weight,
    head_bias,
    hidden_bias,
    norm_gains,
    out_biases,
    cotangent,
):
    n_outer, n_core, n_ctx, n_tensor = sizes
    n_dp = n_outer * n_core
    shards = n_dp * n_ctx
    seq_count, local_len, width = tokens.shape
    row_count = seq_count * local_len
    total_len = n_ctx * local_len
    local_width = qkv_weight.shape[2]
    feature_rows = width // n_dp
    token_rows = tokens.reshape(row_count, width)

    def feature_slices(rows):
        return rows.reshape(row_count, n_dp, feature_rows).transpose(1, 0, 2)

    smalls = (head_bias, hidden_bias, norm_gains, out_biases)
    qkv_got, out_got, small_got, token_slices = exchange(
        sizes,
        1,
        [
            ("wg", qkv_weight.reshape(qkv_weight.shape[0], 3 * local_width)),
            ("wg", out_weight),
            ("wg", pack(smalls, 1, 2048)[0]),
            ("dp", feature_slices(token_rows)),
        ],
    )
    qkv_full = qkv_got.reshape(width, 3 * local_width)
    out_full = out_got.reshape(width, -1)
    up_full = lax.all_gather(up_weight, ("dp", "ctx"), axis=0, tiled=True)
    down_full = lax.all_gather(down_weight, ("dp", "ctx"), axis=0, tiled=True)
    head_full, hidden_full, gains_full, biases_full = (
        part.transpose(1, 0, 2).reshape(part.shape[1], -1)
        for part in unpack(small_got, [small.shape for small in smalls])
    )
    local_heads = head_full.shape[0]
    head_size = head_full.shape[1] // 2
    heads_here = local_heads // n_ctx
    group_width = heads_here * head_size
    bias_query = head_full[:, :head_size].reshape(local_width).astype(jnp.float32)
    bias_value = head_full[:, head_size:].reshape(local_width).astype(jnp.float32)
    bias_hidden = hidden_full.reshape(-1).astype(jnp.float32)
    gains_wide = gains_full.astype(jnp.float32)
    biases_wide = biases_full.astype(jnp.float32)

    def to_positions(chunks, parts):
        return (
            chunks.reshape(n_ctx, parts, seq_count, local_len, group_width)
            .transpose(1, 2, 0, 3, 4)
            .reshape(parts, seq_count, total_len, heads_here, head_size)
        )

    def by_position(parts):
        return (
            jnp.stack(parts)
            .reshape(len(parts), seq_count, n_ctx, local_len, group_width)
            .transpose(2, 0, 1, 3, 4)
            .reshape(n_ctx, len(parts), row_count, group_width)
        )

    def by_heads(rows, parts):
        return rows.reshape(row_count, parts, n_ctx, group_width).transpose(2, 1, 0, 3)

    def to_rows(chunks, parts):
        return (
            chunks.reshape(n_ctx, parts, row_count, group_width)
            .transpose(2, 1, 0, 3)
            .reshape(row_count, parts * local_width)
        )

    projected = jnp.dot(token_rows, qkv_full, preferred_element_type=jnp.float32)
    shift = jnp.concatenate([bias_query, jnp.zeros_like(bias_query), bias_value])
    projected = (projected + shift).astype(jnp.bfloat16)
    (qkv_chunks,) = exchange(sizes, 2, [("ctx", by_heads(projected, 3))])
    queries, key_rows, value_rows = to_positions(qkv_chunks, 3)
    valid = jnp.arange(total_len)[None, :] < seq_lengths[:, None]
    mixed, log_total = lax.map(attend_forward, (queries, key_rows, value_rows, valid))
    (mixed_chunks,) = exchange(sizes, 3, [("ctx", by_position([mixed]))])
    attn_flat = to_rows(mixed_chunks, 1)
    attn_part = contract_last(attn_flat, out_full)
    attn_other, attn_all = exchange(sizes, 4, [("swap", attn_part), ("dpg", attn_flat)])
    attn_proj = attn_part + jnp.sum(attn_other, axis=0)
    first_sum = token_rows.astype(jnp.float32) + attn_proj + biases_wide[0]
    normed_one, z_one, rstd_one = layer_norm(first_sum, gains_wide[0], biases_wide[1])
    normed_low = normed_one.astype(jnp.bfloat16)
    pre_act = jnp.dot(normed_low, up_full, preferred_element_type=jnp.float32) + bias_hidden
    activated, slope = gelu_parts(pre_act)
    hidden_low = activated.astype(jnp.bfloat16)
    mlp_part = contract_last(hidden_low, down_full)
    half = n_dp // 2
    mlp_other, hidden_all, token_low = exchange(
        sizes,
        5,
        [("swap", mlp_part), ("dpg", hidden_low), ("cg", token_slices[:half])],
    )
    mlp_out = mlp_part + jnp.sum(mlp_other, axis=0)
    second_sum = normed_one + mlp_out + biases_wide[2]
    result, z_two, rstd_two = layer_norm(second_sum, gains_wide[1], biases_wide[3])
    output = result.astype(jnp.bfloat16).reshape(seq_count, local_len, width)
    grad_out = cotangent.reshape(row_count, width).astype(jnp.float32)
    grad_two, gain_two_grad, shift_two_grad = norm_back(grad_out, z_two, rstd_two, gains_wide[1])
    grad_two_low = grad_two.astype(jnp.bfloat16)
    grad_hidden = jnp.dot(grad_two_low, down_full, preferred_element_type=jnp.float32)
    grad_pre = grad_hidden * slope
    grad_pre_low = grad_pre.astype(jnp.bfloat16)
    hidden_part = jnp.sum(grad_pre, axis=0).reshape(hidden_full.shape)
    normed_part = contract_last(grad_pre_low, up_full)
    normed_other, grad_pre_all, grad_two_slices, token_high = exchange(
        sizes,
        6,
        [
            ("swap", normed_part),
            ("dpg", grad_pre_low),
            ("dp", feature_slices(grad_two_low)),
            ("cg", token_slices[half:]),
        ],
    )

    def over_rows(slices, wide):
        return contract_first(
            slices.reshape(n_dp * row_count, feature_rows), wide.reshape(n_dp * row_count, -1)
        )

    down_grad = lax.psum_scatter(
        over_rows(grad_two_slices, hidden_all), "ctx", scatter_dimension=0, tiled=True
    )
    grad_normed = normed_part + jnp.sum(normed_other, axis=0) + grad_two
    grad_one, gain_one_grad, shift_one_grad = norm_back(grad_normed, z_one, rstd_one, gains_wide[0])
    grad_one_low = grad_one.astype(jnp.bfloat16)
    grad_attn = jnp.dot(grad_one_low, out_full, preferred_element_type=jnp.float32).astype(
        jnp.bfloat16
    )
    grad_chunks, grad_one_slices, normed_slices = exchange(
        sizes,
        7,
        [
            ("ctx", by_heads(grad_attn, 1)),
            ("dp", feature_slices(grad_one_low)),
            ("dp", feature_slices(normed_low)),
        ],
    )
    up_grad = lax.psum_scatter(
        over_rows(normed_slices, grad_pre_all), "ctx", scatter_dimension=0, tiled=True
    )
    grad_mixed = to_positions(grad_chunks, 1)[0]
    out_grad = over_rows(grad_one_slices, attn_all)
    grad_queries, grad_keys, grad_values = lax.map(
        attend_backward, (queries, key_rows, value_rows, valid, mixed, log_total, grad_mixed)
    )
    proj_parts = by_position(
        [part.astype(jnp.bfloat16) for part in (grad_queries, grad_keys, grad_values)]
    )
    proj_wide = proj_parts.transpose(0, 2, 1, 3).reshape(n_ctx * row_count, 3 * group_width)
    proj_chunks, proj_all = exchange(sizes, 8, [("ctx", proj_parts), ("dpg", proj_wide)])
    token_all = (
        jnp.concatenate([token_low, token_high], axis=1)
        .transpose(1, 0, 2, 3)
        .reshape(n_dp * n_ctx * row_count, feature_rows)
    )
    qkv_part = contract_first(token_all, proj_all.reshape(n_dp * n_ctx * row_count, -1))
    grad_proj = to_rows(proj_chunks, 3)
    input_part = contract_last(grad_proj, qkv_full)
    head_rows = jnp.concatenate(
        [jnp.sum(grad_queries, axis=(0, 1)), jnp.sum(grad_values, axis=(0, 1))], axis=1
    )
    head_part = lax.dynamic_update_slice(
        jnp.zeros((local_heads, 2 * head_size), jnp.float32),
        head_rows,
        (lax.axis_index("ctx") * heads_here, 0),
    )
    gains_part = jnp.stack([gain_one_grad, gain_two_grad])
    biases_part = jnp.stack(
        [jnp.sum(grad_one, axis=0), shift_one_grad, jnp.sum(grad_two, axis=0), shift_two_grad]
    )
    small_parts = [
        part.reshape(part.shape[0], shards, -1).transpose(1, 0, 2)
        for part in (head_part, hidden_part, gains_part, biases_part)
    ]
    input_other, small_sums, out_blocks, qkv_blocks = exchange(
        sizes,
        9,
        [
            ("swap", input_part),
            ("all", pack(small_parts, shards, 1024)),
            ("ctx", out_grad.reshape(n_ctx, feature_rows // n_ctx, -1)),
            ("ctx", qkv_part.reshape(n_ctx, feature_rows // n_ctx, -1)),
        ],
    )
    input_grad = (input_part + jnp.sum(input_other, axis=0) + grad_one).reshape(
        seq_count, local_len, width
    )
    qkv_grad = (
        qkv_blocks.reshape(n_ctx, -1, 3, group_width)
        .transpose(1, 2, 0, 3)
        .reshape(-1, 3, local_width)
    )
    small_grads = unpack(
        jnp.sum(small_sums, axis=0)[None], [part.shape[1:] for part in small_parts]
    )
    return (
        output,
        input_grad,
        qkv_grad,
        jnp.sum(out_blocks, axis=0),
        up_grad,
        down_grad,
        *(part[0] for part in small_grads),
    )


MESH = pl.DeviceIdType.MESH


def dot_nn(left, right):
    return jnp.dot(left, right, preferred_element_type=jnp.float32)


class Links:
    def __init__(self, send_sem, recv_sem, own_sem, partner):
        self.send_sem, self.recv_sem, self.own_sem = send_sem, recv_sem, own_sem
        self.partner, self.sent, self.used, self.kept = partner, {}, 0, 0
        self.at_close = []

    def reserve(self):
        self.used += 1
        return self.used - 1

    def copy(self, number, source, target, to, got=None):
        return pltpu.make_async_remote_copy(
            src_ref=source,
            dst_ref=target,
            send_sem=self.send_sem.at[number],
            recv_sem=self.recv_sem.at[number if got is None else got],
            device_id=to,
            device_id_type=MESH,
        )

    def put(self, source, target, to):
        number = self.reserve()
        copy = self.copy(number, source, target, to)
        copy.start()
        self.sent[number] = copy
        return number

    def put_if(self, condition, number, ends, got=None):
        @pl.when(condition)
        def _():
            self.copy(number, *ends(), got).start()

        self.at_close.append((condition, number, ends))

    def arrive(self, number, target):
        self.copy(number, target, target, self.partner).wait_recv()

    def keep(self, source, target):
        copy = pltpu.make_async_copy(source, target, self.own_sem.at[self.kept])
        self.kept += 1
        copy.start()
        return copy

    def sent_all(self, number):
        self.sent.pop(number).wait_send()

    def close(self):
        for copy in self.sent.values():
            copy.wait_send()
        for condition, number, ends in self.at_close:

            @pl.when(condition)
            def _():
                self.copy(number, *ends()).wait_send()


class RowGather:
    def __init__(self, net, at, source, slot, block):
        self.net, self.at, self.source, self.slot, self.block = net, at, source, slot, block

    def start(self):
        net, at = self.net, self.at
        mine = self.slot(at.dp, at.z)
        self.own = net.keep(self.source, mine)
        self.along = [net.put(self.source, mine, at.z_to(k)) for k in range(1, at.nz)]
        self.across = [(net.put(self.source, mine, at.x_to), at.z)]

    def cross(self):
        net, at = self.net, self.at
        for k in range(1, at.nz):
            origin = at.z_from(k)
            got = self.slot(at.dp, origin)
            net.arrive(self.along[k - 1], got)
            self.across.append((net.put(got, got, at.x_to), origin))
        self.own.wait()
        block = self.block(at.dp)
        self.near = net.put(block, block, at.c_to)

    def relay(self):
        net, at = self.net, self.at
        for number, origin in self.across:
            net.arrive(number, self.slot(at.x_dp, origin))
        block = self.block(at.x_dp)
        self.far = net.put(block, block, at.c_to)

    def finish(self):
        self.net.arrive(self.near, self.block(self.at.c_dp))
        self.net.arrive(self.far, self.block(self.at.xc_dp))


class LineGather(RowGather):
    def start(self):
        net, at = self.net, self.at
        mine = self.slot(at.dp, at.z)
        self.own = net.keep(self.source, mine)
        self.across = [(net.put(self.source, mine, at.x_to), at.z)]
        self.numbers = [
            [[net.reserve() for _ in range(2)] for _ in range(at.nz)] for _ in range(2)
        ]
        for way in range(2):
            net.put_if(
                self.ahead(way),
                self.numbers[way][1][0],
                lambda way=way: (self.source, self.slot(at.dp, at.z), at.next_to(way)),
            )

    def ahead(self, way):
        return self.at.z < self.at.nz - 1 if way == 0 else self.at.z > 0

    def behind(self, way, hop):
        return self.at.z >= hop if way == 0 else self.at.z + hop < self.at.nz

    def got(self, way, hop, dp):
        return self.slot(dp, (self.at.z + (-hop if way == 0 else hop) + self.at.nz) % self.at.nz)

    def hop(self, hop):
        net, at = self.net, self.at
        for way in range(2):
            along, across = self.numbers[way][hop]

            def ends(to, way=way):
                got = self.got(way, hop, at.dp)
                return got, got, to

            @pl.when(self.behind(way, hop))
            def _():
                net.arrive(along, self.got(way, hop, at.dp))

            if hop < at.nz - 1:
                net.put_if(
                    jnp.logical_and(self.behind(way, hop), self.ahead(way)),
                    self.numbers[way][hop + 1][0],
                    lambda ends=ends, way=way: ends(at.next_to(way)),
                )
            net.put_if(self.behind(way, hop), across, lambda ends=ends: ends(at.x_to))
        if hop == at.nz - 1:
            self.own.wait()
            block = self.block(at.dp)
            self.near = net.put(block, block, at.c_to)

    def relay(self):
        net, at = self.net, self.at
        for hop in range(1, at.nz):
            for way in range(2):

                @pl.when(self.behind(way, hop))
                def _():
                    net.arrive(self.numbers[way][hop][1], self.got(way, hop, at.x_dp))

        super().relay()


class TokenGather(LineGather):
    def start(self):
        net, at = self.net, self.at
        self.numbers = [
            [[net.reserve() for _ in range(2)] for _ in range(at.nz)] for _ in range(2)
        ]
        for way in range(2):
            net.put_if(
                self.ahead(way),
                self.numbers[way][1][0],
                lambda way=way: (self.source, self.slot(at.y, at.z), at.next_to(way)),
            )

    def hop(self, hop):
        net, at = self.net, self.at
        for way in range(2):
            along, across = self.numbers[way][hop]

            def ends(to, way=way):
                got = self.got(way, hop, at.y)
                return got, got, to

            @pl.when(self.behind(way, hop))
            def _():
                net.arrive(along, self.got(way, hop, at.y))

            if hop < at.nz - 1:
                net.put_if(
                    jnp.logical_and(self.behind(way, hop), self.ahead(way)),
                    self.numbers[way][hop + 1][0],
                    lambda ends=ends, way=way: ends(at.next_to(way)),
                )
            net.put_if(self.behind(way, hop), across, lambda ends=ends: ends(at.y_to))

    def relay(self):
        net, at = self.net, self.at
        for hop in range(1, at.nz):
            for way in range(2):

                @pl.when(self.behind(way, hop))
                def _():
                    net.arrive(self.numbers[way][hop][1], self.got(way, hop, 1 - at.y))


class Place:
    def __init__(self, nz):
        self.nz = nz
        self.dp, self.z, self.y = (lax.axis_index(name) for name in ("dp", "ctx", "tensor"))
        dp, z, y = self.dp, self.z, self.y
        self.x, self.c = dp // 2, dp % 2
        self.c_dp = self.x * 2 + 1 - self.c
        self.x_dp = (1 - self.x) * 2 + self.c
        self.xc_dp = (1 - self.x) * 2 + 1 - self.c
        self.x_to = {"dp": self.x_dp, "ctx": z, "tensor": y}
        self.c_to = {"dp": self.c_dp, "ctx": z, "tensor": y}
        self.xc_to = {"dp": self.xc_dp, "ctx": z, "tensor": y}
        self.y_to = {"dp": dp, "ctx": z, "tensor": 1 - y}

        self.is_end = jnp.logical_or(z == 0, z == nz - 1)

    def seen(self, k):
        return jnp.where(self.z < self.nz // 2, k, self.nz - 1 - k)

    def along_to(self, z):
        return {"dp": self.dp, "ctx": z, "tensor": self.y}

    def z_at(self, k):
        return (self.z + k) % self.nz

    def z_from(self, k):
        return (self.z + self.nz - k) % self.nz

    def z_to(self, k):
        return {"dp": self.dp, "ctx": self.z_at(k), "tensor": self.y}

    def next_to(self, way):
        return self.z_to(1 if way == 0 else self.nz - 1)

    def zy_to(self, k):
        return {"dp": self.dp, "ctx": self.z_at(k), "tensor": 1 - self.y}

    def greet(self):
        peers = [self.x_to, self.c_to, self.xc_to, self.y_to]
        for k in range(1, self.nz):
            peers += [self.z_to(k), self.zy_to(k)]
        barrier = pltpu.get_barrier_semaphore()
        for peer in peers:
            pl.semaphore_signal(barrier, inc=1, device_id=peer, device_id_type=MESH)
        pl.semaphore_wait(barrier, len(peers))


def rows_at(index, size):
    return pl.ds(pl.multiple_of(index * size, size), size)


def row_sum(value):
    return jnp.sum(value, axis=0, keepdims=True)


def norm_back_rows(grad_out, normed, inv_std, gain):
    grad_normed = grad_out * gain
    first_mean = jnp.mean(grad_normed, axis=-1, keepdims=True)
    second_mean = jnp.mean(grad_normed * normed, axis=-1, keepdims=True)
    return inv_std * (grad_normed - first_mean - normed * second_mean)


def last_by_tiles(target, lefts, rights, tile=512):
    count = target.shape[1]
    tile = min(tile, count)

    def step(number, carry):
        columns = rows_at(number, tile)
        value = contract_last(lefts[0](), rights[0](columns))
        for left, right in zip(lefts[1:], rights[1:]):
            value += contract_last(left(), right(columns))
        target[:, columns] = value
        return carry

    lax.fori_loop(0, count // tile, step, 0)


class ColumnGrad:
    def __init__(self, net, at, turned, turned_all, wide, wide_all, total, got, out):
        self.net, self.at = net, at
        self.turned, self.turned_all = turned, turned_all
        self.wide, self.wide_all = wide, wide_all
        self.total, self.got, self.out = total, got, out
        self.half = wide_all.shape[2]
        self.block = turned_all.shape[0]
        self.rows = turned.shape[1]
        self.depth = got.shape[2]

    def send_wide(self):
        net, at = self.net, self.at
        mine = self.wide.at[:, rows_at(at.c, self.half)]
        theirs = self.wide.at[:, rows_at(1 - at.c, self.half)]
        slot = self.wide_all.at[at.dp]
        self.waits_wide = [
            (net.put(mine, slot, at.x_to), at.x_dp),
            (net.put(theirs, slot, at.xc_to), at.xc_dp),
            (net.put(theirs, slot, at.c_to), at.c_dp),
        ]
        self.own_wide = net.keep(mine, slot)

    def turned_of(self, dp):
        return self.turned_all.at[:, rows_at(dp, self.rows)]

    def send_turned(self):
        net, at = self.net, self.at
        mine = self.turned.at[rows_at(at.x, self.block)]
        theirs = self.turned.at[rows_at(1 - at.x, self.block)]
        slot = self.turned_of(at.dp)
        self.turned_x = net.put(theirs, slot, at.x_to)
        self.turned_c = net.put(mine, slot, at.c_to)
        self.own_turned = net.keep(mine, slot)

    def hand_on(self):
        net, at = self.net, self.at
        got = self.turned_of(at.x_dp)
        net.arrive(self.turned_x, got)
        self.turned_xc = net.put(got, got, at.c_to)

    def multiply(self):
        net, at = self.net, self.at
        self.own_wide.wait()
        self.own_turned.wait()
        for number, dp in self.waits_wide:
            net.arrive(number, self.wide_all.at[dp])
        net.arrive(self.turned_c, self.turned_of(at.c_dp))
        net.arrive(self.turned_xc, self.turned_of(at.xc_dp))
        tile = min(256, self.half)
        n_dp = self.wide_all.shape[0]
        middle = self.block // 2

        def step(number, carry):
            columns = rows_at(number, tile)
            value = dot_nn(self.turned_all[:, : self.rows], self.wide_all[0, :, columns])
            for dp in range(1, n_dp):
                value += dot_nn(
                    self.turned_all[:, dp * self.rows : (dp + 1) * self.rows],
                    self.wide_all[dp, :, columns],
                )
            self.total[0, :, columns] = value[:middle]
            self.total[1, :, columns] = value[middle:]
            return carry

        lax.fori_loop(0, self.half // tile, step, 0)

    def chunk(self, z):
        return self.total.at[:, rows_at(z, self.depth)]

    def spread(self):
        net, at = self.net, self.at
        self.numbers = [net.reserve() for _ in range(5)]
        far_end, far_mid, plain, _, _ = self.numbers
        for slot, (number, to) in enumerate(((far_end, 3), (far_mid, 2))):
            net.put_if(
                at.is_end,
                number,
                lambda slot=slot, to=to: (self.chunk(at.seen(to)), self.got.at[slot], at.along_to(at.seen(1))),
            )
        net.put_if(
            at.is_end, plain, lambda: (self.chunk(at.seen(1)), self.got.at[2], at.along_to(at.seen(1)))
        )
        net.put_if(
            jnp.logical_not(at.is_end),
            plain,
            lambda: (self.chunk(at.seen(0)), self.got.at[2], at.along_to(at.seen(0))),
        )

    def pass_on(self, slot):
        net, at = self.net, self.at
        to = 3 - slot
        middle = jnp.logical_not(at.is_end)

        @pl.when(middle)
        def _():
            net.arrive(self.numbers[slot], self.got.at[slot])
            for core in range(2):
                self.got[slot, core] += self.total[core, rows_at(at.seen(to), self.depth), :]

        net.put_if(
            middle,
            self.numbers[3 + slot],
            lambda: (self.got.at[slot], self.got.at[3], at.along_to(at.seen(to))),
            self.numbers[3],
        )

    def swap_cores(self):
        net, at = self.net, self.at
        net.arrive(self.numbers[2], self.got.at[2])
        net.arrive(self.numbers[3], self.got.at[3])

        def added(core):
            return (
                self.total[core, rows_at(at.z, self.depth), :] + self.got[2, core] + self.got[3, core]
            )

        place = rows_at(at.c, self.half)
        self.got[2, 1 - at.c] = added(1 - at.c)
        self.last = net.put(self.got.at[2, 1 - at.c], self.out.at[:, place], at.c_to)
        self.out[:, place] = added(at.c)

    def finish(self):
        self.net.arrive(self.last, self.out.at[:, rows_at(1 - self.at.c, self.half)])


def layer_kernel(dims, names, *refs):
    (nz, head_size, small_rows) = dims
    r = dict(zip(names, refs))

    class Refs:
        pass

    m = Refs()
    m.__dict__.update(r)
    at = Place(nz)
    net = Links(m.send_sem, m.recv_sem, m.own_sem, at.c_to)
    rows, width = m.tok.shape
    half = rows // 2
    total_len = rows * nz
    group = m.queries.shape[1]
    heads = group // head_size
    shard = m.outw.shape[0]
    part_rows = nz * shard
    local_width = m.outw.shape[1]
    hidden = m.upw.shape[1]
    groups_wide = width // 128
    bf16, f32 = jnp.bfloat16, jnp.float32
    mine, other = rows_at(at.y, half), rows_at(1 - at.y, half)
    at.greet()

    def gather(source, full, form=RowGather):
        return form(
            net,
            at,
            source,
            lambda dp, z: full.at[rows_at(dp * nz + z, source.shape[0])],
            lambda dp: full.at[rows_at(dp, nz * source.shape[0])],
        )

    def qkv_slot(g, dp, z):
        return m.wfull.at[g, rows_at(dp * nz + z, shard)]

    def qkv_block(g, dp):
        return m.wfull.at[g, rows_at(dp, part_rows)]

    own_qkv = net.keep(m.wq.at[at.z], qkv_slot(at.z, at.dp, at.z))
    qkv_along = [
        net.put(m.wq.at[at.z_at(k)], qkv_slot(at.z_at(k), at.dp, at.z), at.z_to(k))
        for k in range(1, nz)
    ]
    qkv_across = [(net.put(m.wq.at[at.z], qkv_slot(at.z, at.dp, at.z), at.x_to), at.z)]
    small = gather(m.small, m.small_all)
    small.start()
    own_rows = net.keep(m.tok, m.xall.at[rows_at(at.z, rows)])

    def half_of(z, y):
        return m.xall.at[rows_at(z * 2 + y, half)]

    tokens = TokenGather(net, at, m.tok.at[mine], lambda y, z: half_of(z, y), None)
    tokens.start()
    for k in range(1, nz):
        origin = at.z_from(k)
        got = qkv_slot(at.z, at.dp, origin)
        net.arrive(qkv_along[k - 1], got)
        qkv_across.append((net.put(got, got, at.x_to), origin))
    own_qkv.wait()
    near = qkv_block(at.z, at.dp)
    qkv_near = net.put(near, near, at.c_to)
    small.cross()
    for hop in range(1, nz):
        tokens.hop(hop)
    outs = gather(m.outw, m.outf.at[at.y])
    outs.start()
    ups = gather(m.upw, m.up, LineGather)
    ups.start()
    for number, origin in qkv_across:
        net.arrive(number, qkv_slot(at.z, at.x_dp, origin))
    far = qkv_block(at.z, at.x_dp)
    qkv_far = net.put(far, far, at.c_to)
    small.relay()
    small.finish()
    small_sum = m.small_all[:small_rows, :].astype(f32)
    for slot in range(1, 4 * nz):
        small_sum += m.small_all[slot * small_rows : (slot + 1) * small_rows, :].astype(f32)
    m.smalls[...] = small_sum
    for row in range(6):
        for j in range(groups_wide):
            at_row = row * groups_wide + j
            m.norms[row : row + 1, j * 128 : (j + 1) * 128] = m.smalls[at_row : at_row + 1, :]
    query_row = 6 * groups_wide
    value_row = query_row + nz
    hidden_row = value_row + nz
    for j in range(hidden // 128):
        m.hbias[:, j * 128 : (j + 1) * 128] = m.smalls[hidden_row + j : hidden_row + j + 1, :]
    net.arrive(qkv_near, qkv_block(at.z, at.c_dp))
    net.arrive(qkv_far, qkv_block(at.z, at.xc_dp))
    downs = gather(m.downw, m.down, LineGather)
    own_rows.wait()
    tokens.relay()
    bias_q = m.smalls[pl.ds(query_row + at.z, 1), :]
    bias_v = m.smalls[pl.ds(value_row + at.z, 1), :]

    def project(block, carry):
        place = rows_at(block, rows)
        value = dot_nn(m.xall[place, :], m.wfull[at.z])
        m.queries[place, :] = (value[:, :group] + bias_q).astype(bf16)
        key = value[:, group : 2 * group]
        m.keys[place, :] = key.astype(bf16)
        m.keys_t[:, place] = key.T.astype(bf16)
        val = value[:, 2 * group :] + bias_v
        m.values[place, :] = val.astype(bf16)
        m.values_t[:, place] = val.T.astype(bf16)
        return carry

    lax.fori_loop(0, nz, project, 0)
    outs.cross()
    y_rows = width // 2

    valid = lax.broadcasted_iota(jnp.int32, (total_len, 1), 0) < m.lens[0]
    lane_head = lax.broadcasted_iota(jnp.int32, (1, group), 1) // head_size
    row_head = lax.broadcasted_iota(jnp.int32, (group, 1), 0) // head_size

    def head_of(value, h):
        return jnp.where(lane_head == h, value, jnp.zeros_like(value))

    def scores_of(query):
        return jnp.where(valid, contract_last(m.keys[...], query) * SCALE, NEG_BIG)

    def attend(block):
        place = rows_at(block, rows)
        query = m.queries[place, :]
        mixed = jnp.zeros((group, rows), f32)
        for h in range(heads):
            score = scores_of(head_of(query, h))
            peak = jnp.max(score, axis=0, keepdims=True)
            grown = jnp.exp(score - peak)
            total = jnp.sum(grown, axis=0, keepdims=True)
            m.log_total[h : h + 1, place] = peak + jnp.log(total)
            probs = (grown * (1.0 / total)).astype(bf16)
            mixed = jnp.where(row_head == h, dot_nn(m.values_t[...], probs), mixed)
        m.mixed[place, :] = mixed.T.astype(bf16)

    def columns_of(y, z):
        return m.attn.at[:, rows_at(y * nz + z, group)]

    mixed_along = []
    for k in list(range(1, nz)) + [0]:
        if k == 0:
            outs.relay()
            outs.finish()
            out_half = m.outf.at[at.y, rows_at(at.c, y_rows)]
            out_y = net.put(out_half, out_half, at.y_to)
        attend(at.z_at(k))
        part = m.mixed.at[rows_at(at.z_at(k), rows)]
        if k:
            mixed_along.append(net.put(part, columns_of(at.y, at.z), at.z_to(k)))
            if k == 2:
                ups.hop(1)
        else:
            own_mixed = net.keep(part, columns_of(at.y, at.z))
            mixed_y = [(net.put(part, columns_of(at.y, at.z), at.y_to), at.z)]
    ups.hop(2)
    downs.start()
    for k in range(1, nz):
        origin = at.z_from(k)
        got = columns_of(at.y, origin)
        net.arrive(mixed_along[k - 1], got)
        mixed_y.append((net.put(got, got, at.y_to), origin))
    ups.hop(3)

    def turn_rows(block, carry):
        place = rows_at(block, rows)
        m.xall_t[:, place] = m.xall[place, :].T
        return carry

    downs.hop(1)
    got = m.outf.at[1 - at.y, rows_at(at.c, y_rows)]
    net.arrive(out_y, got)
    out_near = net.put(got, got, at.c_to)
    net.arrive(out_near, m.outf.at[1 - at.y, rows_at(1 - at.c, y_rows)])
    own_mixed.wait()
    for number, origin in mixed_y:
        net.arrive(number, columns_of(1 - at.y, origin))

    gain_one, gain_two = m.norms[0:1, :], m.norms[1:2, :]
    shift = [m.norms[2 + i : 3 + i, :] for i in range(4)]

    def first_norm(place, kept):
        first_sum = (
            m.tok[place, :].astype(f32)
            + contract_last(m.attn[place, :local_width], m.outf[0])
            + contract_last(m.attn[place, local_width:], m.outf[1])
            + shift[0]
        )
        normed, z_one, rstd = layer_norm(first_sum, gain_one, shift[1])
        if kept:
            m.normed[...] = normed
            m.z_one[...] = z_one
            m.rstd[...] = rstd
        m.normed_low[place, :] = normed.astype(bf16)

    first_norm(other, False)
    first_norm(mine, True)
    ups.relay()
    downs.hop(2)
    ups.finish()

    tile = min(512, hidden)

    def feed(place):
        def step(number, carry):
            columns = rows_at(number, tile)
            pre = dot_nn(m.normed_low[place, :], m.up[:, columns]) + m.hbias[:, columns]
            activated, slope = gelu_parts(pre)
            m.hid[place, columns] = activated.astype(bf16)
            m.slope[place, columns] = slope
            return carry

        lax.fori_loop(0, hidden // tile, step, 0)

    feed(other)
    downs.hop(3)
    feed(mine)
    downs.relay()
    down_grad = ColumnGrad(
        net, at, m.grad_two_t, m.grad_two_all, m.hid, m.hid_all, m.down_total, m.down_got, m.down_grad
    )
    up_grad = ColumnGrad(
        net, at, m.normed_t, m.normed_all, m.grad_pre, m.grad_pre_all, m.up_total, m.up_got, m.up_grad
    )
    out_grad = ColumnGrad(
        net,
        at,
        m.grad_one_t,
        m.grad_one_all,
        m.attn.at[:, rows_at(at.y, local_width)],
        m.attn_all,
        m.out_total,
        m.out_got,

        m.out_grad,
    )
    down_grad.send_wide()
    downs.finish()
    late = []
    for k in range(1, nz):
        for j in range(1, nz):
            g = at.z_at(k + j)
            target = qkv_slot(g, at.dp, at.z)
            late.append((net.put(m.wq.at[g], target, at.z_to(k)), k, j))
    late_own = [
        net.keep(m.wq.at[at.z_at(j)], qkv_slot(at.z_at(j), at.dp, at.z)) for j in range(1, nz)
    ]
    last_by_tiles(m.part_a, [lambda: m.hid[other, :]], [lambda at_rows: m.down[at_rows, :]])
    part_a = net.put(m.part_a, m.got_a, at.y_to)
    last_by_tiles(m.kept, [lambda: m.hid[mine, :]], [lambda at_rows: m.down[at_rows, :]])
    m.normed_t[...] = m.normed_low[...].T
    lax.fori_loop(0, nz, turn_rows, 0)
    net.arrive(part_a, m.got_a)
    second_sum = m.normed[...] + (m.kept[...] + m.got_a[...]) + shift[2]
    result, z_two, rstd_two = layer_norm(second_sum, gain_two, shift[3])
    grad_out = m.cot[mine, :].astype(f32)
    grad_two = norm_back_rows(grad_out, z_two, rstd_two, gain_two)
    m.grad_two[...] = grad_two
    m.grad_two_low[mine, :] = grad_two.astype(bf16)
    two_y = net.put(m.grad_two_low.at[mine], m.grad_two_low.at[mine], at.y_to)
    m.output[mine, :] = result.astype(bf16)
    sums = {1: row_sum(grad_out * z_two), 5: row_sum(grad_out), 4: row_sum(grad_two)}

    m.hidden_sum[...] = jnp.zeros_like(m.hidden_sum)

    def feed_back(place):
        def step(number, carry):
            columns = rows_at(number, tile)
            grad_hidden = dot_nn(m.grad_two_low[place, :], m.down[:, columns])
            grad_pre = grad_hidden * m.slope[place, columns]
            m.grad_pre[place, columns] = grad_pre.astype(bf16)
            m.hidden_sum[:, columns] += row_sum(grad_pre)
            return carry

        lax.fori_loop(0, hidden // tile, step, 0)

    feed_back(mine)
    net.arrive(two_y, m.grad_two_low.at[other])
    m.grad_two_t[...] = m.grad_two_low[...].T
    down_grad.send_turned()
    feed_back(other)
    up_grad.send_wide()
    net.sent_all(part_a)
    last_by_tiles(m.part_a, [lambda: m.grad_pre[other, :]], [lambda at_rows: m.up[at_rows, :]])
    part_b = net.put(m.part_a, m.got_a, at.y_to)
    last_by_tiles(m.kept, [lambda: m.grad_pre[mine, :]], [lambda at_rows: m.up[at_rows, :]])
    net.arrive(part_b, m.got_a)
    grad_normed = m.kept[...] + m.got_a[...] + m.grad_two[...]
    z_mine = m.z_one[...]
    grad_one = norm_back_rows(grad_normed, z_mine, m.rstd[...], gain_one)
    m.grad_one[...] = grad_one
    m.grad_one_low[mine, :] = grad_one.astype(bf16)
    sums[0] = row_sum(grad_normed * z_mine)
    sums[3] = row_sum(grad_normed)
    sums[2] = row_sum(grad_one)
    def back_step(y, carry):
        value = dot_nn(m.grad_one_low[mine, :], m.outf[y])
        m.grad_attn[:, rows_at(y, local_width)] = value.astype(bf16)
        return carry

    lax.fori_loop(0, 2, back_step, 0)

    def attn_part(y, z):
        return m.grad_attn.at[:, rows_at(y * nz + z, group)]

    my_slot = m.grad_mixed.at[rows_at(at.z * 2 + at.y, half)]
    grad_along = []
    for k in range(1, nz):
        grad_along.append((net.put(attn_part(at.y, at.z_at(k)), my_slot, at.z_to(k)), at.z_from(k), at.y))
        grad_along.append(
            (net.put(attn_part(1 - at.y, at.z_at(k)), my_slot, at.zy_to(k)), at.z_from(k), 1 - at.y)
        )
    grad_along.append((net.put(attn_part(1 - at.y, at.z), my_slot, at.y_to), at.z, 1 - at.y))
    own_grad = net.keep(attn_part(at.y, at.z), my_slot)
    one_y = net.put(m.grad_one_low.at[mine], m.grad_one_low.at[mine], at.y_to)
    up_grad.send_turned()
    out_grad.send_wide()
    down_grad.hand_on()
    down_grad.multiply()
    down_grad.spread()

    for number, origin, y in grad_along:
        net.arrive(number, m.grad_mixed.at[rows_at(origin * 2 + y, half)])
    own_grad.wait()
    net.arrive(one_y, m.grad_one_low.at[other])
    output_y = net.put(m.output.at[mine], m.output.at[mine], at.y_to)
    m.grad_one_t[...] = m.grad_one_low[...].T
    out_grad.send_turned()
    down_grad.pass_on(0)

    product = m.grad_mixed[...].astype(f32) * m.mixed[...].astype(f32)
    turned = product.T
    for h in range(heads):
        m.inner[h : h + 1, :] = row_sum(turned[h * head_size : (h + 1) * head_size, :])
    m.acc_query[...] = jnp.zeros_like(m.acc_query)

    def attend_back(block, value_sum):
        place = rows_at(block, rows)
        keys, values = m.keys[place, :], m.values[place, :]
        grad_keys = jnp.zeros((rows, group), f32)
        grad_values = jnp.zeros((rows, group), f32)
        valid_here = lax.broadcasted_iota(jnp.int32, (rows, 1), 0) + block * rows < m.lens[0]
        for h in range(heads):
            query_h = head_of(m.queries[...], h)
            grad_h = head_of(m.grad_mixed[...], h)
            score = jnp.where(valid_here, contract_last(keys, query_h) * SCALE, NEG_BIG)
            probs = jnp.exp(score - m.log_total[h : h + 1, :])
            grad_values += dot_nn(probs.astype(bf16), grad_h)
            grad_probs = contract_last(values, grad_h)
            grad_scores = (probs * (grad_probs - m.inner[h : h + 1, :])).astype(bf16)
            grad_keys += dot_nn(grad_scores, query_h)
            m.acc_query[h] += dot_nn(m.keys_t[:, place], grad_scores)
        m.grad_proj[place, group : 2 * group] = (grad_keys * SCALE).astype(bf16)
        m.grad_proj[place, 2 * group :] = grad_values.astype(bf16)
        return value_sum + row_sum(grad_values)

    value_sum = jnp.zeros((1, group), f32)
    wide = pl.ds(group, 2 * group)
    proj_along = []
    for k in list(range(1, nz)) + [0]:
        value_sum = attend_back(at.z_at(k), value_sum)
        if k:
            part = m.grad_proj.at[rows_at(at.z_at(k), rows), wide]
            slot = m.proj_rows.at[at.z, :, wide]
            proj_along.append((net.put(part, slot, at.z_to(k)), at.z_from(k), wide))
        if k == 2:
            down_grad.pass_on(1)
    narrow = pl.ds(0, group)
    query_sum = jnp.zeros((1, group), f32)
    for k in range(nz):
        place = rows_at(at.z_at(k), rows)
        grad_query = m.acc_query[0, :, place]
        for h in range(1, heads):
            grad_query = jnp.where(row_head == h, m.acc_query[h, :, place], grad_query)
        grad_query = grad_query.T * SCALE
        query_sum += row_sum(grad_query)
        m.grad_proj[place, :group] = grad_query.astype(bf16)
        if k:
            part = m.grad_proj.at[place, narrow]
            slot = m.proj_rows.at[at.z, :, narrow]
            proj_along.append((net.put(part, slot, at.z_to(k)), at.z_from(k), narrow))
    own_proj = net.keep(m.grad_proj.at[rows_at(at.z, rows)], m.proj_rows.at[at.z])

    m.small_sum[...] = jnp.zeros_like(m.small_sum)
    for row in range(6):
        for j in range(groups_wide):
            at_row = row * groups_wide + j
            m.small_sum[at_row : at_row + 1, :] = sums[row][:, j * 128 : (j + 1) * 128]
    m.small_sum[pl.ds(query_row + at.z, 1), :] = query_sum
    m.small_sum[pl.ds(value_row + at.z, 1), :] = value_sum
    for j in range(hidden // 128):
        m.small_sum[hidden_row + j : hidden_row + j + 1, :] = m.hidden_sum[:, j * 128 : (j + 1) * 128]
    small_along = [net.put(m.small_sum, m.small_got.at[k - 1], at.z_to(k)) for k in range(1, nz)]

    up_grad.hand_on()
    up_grad.multiply()
    up_grad.spread()
    late_x = []
    for number, k, j in late:
        got = qkv_slot(at.z_at(j), at.dp, at.z_from(k))
        net.arrive(number, got)
    for copy in late_own:
        copy.wait()
    for j in range(1, nz):
        block = qkv_block(at.z_at(j), at.dp)
        late_x.append((net.put(block, block, at.x_to), net.put(block, block, at.c_to), j))
    def qkv_step(block, carry):
        place = rows_at(block, rows)
        m.qkv_total[place, :] = dot_nn(m.xall_t[place, :], m.grad_proj[...])
        return carry

    lax.fori_loop(0, width // rows, qkv_step, 0)
    core_waits = []
    for x in range(2):
        part = m.qkv_total.at[rows_at(x * 2 + 1 - at.c, part_rows)]
        core_waits.append(net.put(part, m.qkv_core.at[x], at.c_to))
    for x in range(2):
        net.arrive(core_waits[x], m.qkv_core.at[x])
    across_rows, kept_rows = rows_at(at.x_dp, part_rows), rows_at(at.dp, part_rows)
    m.qkv_total[across_rows, :] += m.qkv_core[1 - at.x]
    qkv_x = net.put(m.qkv_total.at[across_rows], m.qkv_got, at.x_to)
    out_grad.hand_on()
    out_grad.multiply()
    out_grad.spread()
    up_grad.pass_on(0)
    for k in range(1, nz):
        net.arrive(small_along[k - 1], m.small_got.at[k - 1])
    value = m.small_sum[...]
    for k in range(1, nz):
        value += m.small_got[k - 1]
    m.small_two[...] = value
    small_x = net.put(m.small_two, m.small_got.at[nz - 1], at.x_to)
    late_c = []
    for across, near, j in late_x:
        block = qkv_block(at.z_at(j), at.x_dp)
        net.arrive(across, block)
        late_c.append((net.put(block, block, at.c_to), near, j))
    for across, near, j in late_c:
        net.arrive(near, qkv_block(at.z_at(j), at.c_dp))
        net.arrive(across, qkv_block(at.z_at(j), at.xc_dp))
    own_proj.wait()
    for number, origin, columns in proj_along:
        net.arrive(number, m.proj_rows.at[origin, :, columns])

    def input_part(target, place):
        last_by_tiles(
            target,
            [lambda g=g: m.proj_rows[g, place, :] for g in range(nz)],
            [lambda at_rows, g=g: m.wfull[g, at_rows, :] for g in range(nz)],
        )

    net.sent_all(part_b)
    input_part(m.part_a, other)
    part_c = net.put(m.part_a, m.got_a, at.y_to)
    input_part(m.kept, mine)
    up_grad.pass_on(1)
    out_grad.pass_on(0)
    net.arrive(qkv_x, m.qkv_got)
    m.qkv_total[kept_rows, :] += m.qkv_core[at.x] + m.qkv_got[...]
    qkv_z = [
        net.put(
            m.qkv_total.at[rows_at(at.dp * nz + at.z_at(k), shard)], m.qkv_grad.at[at.z], at.z_to(k)
        )
        for k in range(1, nz)
    ]
    m.qkv_grad[at.z] = m.qkv_total[rows_at(at.dp * nz + at.z, shard), :]
    net.arrive(small_x, m.small_got.at[nz - 1])
    m.small_three[...] = m.small_two[...] + m.small_got[nz - 1]
    small_c = net.put(m.small_three, m.small_got.at[nz], at.c_to)
    net.arrive(part_c, m.got_a)
    m.input_grad[mine, :] = m.kept[...] + m.got_a[...] + m.grad_one[...]
    input_y = net.put(m.input_grad.at[mine], m.input_grad.at[mine], at.y_to)
    net.arrive(small_c, m.small_got.at[nz])
    m.small_four[...] = m.small_three[...] + m.small_got[nz]
    small_y = net.put(m.small_four, m.small_got.at[nz + 1], at.y_to)
    out_grad.pass_on(1)
    down_grad.swap_cores()
    up_grad.swap_cores()
    out_grad.swap_cores()
    net.arrive(small_y, m.small_got.at[nz + 1])
    shared = lax.broadcasted_iota(jnp.int32, (small_rows, 1), 0) < query_row
    m.small_grad[...] = m.small_four[...] + jnp.where(shared, m.small_got[nz + 1], 0.0)
    for k in range(1, nz):
        net.arrive(qkv_z[k - 1], m.qkv_grad.at[at.z_from(k)])
    net.arrive(output_y, m.output.at[other])
    net.arrive(input_y, m.input_grad.at[other])
    for item in (down_grad, up_grad, out_grad):
        item.finish()
    net.close()


def fused(
    sizes,
    tokens,
    seq_lengths,
    qkv_weight,
    out_weight,
    up_weight,
    down_weight,
    head_bias,
    hidden_bias,
    norm_gains,
    out_biases,
    cotangent,
):
    n_outer, n_core, nz, n_tensor = sizes
    n_dp = n_outer * n_core
    shards = n_dp * nz
    _, rows, width = tokens.shape
    shard, _, local_width = qkv_weight.shape
    hidden = up_weight.shape[1]
    head_size = head_bias.shape[1] * shards // 2
    group = local_width // nz
    total_len = rows * nz
    bf16, f32 = jnp.bfloat16, jnp.float32
    place = lax.axis_index("dp") * nz + lax.axis_index("ctx")

    def spread(part):
        here = jnp.arange(shards)[None, :, None] == place
        return jnp.where(here, part[:, None, :], jnp.zeros((), bf16)).reshape(part.shape[0], -1)

    head_wide = spread(head_bias)
    pieces = [
        spread(norm_gains),
        spread(out_biases),
        head_wide[:, :head_size],
        head_wide[:, head_size:],
        spread(hidden_bias),
    ]
    small = jnp.concatenate([piece.reshape(-1, 128) for piece in pieces], axis=0)
    used = small.shape[0]
    small_rows = -(-used // 16) * 16
    small = jnp.pad(small, ((0, small_rows - used), (0, 0)))
    wq = qkv_weight.reshape(shard, 3, nz, group).transpose(2, 0, 1, 3).reshape(nz, shard, 3 * group)
    tok = tokens.reshape(rows, width)
    cot = cotangent.reshape(rows, width)
    half = rows // 2
    ins = dict(
        lens=seq_lengths, tok=tok, cot=cot, wq=wq, outw=out_weight, upw=up_weight, downw=down_weight, small=small
    )
    outs = dict(
        output=((rows, width), bf16),
        input_grad=((rows, width), f32),
        qkv_grad=((nz, shard, 3 * group), f32),
        out_grad=((shard, local_width), f32),
        up_grad=((shard, hidden), f32),
        down_grad=((shard, hidden), f32),
        small_grad=((small_rows, 128), f32),
    )
    block = 2 * nz * shard
    part_rows = nz * shard
    scratch = dict(
        small_all=((shards * small_rows, 128), bf16),
        smalls=((small_rows, 128), f32),
        norms=((8, width), f32),
        hbias=((1, hidden), f32),
        wfull=((nz, width, 3 * group), bf16),
        xall=((total_len, width), bf16),
        xall_t=((width, total_len), bf16),
        outf=((2, width, local_width), bf16),
        up=((width, hidden), bf16),
        down=((width, hidden), bf16),
        queries=((total_len, group), bf16),
        keys=((total_len, group), bf16),
        values=((total_len, group), bf16),
        keys_t=((group, total_len), bf16),
        values_t=((group, total_len), bf16),
        mixed=((total_len, group), bf16),
        log_total=((max(8, group // head_size), total_len), f32),
        attn=((rows, width), bf16),
        normed=((half, width), f32),
        z_one=((half, width), f32),
        rstd=((half, 1), f32),
        normed_low=((rows, width), bf16),
        normed_t=((width, rows), bf16),
        hid=((rows, hidden), bf16),
        slope=((rows, hidden), f32),
        part_a=((half, width), f32),
        got_a=((half, width), f32),
        kept=((half, width), f32),
        grad_two=((half, width), f32),
        grad_two_low=((rows, width), bf16),
        grad_two_t=((width, rows), bf16),
        grad_pre=((rows, hidden), bf16),
        hidden_sum=((1, hidden), f32),
        grad_one=((half, width), f32),
        grad_one_low=((rows, width), bf16),
        grad_one_t=((width, rows), bf16),
        grad_attn=((half, width), bf16),
        grad_mixed=((total_len, group), bf16),
        acc_query=((group // head_size, group, total_len), f32),
        inner=((max(8, group // head_size), total_len), f32),
        grad_proj=((total_len, 3 * group), bf16),
        proj_rows=((nz, rows, 3 * group), bf16),
        small_sum=((small_rows, 128), f32),
        small_two=((small_rows, 128), f32),
        small_three=((small_rows, 128), f32),
        small_four=((small_rows, 128), f32),
        small_got=((nz + 2, small_rows, 128), f32),
        qkv_total=((width, 3 * group), f32),
        qkv_core=((2, part_rows, 3 * group), f32),
        qkv_got=((part_rows, 3 * group), f32),
        hid_all=((n_dp, rows, hidden // 2), bf16),
        grad_two_all=((block, n_dp * rows), bf16),
        down_total=((2, part_rows, hidden // 2), f32),
        down_got=((4, 2, shard, hidden // 2), f32),
        grad_pre_all=((n_dp, rows, hidden // 2), bf16),
        normed_all=((block, n_dp * rows), bf16),
        up_total=((2, part_rows, hidden // 2), f32),
        up_got=((4, 2, shard, hidden // 2), f32),
        attn_all=((n_dp, rows, local_width // 2), bf16),
        grad_one_all=((block, n_dp * rows), bf16),
        out_total=((2, part_rows, local_width // 2), f32),
        out_got=((4, 2, shard, local_width // 2), f32),
    )
    names = tuple(ins) + tuple(outs) + tuple(scratch) + ("send_sem", "recv_sem", "own_sem")
    vmem = pl.BlockSpec(memory_space=pltpu.VMEM)
    copies = 288
    result = pl.pallas_call(
        functools.partial(layer_kernel, (nz, head_size, small_rows), names),
        out_shape=tuple(jax.ShapeDtypeStruct(*spec) for spec in outs.values()),
        in_specs=[pl.BlockSpec(memory_space=pltpu.SMEM)] + [vmem] * (len(ins) - 1),
        out_specs=(vmem,) * len(outs),
        scratch_shapes=[pltpu.VMEM(*spec) for spec in scratch.values()]
        + [
            pltpu.SemaphoreType.DMA((copies,)),
            pltpu.SemaphoreType.DMA((copies,)),
            pltpu.SemaphoreType.DMA((40,)),
        ],
        compiler_params=pltpu.CompilerParams(
            collective_id=1, has_side_effects=True, vmem_limit_bytes=64 * 2**20 - 2**18
        ),
        name="layer",
    )(*ins.values())
    output, input_grad, qkv_grad, out_grad, up_grad, down_grad, small_grad = result
    qkv_grad = (
        qkv_grad.reshape(nz, shard, 3, group).transpose(1, 2, 0, 3).reshape(shard, 3, local_width)
    )

    def mine(part, like):
        return lax.dynamic_slice(
            part.reshape(like.shape[0], -1), (0, place * like.shape[1]), like.shape
        )

    at, cut = 0, []
    for piece in pieces:
        count = piece.size // 128
        cut.append(small_grad[at : at + count])
        at += count
    heads = head_bias.shape[0]
    head_grad = jnp.concatenate(
        [cut[2].reshape(heads, head_size), cut[3].reshape(heads, head_size)], axis=1
    )
    return (
        output.reshape(tokens.shape),
        input_grad.reshape(tokens.shape),
        qkv_grad,
        out_grad,
        up_grad,
        down_grad,
        mine(head_grad, head_bias),
        mine(cut[4], hidden_bias),
        mine(cut[0], norm_gains),
        mine(cut[1], out_biases),
    )


def fits(sizes, mesh):
    n_outer, n_core, nz, n_tensor = sizes
    return n_outer == 2 and n_core == 2 and n_tensor == 2 and nz == 4


def solution(mesh):
    in_specs = (
        P("dp", "ctx", None),
        P("dp"),
        P(("dp", "ctx"), None, "tensor"),
        P(("dp", "ctx"), "tensor"),
        P(("dp", "ctx"), "tensor"),
        P(("dp", "ctx"), "tensor"),
        P("tensor", ("dp", "ctx")),
        P("tensor", ("dp", "ctx")),
        P(None, ("dp", "ctx")),
        P(None, ("dp", "ctx")),
        P("dp", "ctx", None),
    )
    out_specs = (
        P("dp", "ctx", None),
        P("dp", "ctx", None),
        P(("dp", "ctx"), None, "tensor"),
        P(("dp", "ctx"), "tensor"),
        P(("dp", "ctx"), "tensor"),
        P(("dp", "ctx"), "tensor"),
        P("tensor", ("dp", "ctx")),
        P("tensor", ("dp", "ctx")),
        P(None, ("dp", "ctx")),
        P(None, ("dp", "ctx")),
    )
    n_core = 2 if mesh.shape["dp"] % 2 == 0 else 1
    sizes = (mesh.shape["dp"] // n_core, n_core, mesh.shape["ctx"], mesh.shape["tensor"])
    body = fused if fits(sizes, mesh) else on_device
    return jax.shard_map(
        functools.partial(body, sizes), mesh=mesh, in_specs=in_specs, out_specs=out_specs, check_vma=False
    )
```
